32 devices in a mesh: stream: 2 (over x), fsdp: 16 (over z, y, core).
Axes of the slice: x: 2, y: 2, z: 4, core: 2. Of those that a mesh axis runs over, the one named last changes fastest.
Arguments:
- tokens: bfloat16 [2, 8192, 1024], P('stream', 'fsdp'), may hold values from -6 to 6
- resets: int32 [2, 16], P('stream', 'fsdp'), may hold values from 0 to 1, as said below
- retrieved: int32 [2, 8192, 8, 32], P('stream', 'fsdp'), may hold values from 0 to 255, as said below
- memory_keys: bfloat16 [2, 256, 1024], P('stream', 'fsdp'), may hold values from -6 to 6
- memory_values: bfloat16 [2, 256, 1024], P('stream', 'fsdp'), may hold values from -6 to 6
- qkv_weight: bfloat16 [1024, 3072], P('fsdp'), may hold values from -0.1875 to 0.1875
- out_weight: bfloat16 [1024, 1024], P('fsdp'), may hold values from -1.5 to 1.5
- up_weight: bfloat16 [1024, 4096], P('fsdp'), may hold values from -0.1875 to 0.1875
- up_bias: bfloat16 [4096], P('fsdp'), may hold values from -3 to 3
- down_weight: bfloat16 [4096, 1024], P('fsdp'), may hold values from -0.09375 to 0.09375
- down_bias: bfloat16 [1024], P('fsdp'), may hold values from -3 to 3
- attn_gain: bfloat16 [1024], P('fsdp'), may hold values from 0.5 to 1.5
- attn_shift: bfloat16 [1024], P('fsdp'), may hold values from -2 to 2
- ffn_gain: bfloat16 [1024], P('fsdp'), may hold values from 0.5 to 1.5
- ffn_shift: bfloat16 [1024], P('fsdp'), may hold values from -2 to 2
- position_bias: bfloat16 [256], P('fsdp'), may hold values from -4 to 4
- memory_gate: bfloat16 [8], replicated, may hold values from -2 to 2
- cotangent: bfloat16 [2, 8192, 1024], P('stream', 'fsdp'), may hold values from -6 to 6
Outputs:
- output: bfloat16 [2, 8192, 1024], P('stream', 'fsdp')
- token_grad: float32 [2, 8192, 1024], P('stream', 'fsdp')
- qkv_grad: float32 [1024, 3072], P('fsdp')
- out_grad: float32 [1024, 1024], P('fsdp')
- up_grad: float32 [1024, 4096], P('fsdp')
- up_bias_grad: float32 [4096], P('fsdp')
- down_grad: float32 [4096, 1024], P('fsdp')
- down_bias_grad: float32 [1024], P('fsdp')
- attn_gain_grad: float32 [1024], P('fsdp')
- attn_shift_grad: float32 [1024], P('fsdp')
- ffn_gain_grad: float32 [1024], P('fsdp')
- ffn_shift_grad: float32 [1024], P('fsdp')
- position_grad: float32 [256], P('fsdp')
- gate_grad: float32 [8], replicated
The draws below stay inside these ranges and needn't reach their ends.
Inputs may be any that keep to these rules, and one draw needn't show every extreme that they name: `resets`: the first segment of every stream is 1; in one stream, drawn from the seed, no other segment is 1. `retrieved`: each token and head names 32 different memory rows of its stream.
All inputs are finite; a program needn't handle non-finite values.
Results may differ from the reference program's by a relative error of at most 0.015.
Values may be sent and summed in bfloat16 or wider, within the bound.
No kernel may reach another device: no remote copies, remote signals or barrier semaphores. Data moves between devices by JAX's collectives and lax.ppermute only.
A program may use at most 192 MiB of HBM per device.

```python
import math
import jax
import jax.numpy as jnp
from jax import lax

D = 1024
HEADS = 8
DH = 128
FF = 4096
SEG = 512
BUCKETS = 32
TOPK = 32
MEM_DEV = 16
STREAMS = 2
SEGS = 16
SEQLEN = 8192
MEM = 256
N_FSDP = 16


def draw_resets(key, part):
    selected_slots = jax.random.randint(jax.random.fold_in(key, 11), (), 0, STREAMS)
    tosses = jax.random.randint(jax.random.fold_in(key, 12), (STREAMS, SEGS), 0, 4)
    stream_ids = jnp.arange(STREAMS, dtype=jnp.int32)[:, None]
    segment_ids = jnp.arange(SEGS, dtype=jnp.int32)[None, :]
    starts = jnp.where(tosses == 0, 1, 0)
    starts = jnp.where(stream_ids == selected_slots, 0, starts)
    starts = jnp.where(segment_ids == 0, 1, starts)
    return starts.astype(jnp.int32)


def draw_retrieved(key, part):
    mem_total = MEM_DEV * N_FSDP
    starts = jax.random.randint(jax.random.fold_in(key, 21), (STREAMS, SEG * N_FSDP, HEADS, 1), 0, mem_total)
    strides = jax.random.randint(jax.random.fold_in(key, 22), (STREAMS, SEG * N_FSDP, HEADS, 1), 1, mem_total // TOPK + 1)
    steps_along = jnp.arange(TOPK, dtype=jnp.int32)[None, None, None, :]
    places = (starts + strides * steps_along) % mem_total
    orders = jnp.stack([jax.random.permutation(jax.random.fold_in(key, 30 + stream_index), mem_total).astype(jnp.int32) for stream_index in range(STREAMS)])
    stream_ids = jnp.arange(STREAMS, dtype=jnp.int32)[:, None, None, None]
    return orders[stream_ids, places].astype(jnp.int32)


def block_levels(stream_key, shape, shards, low, top_value):
    factor_of, own = 1.0, jax.random.fold_in(stream_key, 6)
    for dim, blocks in shards:
        draws = jnp.exp(jax.random.uniform(jax.random.fold_in(own, dim), (blocks,), jnp.float32, low / len(shards), top_value / len(shards)))
        factor_of = factor_of * jnp.repeat(draws, shape[dim] // blocks).reshape([-1 if axis == dim else 1 for axis in range(len(shape))])
    return factor_of


def noise(key, extent, deviation, reach, split=(), kind=jnp.bfloat16):
    drawn = deviation * jax.random.normal(key, extent, jnp.float32)
    if split:
        drawn = drawn * block_levels(key, extent, split, -0.22, 0.18)
    return jnp.clip(drawn, -reach, reach).astype(kind)


def setup_inputs(seed: int = 0) -> dict:
    keys = jax.random.split(jax.random.key(seed), 19)
    tokens = noise(keys[0], (STREAMS, SEQLEN, D), 1.0, 6.0, ((0, 2), (1, 16)))
    resets = draw_resets(jax.random.fold_in(keys[18], 71), 0)
    retrieved = draw_retrieved(jax.random.fold_in(keys[18], 71), 0)
    memory_keys = noise(keys[3], (STREAMS, MEM, D), 1.0, 6.0, ((0, 2), (1, 16)))
    memory_values = noise(keys[4], (STREAMS, MEM, D), 1.0, 6.0, ((0, 2), (1, 16)))
    qkv_weight = noise(keys[5], (D, 3 * D), D ** -0.5, 0.1875, ((0, 16),))
    out_weight = noise(keys[6], (D, D), (D // 64) ** -0.5, 1.5, ((0, 16),))
    up_weight = noise(keys[7], (D, FF), D ** -0.5, 0.1875, ((0, 16),))
    up_bias = noise(keys[8], (FF,), 0.5, 3.0, ((0, 16),))
    down_weight = noise(keys[9], (FF, D), FF ** -0.5, 0.09375, ((0, 16),))
    down_bias = noise(keys[10], (D,), 0.5, 3.0, ((0, 16),))
    attn_gain = jnp.clip(1.0 + 0.1 * jax.random.normal(keys[11], (D,), jnp.float32), 0.5, 1.5).astype(jnp.bfloat16)
    attn_shift = noise(keys[12], (D,), 0.3, 2.0, ((0, 16),))
    ffn_gain = jnp.clip(1.0 + 0.1 * jax.random.normal(keys[13], (D,), jnp.float32), 0.5, 1.5).astype(jnp.bfloat16)
    ffn_shift = noise(keys[14], (D,), 0.3, 2.0, ((0, 16),))
    position_bias = noise(keys[15], (HEADS * BUCKETS,), 1.0, 4.0, ((0, 16),))
    memory_gate = jnp.clip(jax.random.uniform(keys[16], (HEADS,), jnp.float32, -2.0, 2.0), -2.0, 2.0).astype(jnp.bfloat16)
    cotangent = noise(keys[17], (STREAMS, SEQLEN, D), 1.0, 6.0, ((0, 2), (1, 16)))
    return {"tokens": tokens, "resets": resets, "retrieved": retrieved, "memory_keys": memory_keys, "memory_values": memory_values, "qkv_weight": qkv_weight, "out_weight": out_weight, "up_weight": up_weight, "up_bias": up_bias, "down_weight": down_weight, "down_bias": down_bias, "attn_gain": attn_gain, "attn_shift": attn_shift, "ffn_gain": ffn_gain, "ffn_shift": ffn_shift, "position_bias": position_bias, "memory_gate": memory_gate, "cotangent": cotangent}


@jax.custom_vjp
def low(v):
    return lax.optimization_barrier(v.astype(jnp.bfloat16)).astype(jnp.float32)

@jax.custom_vjp
def reduced_backward(v):
    return v

def low_keep(v):
    return (low(v), None)

def low_pass(kept, grad):
    return (grad,)

def back_keep(v):
    return (v, None)

def back_low(kept, grad):
    return (low(grad),)
low.defvjp(low_keep, low_pass)
reduced_backward.defvjp(back_keep, back_low)
bucket_edges = [bucket_index for bucket_index in range(1, 16)] + [int(math.ceil(16.0 * 8.0 ** ((bucket_index - 16) / 16.0))) for bucket_index in range(16, 32)]
softmax_heat = 16.0
score_masked = -1e+30
peak_score = lax.Precision.HIGHEST

def layer_norm(values, gain_vec, shift_vec):
    center = values - lax.optimization_barrier(jnp.mean(values, axis=-1, keepdims=True))
    spread = lax.optimization_barrier(jnp.mean(center * center, axis=-1, keepdims=True))
    return center * lax.rsqrt(spread + 1e-05) * gain_vec + shift_vec

def unit_rows(values):
    return values * lax.rsqrt(lax.optimization_barrier(jnp.sum(values * values, axis=-1, keepdims=True)) + 1e-06)

def gelu_tanh(values):
    return jax.nn.gelu(values, approximate=True)

def reference(tokens, resets, retrieved, memory_keys, memory_values, qkv_weight, out_weight, up_weight, up_bias, down_weight, down_bias, attn_gain, attn_shift, ffn_gain, ffn_shift, position_bias, memory_gate, cotangent):
    streams = tokens.shape[0]
    mem_unit = low(unit_rows(memory_keys.astype(jnp.float32).reshape(streams, MEM, HEADS, DH)))
    mem_vals = memory_values.astype(jnp.float32).reshape(streams, MEM, HEADS, DH)
    row_ids = jnp.arange(SEG, dtype=jnp.int32)[:, None]
    col_ids = jnp.arange(2 * SEG, dtype=jnp.int32)[None, :]
    rel_pos = jnp.maximum(row_ids - col_ids + SEG, 0)
    thresholds = jnp.array(bucket_edges, dtype=jnp.int32)
    buckets = lax.optimization_barrier(jnp.sum((rel_pos[:, :, None] >= thresholds[None, None, :]).astype(jnp.int32), axis=-1))
    causal = col_ids <= row_ids + SEG
    stream_of = jnp.repeat(jnp.arange(streams, dtype=jnp.int32), SEGS)
    reset_flat = resets.reshape(-1).astype(jnp.int32)
    picked_all = retrieved.reshape(-1, SEG, HEADS, TOPK).astype(jnp.int32)
    params = tuple((p.astype(jnp.float32) for p in (qkv_weight, out_weight, up_weight, up_bias, down_weight, down_bias, attn_gain, attn_shift, ffn_gain, ffn_shift, position_bias, memory_gate)))

    def forward(resid_in, w_qkv, w_out, w_up, b_up, w_down, b_down, gain_one, shift_one, gain_two, shift_two, table_flat, gate_vec):
        flat_in = resid_in.reshape(-1, D)
        normed_one = low(layer_norm(flat_in, gain_one, shift_one))
        qkv_out = reduced_backward(jnp.dot(normed_one, w_qkv, precision=peak_score))
        query_raw = qkv_out[:, :D].reshape(streams, SEGS, SEG, HEADS, DH)
        key_raw = qkv_out[:, D:2 * D].reshape(streams, SEGS, SEG, HEADS, DH)
        value_raw = qkv_out[:, 2 * D:].reshape(streams, SEGS, SEG, HEADS, DH)
        query_unit = low(unit_rows(query_raw))
        key_unit = low(unit_rows(key_raw))
        value_low = low(value_raw)
        zero_block = jnp.zeros_like(key_unit[:, :1])
        key_prev = jnp.concatenate([zero_block, key_unit[:, :-1]], axis=1)
        value_prev = jnp.concatenate([zero_block, value_low[:, :-1]], axis=1)
        bias_table = table_flat.reshape(HEADS, BUCKETS)
        bias_row_slices = bias_table[:, buckets]
        gate_mix = jax.nn.sigmoid(gate_vec)[None, :, None]

        def attend_block(inputs):
            query_rows, key_cur, val_cur, key_old, val_old, reset_one, picked, stream = inputs
            key_sequence = jnp.concatenate([key_old, key_cur], axis=0)
            val_list = jnp.concatenate([val_old, val_cur], axis=0)
            score_matrix = softmax_heat * jnp.einsum('pwu,xwu->wpx', query_rows, key_sequence, precision=peak_score) + bias_row_slices
            score_matrix = reduced_backward(score_matrix)
            permitted_mask = causal & ((col_ids >= SEG) | (reset_one == 0))
            score_matrix = jnp.where(permitted_mask[None], score_matrix, score_masked)
            probs = jax.nn.softmax(score_matrix, axis=-1)
            local_out = reduced_backward(jnp.einsum('hij,jhd->ihd', low(probs), val_list, precision=peak_score))
            memory_key = lax.dynamic_index_in_dim(mem_unit, stream, 0, keepdims=False)
            mem_val = lax.dynamic_index_in_dim(mem_vals, stream, 0, keepdims=False)
            head_ids = jnp.arange(HEADS, dtype=jnp.int32)[None, :, None]
            selected_key = memory_key[picked, head_ids]
            sel_val = mem_val[picked, head_ids]
            recalled_output = reduced_backward(softmax_heat * jnp.einsum('rvs,rvws->rvw', query_rows, selected_key, precision=peak_score))
            weights = jax.nn.softmax(recalled_output, axis=-1)
            remote_out = reduced_backward(jnp.einsum('ihk,ihkd->ihd', low(weights), sel_val, precision=peak_score))
            return low((gate_mix * remote_out + (1.0 - gate_mix) * local_out).reshape(SEG, D))
        attn_in = lax.map(jax.checkpoint(attend_block), (query_unit.reshape(-1, SEG, HEADS, DH), key_unit.reshape(-1, SEG, HEADS, DH), value_low.reshape(-1, SEG, HEADS, DH), key_prev.reshape(-1, SEG, HEADS, DH), value_prev.reshape(-1, SEG, HEADS, DH), reset_flat, picked_all, stream_of))
        attn_proj = reduced_backward(jnp.dot(attn_in.reshape(-1, D), w_out, precision=peak_score))
        resid_one = flat_in + attn_proj
        normed_two = low(layer_norm(resid_one, gain_two, shift_two))
        pre_act = reduced_backward(jnp.dot(normed_two, w_up, precision=peak_score) + b_up)
        activation = low(gelu_tanh(pre_act))
        result = resid_one + reduced_backward(jnp.dot(activation, w_down, precision=peak_score) + b_down)
        return result.reshape(streams, -1, D)
    result, pullback = jax.vjp(forward, tokens.astype(jnp.float32), *params)
    gradients = pullback(cotangent.astype(jnp.float32))
    return (result.astype(jnp.bfloat16), gradients[0], gradients[1], gradients[2], gradients[3], gradients[4], gradients[5], gradients[6], gradients[7], gradients[8], gradients[9], gradients[10], gradients[11], gradients[12])
```

```python
import functools, math
import jax, jax.numpy as jnp
from jax import lax
from jax.experimental import pallas as pl
from jax.experimental.pallas import tpu as pltpu
f32=jnp.float32; bf16=jnp.bfloat16
LOG2E=math.log2(math.e)
NEG=-1e30

def nt(a,b): return lax.dot_general(a,b,(((1,),(1,)),((),())),preferred_element_type=f32)
def nn(a,b): return lax.dot_general(a,b,(((1,),(0,)),((),())),preferred_element_type=f32)
def tn(a,b): return lax.dot_general(a,b,(((0,),(0,)),((),())),preferred_element_type=f32)

def mask_kernel(p_ref, o_ref, *, rows):
    n, k = p_ref.shape
    mem = o_ref.shape[1]
    for r in range(0, n, rows):
        p = p_ref[r:r+rows, :]
        ids = lax.broadcasted_iota(jnp.int32, (rows, mem), 1)
        hit = p[:, 0:1] == ids
        for t in range(1, k):
            hit = hit | (p[:, t:t+1] == ids)
        o_ref[r:r+rows, :] = jnp.where(hit, 1.0, 0.0).astype(bf16)

def picked_masks(picked, mem, interpret=False):
    h, n, k = picked.shape
    return pl.pallas_call(
        functools.partial(mask_kernel, rows=32),
        grid=(h,),
        in_specs=[pl.BlockSpec((None, n, k), lambda i: (i,0,0))],
        out_specs=pl.BlockSpec((None, n, mem), lambda i: (i,0,0)),
        out_shape=jax.ShapeDtypeStruct((h,n,mem), bf16),
        cost_estimate=pl.CostEstimate(flops=2*h*n*k*mem, bytes_accessed=h*n*(mem*2+512), transcendentals=0),
        interpret=interpret,
    )(picked)

def spread(base, blk):
    w = base.shape[1]
    x = jnp.broadcast_to(base, (8, w))
    r = lax.broadcasted_iota(jnp.int32, (8, w), 0)
    for b in (1, 2, 4):
        x = jnp.where((r & b) != 0, pltpu.roll(x, b, 1), x)
    size = 8
    while size < blk:
        x = jnp.concatenate([x, pltpu.roll(x, size, 1)], axis=0)
        size *= 2
    return x

def gather_diagonals(g):
    size, w = g.shape
    while size > 8:
        half = size // 2
        g = g[:half] + pltpu.roll(g[half:], w - half, 1)
        size = half
    r = lax.broadcasted_iota(jnp.int32, (8, w), 0)
    for b in (4, 2, 1):
        g = jnp.where((r & b) != 0, pltpu.roll(g, w - b, 1), g)
    return jnp.sum(g, axis=0, keepdims=True)

BLK=128
def attn_fwd_kernel(gate_ref, reset_ref, q_ref, kp_ref, kc_ref, vp_ref, vc_ref, base_ref, mk_ref, mv_ref, mask_ref,
                    mix_ref, loc_ref, rem_ref, t_ref):
    seg = q_ref.shape[0]
    h = pl.program_id(0)
    s = gate_ref[h]
    keep = jnp.where(reset_ref[0] == 0, 1.0, 0.0).astype(f32)
    t_ref[...] = spread(base_ref[...], BLK)
    heat = 16.0 * LOG2E
    nb = seg // BLK
    vp = vp_ref[...] * keep.astype(bf16)
    mk = mk_ref[...]; mv = mv_ref[...]
    for i in range(nb):
        rows = slice(i*BLK, (i+1)*BLK)
        q = q_ref[rows, :]
        off = (nb-1-i)*BLK
        cw = (i+1)*BLK
        ep = jnp.exp2(nt(q, kp_ref[...]) * heat + t_ref[:, off:off+seg])
        ec = jnp.exp2(nt(q, kc_ref[:cw, :]) * heat + t_ref[:, off+seg:off+seg+cw])
        l = keep * jnp.sum(ep, axis=1, keepdims=True) + jnp.sum(ec, axis=1, keepdims=True)
        o = (nn(ep.astype(bf16), vp) + nn(ec.astype(bf16), vc_ref[:cw, :])) / l
        em = jnp.exp2(nt(q, mk) * heat) * mask_ref[rows, :].astype(f32)
        lm = jnp.sum(em, axis=1, keepdims=True)
        om = nn(em.astype(bf16), mv) / lm
        loc_ref[rows, :] = o.astype(bf16)
        rem_ref[rows, :] = om.astype(bf16)
        mix_ref[rows, :] = (s*om + (1.0-s)*o).astype(bf16)

def attn_fwd(gate, reset, q, kp, kc, vp, vc, base, mk, mv, mask, interpret=False):
    seg, width = q.shape
    heads = base.shape[0]
    dh = width // heads
    mem = mk.shape[0]
    col = lambda n: pl.BlockSpec((n, dh), lambda h, *_: (0, h))
    full = jax.ShapeDtypeStruct((seg, width), bf16)
    wt = base.shape[2]
    return pl.pallas_call(
        attn_fwd_kernel,
        grid_spec=pltpu.PrefetchScalarGridSpec(
            num_scalar_prefetch=2, grid=(heads,),
            in_specs=[col(seg), col(seg), col(seg), col(seg), col(seg),
                      pl.BlockSpec((None,1,wt), lambda h,*_: (h,0,0)), col(mem), col(mem),
                      pl.BlockSpec((None,seg,mem), lambda h,*_: (h,0,0))],
            out_specs=[col(seg), col(seg), col(seg)],
            scratch_shapes=[pltpu.VMEM((BLK, wt), f32)]),
        out_shape=[full, full, full],
        compiler_params=pltpu.CompilerParams(vmem_limit_bytes=48<<20),
        cost_estimate=pl.CostEstimate(flops=heads*seg*(2*seg+mem)*4*dh, bytes_accessed=8*seg*width*2+heads*seg*mem*2, transcendentals=heads*seg*(2*seg+mem)),
        interpret=interpret,
    )(gate, reset, q, kp, kc, vp, vc, base, mk, mv, mask)

def unit_back(g, u, r):
    u = u.astype(f32)
    return (r * (g - u * jnp.sum(g * u, axis=1, keepdims=True))).astype(bf16)

def attn_bwd_kernel(gate_ref, reset_ref, q_ref, kp_ref, kc_ref, vp_ref, vc_ref, base_ref, mk_ref, mv_ref, mask_ref,
                    loc_ref, rem_ref, gm_ref, rq_ref, rkp_ref, rkc_ref,
                    dq_ref, dkp_ref, dkc_ref, dvp_ref, dvc_ref, diag_ref, dgate_ref, t_ref, g_ref, akp, akc, avp, avc):
    seg = q_ref.shape[0]
    h = pl.program_id(0)
    s = gate_ref[h]
    keep = jnp.where(reset_ref[0] == 0, 1.0, 0.0).astype(f32)
    t_ref[...] = spread(base_ref[...], BLK)
    g_ref[...] = jnp.zeros_like(g_ref)
    heat = 16.0 * LOG2E
    nb = seg // BLK
    mk = mk_ref[...]; mv = mv_ref[...]
    dg = jnp.zeros((BLK, 1), f32)
    for i in range(nb):
        rows = slice(i*BLK, (i+1)*BLK)
        q = q_ref[rows, :]
        gm = gm_ref[rows, :]
        off = (nb-1-i)*BLK
        cw = (i+1)*BLK
        al = jnp.sum(gm * loc_ref[rows, :].astype(f32), axis=1, keepdims=True)
        ar = jnp.sum(gm * rem_ref[rows, :].astype(f32), axis=1, keepdims=True)
        dg = dg + (ar - al)
        gl = ((1.0-s)*gm).astype(bf16)
        gr = (s*gm).astype(bf16)
        dl = (1.0-s)*al
        dr = s*ar
        ep = jnp.exp2(nt(q, kp_ref[...]) * heat + t_ref[:, off:off+seg])
        ec = jnp.exp2(nt(q, kc_ref[:cw, :]) * heat + t_ref[:, off+seg:off+seg+cw])
        l = keep * jnp.sum(ep, axis=1, keepdims=True) + jnp.sum(ec, axis=1, keepdims=True)
        il = 1.0 / l
        ilp = il * keep
        pp = ep * ilp
        pc = ec * il
        dsp = pp * (nt(gl, vp_ref[...]) - dl)
        dsc = pc * (nt(gl, vc_ref[:cw, :]) - dl)
        g_ref[:, off:off+seg] += dsp
        g_ref[:, off+seg:off+seg+cw] += dsc
        dsp = dsp.astype(bf16); dsc = dsc.astype(bf16)
        dq = nn(dsp, kp_ref[...]) + nn(dsc, kc_ref[:cw, :])
        ppb = pp.astype(bf16); pcb = pc.astype(bf16)
        dkp = tn(dsp, q); dvp = tn(ppb, gl)
        dkc = tn(dsc, q); dvc = tn(pcb, gl)
        if i == 0:
            akp[...] = dkp; avp[...] = dvp
            akc[...] = jnp.zeros_like(akc); avc[...] = jnp.zeros_like(avc)
            akc[:cw, :] = dkc; avc[:cw, :] = dvc
        else:
            akp[...] += dkp; avp[...] += dvp
            akc[:cw, :] += dkc; avc[:cw, :] += dvc
        em = jnp.exp2(nt(q, mk) * heat) * mask_ref[rows, :].astype(f32)
        ilm = 1.0 / jnp.sum(em, axis=1, keepdims=True)
        dsm = (em * ilm) * (nt(gr, mv) - dr)
        dq = dq + nn(dsm.astype(bf16), mk)
        dq_ref[rows, :] = unit_back(16.0 * dq, q, rq_ref[rows, :])
    dkp_ref[...] = unit_back(16.0 * akp[...], kp_ref[...], rkp_ref[...])
    dkc_ref[...] = unit_back(16.0 * akc[...], kc_ref[...], rkc_ref[...])
    dvp_ref[...] = avp[...].astype(bf16)
    dvc_ref[...] = avc[...].astype(bf16)
    diag_ref[...] = gather_diagonals(g_ref[...])
    dgate_ref[...] = jnp.broadcast_to(jnp.sum(dg) * s * (1.0-s), dgate_ref.shape)

def attn_bwd(gate, reset, q, kp, kc, vp, vc, rq, rkp, rkc, base, mk, mv, mask, loc, rem, gm, interpret=False):
    seg, width = q.shape
    heads = base.shape[0]
    dh = width // heads
    mem = mk.shape[0]
    wt = base.shape[2]
    col = lambda n: pl.BlockSpec((n, dh), lambda h, *_: (0, h))
    row = lambda w: pl.BlockSpec((None,1,w), lambda h,*_: (h,0,0))
    rcol = pl.BlockSpec((None,seg,1), lambda h,*_: (h,0,0))
    fb = jax.ShapeDtypeStruct((seg, width), bf16)
    return pl.pallas_call(
        attn_bwd_kernel,
        grid_spec=pltpu.PrefetchScalarGridSpec(
            num_scalar_prefetch=2, grid=(heads,),
            in_specs=[col(seg)]*5 + [row(wt), col(mem), col(mem),
                      pl.BlockSpec((None,seg,mem), lambda h,*_: (h,0,0)), col(seg), col(seg), col(seg), rcol, rcol, rcol],
            out_specs=[col(seg)]*5 + [row(wt), row(128)],
            scratch_shapes=[pltpu.VMEM((BLK, wt), f32)]*2 + [pltpu.VMEM((seg, dh), f32)]*4),
        out_shape=[fb, fb, fb, fb, fb, jax.ShapeDtypeStruct((heads,1,wt), f32), jax.ShapeDtypeStruct((heads,1,128), f32)],
        compiler_params=pltpu.CompilerParams(vmem_limit_bytes=48<<20),
        cost_estimate=pl.CostEstimate(flops=heads*seg*(2*seg+mem)*10*dh, bytes_accessed=20*seg*width*2+heads*seg*mem*2, transcendentals=heads*seg*(2*seg+mem)),
        interpret=interpret,
    )(gate, reset, q, kp, kc, vp, vc, base, mk, mv, mask, loc, rem, gm, rq, rkp, rkc)

edges=[b for b in range(1,16)]+[int(math.ceil(16.0*8.0**((b-16)/16.0))) for b in range(16,32)]
def diagonal_rel(seg):
    wt = 2*seg + seg - BLK + BLK
    k = jnp.arange(wt, dtype=jnp.int32)
    top = 2*seg - BLK
    return jnp.where(k > wt - BLK, top - (k - wt), top - k)

def bucket_hot(seg):
    rel = diagonal_rel(seg)
    counts = jnp.zeros_like(rel)
    for e in edges: counts = counts + (rel >= e).astype(jnp.int32)
    hot = (counts[None,:] == jnp.arange(len(edges)+1)[:,None]) & (rel >= 0)[None,:]
    return hot.astype(f32), rel
def diagonal_bias(table, hot, rel):
    v = jnp.dot(table, hot, precision=lax.Precision.HIGHEST) * LOG2E
    return jnp.where(rel[None,:] >= 0, v, NEG)[:, None, :]


from jax.sharding import PartitionSpec as P


def passed_along(block, axis, distance):
    devices = range(lax.axis_size(axis))
    return lax.ppermute(block, axis, [(i - distance, i) for i in devices if i - distance in devices])


def norm_stats(x):
    center = x - jnp.mean(x, axis=-1, keepdims=True)
    spread_sq = jnp.mean(center * center, axis=-1, keepdims=True)
    r = lax.rsqrt(spread_sq + 1e-05)
    return center * r, r


def norm_back(grad, n, r, gain):
    gn = grad * gain
    return r * (gn - jnp.mean(gn, axis=-1, keepdims=True) - n * jnp.mean(gn * n, axis=-1, keepdims=True))


def qkv_kernel(xp_ref, xc_ref, gain_ref, shift_ref, w_ref, q_ref, kp_ref, kc_ref, vp_ref, vc_ref, rq_ref, rkp_ref, rkc_ref, np_ref, nc_ref, x_ref, *, dh):
    i = pl.program_id(0)
    per = pl.num_programs(0) // 3
    seg = xc_ref.shape[0]

    @pl.when(i == 0)
    def _():
        gain = gain_ref[...].astype(f32)
        shift = shift_ref[...].astype(f32)
        for src, dst, at in ((xp_ref, np_ref, 0), (xc_ref, nc_ref, seg)):
            n, r = norm_stats(src[...].astype(f32))
            low = (n * gain + shift).astype(bf16)
            x_ref[at : at + seg, :] = low
            dst[...] = low

    def unit(y, out_ref, r_ref):
        for k in range(y.shape[1] // dh):
            part = y[:, k * dh : (k + 1) * dh]
            r = lax.rsqrt(jnp.sum(part * part, axis=1, keepdims=True) + 1e-06)
            out_ref[:, k * dh : (k + 1) * dh] = (part * r).astype(bf16)
            r_ref[k] = r

    w = w_ref[...]

    @pl.when(i < per)
    def _():
        unit(nn(x_ref[seg:, :], w), q_ref, rq_ref)

    @pl.when((i >= per) & (i < 2 * per))
    def _():
        unit(nn(x_ref[:seg, :], w), kp_ref, rkp_ref)
        unit(nn(x_ref[seg:, :], w), kc_ref, rkc_ref)

    @pl.when(i >= 2 * per)
    def _():
        vp_ref[...] = nn(x_ref[:seg, :], w).astype(bf16)
        vc_ref[...] = nn(x_ref[seg:, :], w).astype(bf16)


def project_qkv(xp, xc, gain, shift, w, heads):
    seg, width = xc.shape
    dh = width // heads
    two = 2 * dh
    per = width // two
    whole = pl.BlockSpec((seg, width), lambda i: (0, 0))
    vec = pl.BlockSpec((1, width), lambda i: (0, 0))
    at = lambda s: (lambda i: (0, jnp.clip(i - s * per, 0, per - 1)))
    at3 = lambda s: (lambda i: (jnp.clip(i - s * per, 0, per - 1), 0, 0))
    cols = lambda s: pl.BlockSpec((seg, two), at(s))
    rs = lambda s: pl.BlockSpec((2, seg, 1), at3(s))
    low = jax.ShapeDtypeStruct((seg, width), bf16)
    rr = jax.ShapeDtypeStruct((heads, seg, 1), f32)
    return pl.pallas_call(
        functools.partial(qkv_kernel, dh=dh),
        grid=(3 * per,),
        in_specs=[whole, whole, vec, vec, pl.BlockSpec((width, two), lambda i: (0, i))],
        out_specs=[cols(0), cols(1), cols(1), cols(2), cols(2), rs(0), rs(1), rs(1), whole, whole],
        out_shape=[low] * 5 + [rr] * 3 + [low] * 2,
        scratch_shapes=[pltpu.VMEM((2 * seg, width), bf16)],
        compiler_params=pltpu.CompilerParams(vmem_limit_bytes=48 << 20),
        cost_estimate=pl.CostEstimate(flops=2 * seg * width * width * 5, bytes_accessed=3 * width * width * 2 + 9 * seg * width * 2, transcendentals=0),
    )(xp, xc, gain, shift, w)


def local(
    tokens, resets, retrieved, memory_keys, memory_values, qkv_weight, out_weight, up_weight, up_bias,
    down_weight, down_bias, attn_gain, attn_shift, ffn_gain, ffn_shift, position_bias, memory_gate, cotangent,
):
    heads = memory_gate.shape[0]
    seg, width = tokens.shape[1:]
    dh = width // heads
    mem_rows = memory_keys.shape[1]
    shards = lax.axis_size("fsdp")
    mem = mem_rows * shards
    part = width // shards
    bias_part = up_bias.shape[0]
    pos_part = position_bias.shape[0]
    keys = memory_keys[0].astype(f32).reshape(mem_rows, heads, dh)
    keys = keys * lax.rsqrt(jnp.sum(keys * keys, axis=-1, keepdims=True) + 1e-06)
    small = jnp.concatenate([up_bias, down_bias, attn_gain, attn_shift, ffn_gain, ffn_shift, position_bias])
    small = jnp.pad(small, (0, width - small.shape[0]))[None]
    pack = jnp.concatenate([keys.reshape(mem_rows, width).astype(bf16), memory_values[0], jnp.pad(small, ((0, 15), (0, 0)))], axis=0)
    pack = lax.all_gather(pack, "fsdp", axis=0)
    mk = pack[:, :mem_rows].reshape(mem, width)
    mv = pack[:, mem_rows : 2 * mem_rows].reshape(mem, width)
    small = pack[:, 2 * mem_rows]
    b_up = small[:, :bias_part].reshape(-1)
    vecs = [small[:, bias_part + k * part : bias_part + (k + 1) * part].reshape(1, -1) for k in range(5)]
    b_down, gain_one, shift_one, gain_two, shift_two = vecs
    table = small[:, bias_part + 5 * part : bias_part + 5 * part + pos_part].reshape(heads, -1).astype(f32)
    w_qkv = lax.all_gather(qkv_weight, "fsdp", axis=0, tiled=True)
    w_out = lax.all_gather(out_weight, "fsdp", axis=0, tiled=True)
    w_up = lax.all_gather(up_weight, "fsdp", axis=0, tiled=True)
    w_down = lax.all_gather(down_weight, "fsdp", axis=0, tiled=True)
    before = passed_along(tokens[0], "fsdp", 1)
    mask = picked_masks(retrieved[0].transpose(1, 0, 2), mem)
    hot, rel = bucket_hot(seg)
    base = diagonal_bias(table, hot, rel)
    gate = jax.nn.sigmoid(memory_gate.astype(f32))
    reset = resets[0]
    q, kp, kc, vp, vc, rq, rkp, rkc, n_prev, n_cur = project_qkv(before, tokens[0], gain_one, shift_one, w_qkv, heads)
    attn_in, loc, rem = attn_fwd(gate, reset, q, kp, kc, vp, vc, base, mk, mv, mask)
    resid_in = tokens[0].astype(f32)
    resid_one = resid_in + nn(attn_in, w_out)
    n_two, r_two = norm_stats(resid_one)
    g_two = gain_two.astype(f32)
    normed_two = (n_two * g_two + shift_two.astype(f32)).astype(bf16)
    pre_act = nn(normed_two, w_up) + b_up.astype(f32)
    act_full, gelu_vjp = jax.vjp(lambda v: jax.nn.gelu(v, approximate=True), pre_act)
    activation = act_full.astype(bf16)
    output = (resid_one + nn(activation, w_down) + b_down.astype(f32)).astype(bf16)[None]
    grad_down = cotangent[0]
    grad_out = grad_down.astype(f32)
    down_bias_g = jnp.sum(grad_out, axis=0)
    down_g = tn(activation, grad_down).astype(bf16)
    grad_pre = gelu_vjp(nt(grad_down, w_down))[0].astype(bf16)
    up_bias_g = jnp.sum(grad_pre.astype(f32), axis=0)
    up_g = tn(normed_two, grad_pre).astype(bf16)
    grad_h2 = nt(grad_pre, w_up)
    gain_two_g = jnp.sum(grad_h2 * n_two, axis=0)
    shift_two_g = jnp.sum(grad_h2, axis=0)
    grad_one = grad_out + norm_back(grad_h2, n_two, r_two, g_two)
    grad_attn = grad_one.astype(bf16)
    out_g = tn(attn_in, grad_attn).astype(bf16)
    gm = nt(grad_attn, w_out)
    dq, dkp, dkc, dvp, dvc, diag, dgate = attn_bwd(gate, reset, q, kp, kc, vp, vc, rq, rkp, rkc, base, mk, mv, mask, loc, rem, gm)
    gate_g = dgate[:, 0, 0]
    table_g = jnp.dot(diag[:, 0], hot.T, precision=lax.Precision.HIGHEST)
    wq, wk, wv = w_qkv[:, :width], w_qkv[:, width : 2 * width], w_qkv[:, 2 * width :]
    back = (nt(dkp, wk) + nt(dvp, wv)).astype(bf16)
    back = passed_along(back, "fsdp", -1)
    qkv_g = jnp.concatenate([tn(n_cur, dq), tn(n_cur, dkc) + tn(n_prev, dkp), tn(n_cur, dvc) + tn(n_prev, dvp)], axis=1).astype(bf16)
    grad_h1 = nt(dq, wq) + nt(dkc, wk) + nt(dvc, wv) + back.astype(f32)
    n_one, r_one = norm_stats(resid_in)
    gain_one_g = jnp.sum(grad_h1 * n_one, axis=0)
    shift_one_g = jnp.sum(grad_h1, axis=0)
    token_grad = (grad_one + norm_back(grad_h1, n_one, r_one, gain_one.astype(f32)))[None]
    small_g = jnp.concatenate(
        [up_bias_g.reshape(shards, -1)]
        + [v.reshape(shards, -1) for v in (down_bias_g, gain_one_g, shift_one_g, gain_two_g, shift_two_g, table_g)]
        + [jnp.broadcast_to(gate_g[None], (shards, heads))],
        axis=1,
    )
    small_g = lax.psum(lax.psum_scatter(small_g, "fsdp", scatter_dimension=0, tiled=True)[0], "stream")
    big = [lax.psum_scatter(g, "fsdp", scatter_dimension=0, tiled=True) for g in (down_g, up_g, out_g, qkv_g)]
    down_t, up_t, out_t, qkv_t = [g.astype(f32) for g in lax.psum(big, "stream")]
    cuts = [bias_part] + [part] * 5 + [pos_part, heads]
    at = 0
    outs = []
    for c in cuts:
        outs.append(small_g[at : at + c])
        at += c
    ub, db, g1, s1, g2, s2, pg, gg = outs
    return output, token_grad, qkv_t, out_t, up_t, ub, down_t, db, g1, s1, g2, s2, pg, gg


def solution(mesh):
    row = P("stream", "fsdp", None)
    return jax.shard_map(
        local,
        mesh=mesh,
        in_specs=(
            row, P("stream", "fsdp"), P("stream", "fsdp", None, None), row, row, P("fsdp", None), P("fsdp", None),
            P("fsdp", None), P("fsdp"), P("fsdp", None), P("fsdp"), P("fsdp"), P("fsdp"), P("fsdp"), P("fsdp"),
            P("fsdp"), P(), row,
        ),
        out_specs=(
            row, row, P("fsdp", None), P("fsdp", None), P("fsdp", None), P("fsdp"), P("fsdp", None), P("fsdp"),
            P("fsdp"), P("fsdp"), P("fsdp"), P("fsdp"), P("fsdp"), P(),
        ),
        check_vma=False,
    )
```

```python
import functools, math
import jax, jax.numpy as jnp
from jax import lax
from jax.experimental import pallas as pl
from jax.experimental.pallas import tpu as pltpu
f32=jnp.float32; bf16=jnp.bfloat16
LOG2E=math.log2(math.e)
NEG=-1e30

def nt(a,b): return lax.dot_general(a,b,(((1,),(1,)),((),())),preferred_element_type=f32)
def nn(a,b): return lax.dot_general(a,b,(((1,),(0,)),((),())),preferred_element_type=f32)
def tn(a,b): return lax.dot_general(a,b,(((0,),(0,)),((),())),preferred_element_type=f32)

def mask_kernel(p_ref, o_ref, *, rows):
    n, k = p_ref.shape
    mem = o_ref.shape[1]
    for r in range(0, n, rows):
        p = p_ref[r:r+rows, :]
        ids = lax.broadcasted_iota(jnp.int32, (rows, mem), 1)
        hit = p[:, 0:1] == ids
        for t in range(1, k):
            hit = hit | (p[:, t:t+1] == ids)
        o_ref[r:r+rows, :] = jnp.where(hit, 1.0, 0.0).astype(bf16)

def picked_masks(picked, mem, interpret=False):
    h, n, k = picked.shape
    return pl.pallas_call(
        functools.partial(mask_kernel, rows=32),
        grid=(h,),
        in_specs=[pl.BlockSpec((None, n, k), lambda i: (i,0,0))],
        out_specs=pl.BlockSpec((None, n, mem), lambda i: (i,0,0)),
        out_shape=jax.ShapeDtypeStruct((h,n,mem), bf16),
        cost_estimate=pl.CostEstimate(flops=2*h*n*k*mem, bytes_accessed=h*n*(mem*2+512), transcendentals=0),
        interpret=interpret,
    )(picked)

def spread(base, blk):
    w = base.shape[1]
    x = jnp.broadcast_to(base, (8, w))
    r = lax.broadcasted_iota(jnp.int32, (8, w), 0)
    for b in (1, 2, 4):
        x = jnp.where((r & b) != 0, pltpu.roll(x, b, 1), x)
    size = 8
    while size < blk:
        x = jnp.concatenate([x, pltpu.roll(x, size, 1)], axis=0)
        size *= 2
    return x

def gather_diagonals(g):
    size, w = g.shape
    while size > 8:
        half = size // 2
        g = g[:half] + pltpu.roll(g[half:], w - half, 1)
        size = half
    r = lax.broadcasted_iota(jnp.int32, (8, w), 0)
    for b in (4, 2, 1):
        g = jnp.where((r & b) != 0, pltpu.roll(g, w - b, 1), g)
    return jnp.sum(g, axis=0, keepdims=True)

BLK=128
def attn_fwd_kernel(gate_ref, reset_ref, q_ref, kp_ref, kc_ref, vp_ref, vc_ref, base_ref, mk_ref, mv_ref, mask_ref,
                    mix_ref, loc_ref, rem_ref, t_ref):
    seg = q_ref.shape[0]
    h = pl.program_id(0)
    s = gate_ref[h]
    keep = jnp.where(reset_ref[0] == 0, 1.0, 0.0).astype(f32)
    t_ref[...] = spread(base_ref[...], BLK)
    heat = 16.0 * LOG2E
    nb = seg // BLK
    vp = vp_ref[...] * keep.astype(bf16)
    mk = mk_ref[...]; mv = mv_ref[...]
    for i in range(nb):
        rows = slice(i*BLK, (i+1)*BLK)
        q = q_ref[rows, :]
        off = (nb-1-i)*BLK
        cw = (i+1)*BLK
        ep = jnp.exp2(nt(q, kp_ref[...]) * heat + t_ref[:, off:off+seg])
        ec = jnp.exp2(nt(q, kc_ref[:cw, :]) * heat + t_ref[:, off+seg:off+seg+cw])
        l = keep * jnp.sum(ep, axis=1, keepdims=True) + jnp.sum(ec, axis=1, keepdims=True)
        o = (nn(ep.astype(bf16), vp) + nn(ec.astype(bf16), vc_ref[:cw, :])) / l
        em = jnp.exp2(nt(q, mk) * heat) * mask_ref[rows, :].astype(f32)
        lm = jnp.sum(em, axis=1, keepdims=True)
        om = nn(em.astype(bf16), mv) / lm
        loc_ref[rows, :] = o.astype(bf16)
        rem_ref[rows, :] = om.astype(bf16)
        mix_ref[rows, :] = (s*om + (1.0-s)*o).astype(bf16)

def attn_fwd(gate, reset, q, kp, kc, vp, vc, base, mk, mv, mask, interpret=False):
    seg, width = q.shape
    heads = base.shape[0]
    dh = width // heads
    mem = mk.shape[0]
    col = lambda n: pl.BlockSpec((n, dh), lambda h, *_: (0, h))
    full = jax.ShapeDtypeStruct((seg, width), bf16)
    wt = base.shape[2]
    return pl.pallas_call(
        attn_fwd_kernel,
        grid_spec=pltpu.PrefetchScalarGridSpec(
            num_scalar_prefetch=2, grid=(heads,),
            in_specs=[col(seg), col(seg), col(seg), col(seg), col(seg),
                      pl.BlockSpec((None,1,wt), lambda h,*_: (h,0,0)), col(mem), col(mem),
                      pl.BlockSpec((None,seg,mem), lambda h,*_: (h,0,0))],
            out_specs=[col(seg), col(seg), col(seg)],
            scratch_shapes=[pltpu.VMEM((BLK, wt), f32)]),
        out_shape=[full, full, full],
        compiler_params=pltpu.CompilerParams(vmem_limit_bytes=48<<20),
        cost_estimate=pl.CostEstimate(flops=heads*seg*(2*seg+mem)*4*dh, bytes_accessed=8*seg*width*2+heads*seg*mem*2, transcendentals=heads*seg*(2*seg+mem)),
        interpret=interpret,
    )(gate, reset, q, kp, kc, vp, vc, base, mk, mv, mask)

def unit_back(g, u, r):
    u = u.astype(f32)
    return (r * (g - u * jnp.sum(g * u, axis=1, keepdims=True))).astype(bf16)

def attn_bwd_kernel(gate_ref, reset_ref, q_ref, kp_ref, kc_ref, vp_ref, vc_ref, base_ref, mk_ref, mv_ref, mask_ref,
                    loc_ref, rem_ref, gm_ref, rq_ref, rkp_ref, rkc_ref,
                    dc_ref, dp_ref, diag_ref, dgate_ref, t_ref, g_ref, akp, akc, avp, avc):
    seg = q_ref.shape[0]
    h = pl.program_id(0)
    s = gate_ref[h]
    keep = jnp.where(reset_ref[0] == 0, 1.0, 0.0).astype(f32)
    t_ref[...] = spread(base_ref[...], BLK)
    g_ref[...] = jnp.zeros_like(g_ref)
    heat = 16.0 * LOG2E
    nb = seg // BLK
    mk = mk_ref[...]; mv = mv_ref[...]
    dg = jnp.zeros((BLK, 1), f32)
    for i in range(nb):
        rows = slice(i*BLK, (i+1)*BLK)
        q = q_ref[rows, :]
        gm = gm_ref[rows, :]
        off = (nb-1-i)*BLK
        cw = (i+1)*BLK
        al = jnp.sum(gm * loc_ref[rows, :].astype(f32), axis=1, keepdims=True)
        ar = jnp.sum(gm * rem_ref[rows, :].astype(f32), axis=1, keepdims=True)
        dg = dg + (ar - al)
        gl = ((1.0-s)*gm).astype(bf16)
        gr = (s*gm).astype(bf16)
        dl = (1.0-s)*al
        dr = s*ar
        ep = jnp.exp2(nt(q, kp_ref[...]) * heat + t_ref[:, off:off+seg])
        ec = jnp.exp2(nt(q, kc_ref[:cw, :]) * heat + t_ref[:, off+seg:off+seg+cw])
        l = keep * jnp.sum(ep, axis=1, keepdims=True) + jnp.sum(ec, axis=1, keepdims=True)
        il = 1.0 / l
        ilp = il * keep
        pp = ep * ilp
        pc = ec * il
        dsp = pp * (nt(gl, vp_ref[...]) - dl)
        dsc = pc * (nt(gl, vc_ref[:cw, :]) - dl)
        g_ref[:, off:off+seg] += dsp
        g_ref[:, off+seg:off+seg+cw] += dsc
        dsp = dsp.astype(bf16); dsc = dsc.astype(bf16)
        dq = nn(dsp, kp_ref[...]) + nn(dsc, kc_ref[:cw, :])
        ppb = pp.astype(bf16); pcb = pc.astype(bf16)
        dkp = tn(dsp, q); dvp = tn(ppb, gl)
        dkc = tn(dsc, q); dvc = tn(pcb, gl)
        if i == 0:
            akp[...] = dkp; avp[...] = dvp
            akc[...] = jnp.zeros_like(akc); avc[...] = jnp.zeros_like(avc)
            akc[:cw, :] = dkc; avc[:cw, :] = dvc
        else:
            akp[...] += dkp; avp[...] += dvp
            akc[:cw, :] += dkc; avc[:cw, :] += dvc
        em = jnp.exp2(nt(q, mk) * heat) * mask_ref[rows, :].astype(f32)
        ilm = 1.0 / jnp.sum(em, axis=1, keepdims=True)
        dsm = (em * ilm) * (nt(gr, mv) - dr)
        dq = dq + nn(dsm.astype(bf16), mk)
        dc_ref[0, rows, :] = unit_back(16.0 * dq, q, rq_ref[rows, :])
    dp_ref[0] = unit_back(16.0 * akp[...], kp_ref[...], rkp_ref[...])
    dc_ref[1] = unit_back(16.0 * akc[...], kc_ref[...], rkc_ref[...])
    dp_ref[1] = avp[...].astype(bf16)
    dc_ref[2] = avc[...].astype(bf16)
    diag_ref[...] = gather_diagonals(g_ref[...])
    dgate_ref[...] = jnp.broadcast_to(jnp.sum(dg) * s * (1.0-s), dgate_ref.shape)

def attn_bwd(gate, reset, q, kp, kc, vp, vc, rq, rkp, rkc, base, mk, mv, mask, loc, rem, gm, interpret=False):
    seg, width = q.shape
    heads = base.shape[0]
    dh = width // heads
    mem = mk.shape[0]
    wt = base.shape[2]
    col = lambda n: pl.BlockSpec((n, dh), lambda h, *_: (0, h))
    row = lambda w: pl.BlockSpec((None,1,w), lambda h,*_: (h,0,0))
    rcol = pl.BlockSpec((None,seg,1), lambda h,*_: (h,0,0))
    fb = jax.ShapeDtypeStruct((seg, width), bf16)
    return pl.pallas_call(
        attn_bwd_kernel,
        grid_spec=pltpu.PrefetchScalarGridSpec(
            num_scalar_prefetch=2, grid=(heads,),
            in_specs=[col(seg)]*5 + [row(wt), col(mem), col(mem),
                      pl.BlockSpec((None,seg,mem), lambda h,*_: (h,0,0)), col(seg), col(seg), col(seg), rcol, rcol, rcol],
            out_specs=[pl.BlockSpec((3,seg,dh), lambda h,*_: (0,0,h)), pl.BlockSpec((2,seg,dh), lambda h,*_: (0,0,h)), row(wt), row(128)],
            scratch_shapes=[pltpu.VMEM((BLK, wt), f32)]*2 + [pltpu.VMEM((seg, dh), f32)]*4),
        out_shape=[jax.ShapeDtypeStruct((3,seg,width),bf16), jax.ShapeDtypeStruct((2,seg,width),bf16), jax.ShapeDtypeStruct((heads,1,wt), f32), jax.ShapeDtypeStruct((heads,1,128), f32)],
        compiler_params=pltpu.CompilerParams(vmem_limit_bytes=48<<20),
        cost_estimate=pl.CostEstimate(flops=heads*seg*(2*seg+mem)*10*dh, bytes_accessed=20*seg*width*2+heads*seg*mem*2, transcendentals=heads*seg*(2*seg+mem)),
        interpret=interpret,
    )(gate, reset, q, kp, kc, vp, vc, base, mk, mv, mask, loc, rem, gm, rq, rkp, rkc)

edges=[b for b in range(1,16)]+[int(math.ceil(16.0*8.0**((b-16)/16.0))) for b in range(16,32)]
def diagonal_rel(seg):
    wt = 2*seg + seg - BLK + BLK
    k = jnp.arange(wt, dtype=jnp.int32)
    top = 2*seg - BLK
    return jnp.where(k > wt - BLK, top - (k - wt), top - k)

def bucket_hot(seg):
    rel = diagonal_rel(seg)
    counts = jnp.zeros_like(rel)
    for e in edges: counts = counts + (rel >= e).astype(jnp.int32)
    hot = (counts[None,:] == jnp.arange(len(edges)+1)[:,None]) & (rel >= 0)[None,:]
    return hot.astype(f32), rel
def diagonal_bias(table, hot, rel):
    v = jnp.dot(table, hot, precision=lax.Precision.HIGHEST) * LOG2E
    return jnp.where(rel[None,:] >= 0, v, NEG)[:, None, :]


from jax.sharding import PartitionSpec as P


def xor_perm(bit, n):
    return [(i, i ^ bit) for i in range(n)]


def places():
    n = lax.axis_size("fsdp")
    i = lax.axis_index("fsdp")
    return n // 4, i // 4, (i // 2) % 2, i % 2, lax.axis_index("stream")


def send_core(v):
    return lax.ppermute(v, "fsdp", xor_perm(1, lax.axis_size("fsdp")))


def send_y(v):
    return lax.ppermute(v, "fsdp", xor_perm(2, lax.axis_size("fsdp")))


def send_z(v, k):
    return lax.ppermute(v, "fsdp", xor_perm(4 * k, lax.axis_size("fsdp")))


def send_x(v):
    return lax.ppermute(v, "stream", [(0, 1), (1, 0)])


def after(value, *others):
    return lax.optimization_barrier((value,) + others)[0]


def halves(w, x):
    c = w.shape[1] // 4
    pick = lambda k: jnp.where(x == 0, w[:, k * c : (k + 1) * c], w[:, (k + 2) * c : (k + 3) * c])
    return jnp.stack([pick(0), pick(1)])


def gather_start(w, gate=None):
    nz, z, y, c, x = places()
    own = halves(w, x)
    if gate is not None:
        own = after(own, *gate)
    return [own] + [send_z(own, k) for k in range(1, nz)]


def gather_rest(got):
    a4 = jnp.stack([g[0] for g in got])
    b4 = jnp.stack([g[1] for g in got])
    ra4, rb4 = send_y(a4), send_x(b4)
    a8, b8 = jnp.concatenate([a4, ra4]), jnp.concatenate([b4, rb4])
    ra8, rb8 = send_x(a8), send_y(b8)
    mine = [a8, ra8, b8, rb8]
    return mine + [send_core(v) for v in mine]


def scatter(parts):
    nz, z, y, c, x = places()
    rows, cols = parts[0].shape
    r = rows // (4 * nz)
    parts = [p.reshape(nz, 2, 2, r, cols) for p in parts]
    take = lambda v, i, axis: lax.dynamic_index_in_dim(v, i, axis, keepdims=False)
    got = send_core(jnp.stack([take(p, 1 - c, 2) for p in parts]))
    low = lambda v: v.astype(bf16)
    add = lambda u, v: low(u.astype(f32) + v.astype(f32))
    mine = [add(take(p, c, 2), g) for p, g in zip(parts, got)]
    pick = lambda u, v: jnp.where(x == 0, u, v)
    a_send, a_keep = pick(mine[2], mine[0]), pick(mine[0], mine[2])
    b_send = jnp.stack([take(mine[1], 1 - y, 1), take(mine[3], 1 - y, 1)])
    b_keep = jnp.stack([take(mine[1], y, 1), take(mine[3], y, 1)])
    a = add(a_keep, send_x(a_send))
    b = add(b_keep, send_y(b_send))
    a2 = add(take(a, y, 1), send_y(take(a, 1 - y, 1)))
    b2 = add(take(b, x, 0), send_x(take(b, 1 - x, 0)))
    ab = jnp.stack([a2, b2], axis=1)
    total = take(ab, z, 0).astype(f32)
    for k in range(1, nz):
        total = total + send_z(take(ab, z ^ k, 0), k).astype(f32)
    total = low(total)
    other = send_x(total)
    lo, hi = pick(total, other), pick(other, total)
    return jnp.concatenate([lo[0], lo[1], hi[0], hi[1]], axis=1).astype(f32)


def passed_along(block, axis, distance):
    devices = range(lax.axis_size(axis))
    return lax.ppermute(block, axis, [(i - distance, i) for i in devices if i - distance in devices])


def norm_stats(x):
    center = x - jnp.mean(x, axis=-1, keepdims=True)
    spread_sq = jnp.mean(center * center, axis=-1, keepdims=True)
    r = lax.rsqrt(spread_sq + 1e-05)
    return center * r, r


def norm_back(grad, n, r, gain):
    gn = grad * gain
    return r * (gn - jnp.mean(gn, axis=-1, keepdims=True) - n * jnp.mean(gn * n, axis=-1, keepdims=True))


def assemble_kernel(at_ref, *refs, nz):
    pieces, out, buf, sems, osem = refs[:8], refs[8], refs[9], refs[10], refs[11]
    rows, cols = pieces[0].shape[1:]
    z, y, c, x = [at_ref[k] for k in range(4)]
    copies = []
    for kind in range(4):
        group = []
        for core in range(2):
            for i in range(2):
                for k in range(nz):
                    yy = (y ^ i) if kind < 2 else (y if kind == 2 else 1 - y)
                    xx = (x if kind == 0 else 1 - x) if kind < 2 else (x ^ i)
                    row = (((z ^ k) * 2 + yy) * 2 + (c if core == 0 else 1 - c)) * rows
                    col = (2 * xx + kind // 2) * cols
                    dst = buf.at[pl.ds(pl.multiple_of(row, rows), rows), pl.ds(pl.multiple_of(col, cols), cols)]
                    group.append(pltpu.make_async_copy(pieces[core * 4 + kind].at[i * nz + k], dst, sems.at[kind]))
        copies.append(group)
    for group in copies:
        for copy in group:
            copy.start()
    half = out.shape[1] // 2
    outs = []
    for group in copies:
        for copy in group:
            copy.wait()
    done = pltpu.make_async_copy(buf, out, osem)
    done.start()
    done.wait()


def assemble(pieces):
    nz, z, y, c, x = places()
    rows, cols = pieces[0].shape[1:]
    at = jnp.stack([z, y, c, x]).astype(jnp.int32)
    hbm = pl.BlockSpec(memory_space=pl.ANY)
    full = (nz * 4 * rows, 4 * cols)
    return pl.pallas_call(
        functools.partial(assemble_kernel, nz=nz),
        in_specs=[pl.BlockSpec(memory_space=pltpu.SMEM)] + [hbm] * 8,
        out_specs=hbm,
        out_shape=jax.ShapeDtypeStruct(full, bf16),
        scratch_shapes=[pltpu.VMEM(full, bf16), pltpu.SemaphoreType.DMA((4,)), pltpu.SemaphoreType.DMA],
        compiler_params=pltpu.CompilerParams(vmem_limit_bytes=20 << 20),
        cost_estimate=pl.CostEstimate(flops=0, bytes_accessed=4 * full[0] * full[1], transcendentals=0),
    )(at, *pieces)


def middle_kernel(att_ref, tok_ref, cot_ref, wo_ref, up_ref, dn_ref, bu_ref, bd_ref, gain_ref, shift_ref,
                  out_ref, one_ref, gm_ref, gup_ref, gdn_ref, gout_ref, gbu_ref, vec_ref,
                  res_ref, n_ref, low_ref, r_ref, acc_ref, gh_ref):
    j = pl.program_id(0)
    last = pl.num_programs(0) - 1
    width = tok_ref.shape[1]

    @pl.when(j == 0)
    def _():
        res = tok_ref[...].astype(f32) + nn(att_ref[...], wo_ref[...])
        res_ref[...] = res
        n, r = norm_stats(res)
        n_ref[...] = n
        r_ref[...] = r
        low_ref[...] = (n * gain_ref[...].astype(f32) + shift_ref[...].astype(f32)).astype(bf16)

    low = low_ref[...]
    cot = cot_ref[...]
    up = up_ref[...]
    dn = dn_ref[...]
    p = nn(low, up) + bu_ref[...].astype(f32)
    ga = nt(cot, dn)
    k0 = math.sqrt(2.0 / math.pi)
    p2 = p * p
    t = jnp.tanh(p * (k0 + (k0 * 0.044715) * p2))
    half = 0.5 * (1.0 + t)
    act = (p * half).astype(bf16)
    slope = half + 0.5 * p * (1.0 - t * t) * (k0 + (3.0 * k0 * 0.044715) * p2)
    gp = (ga * slope).astype(bf16)
    o = nn(act, dn)
    g = nt(gp, up)
    gup_ref[...] = tn(low, gp).astype(bf16)
    gd = tn(act, cot).astype(bf16)
    cols = width // 4
    for q in range(4):
        gdn_ref[q] = gd[:, q * cols : (q + 1) * cols]
    gbu_ref[...] = jnp.sum(gp.astype(f32), axis=0, keepdims=True)

    @pl.when(j == 0)
    def _():
        acc_ref[...] = o
        gh_ref[...] = g

    @pl.when(j > 0)
    def _():
        acc_ref[...] += o
        gh_ref[...] += g

    @pl.when(j == last)
    def _():
        out_ref[...] = (res_ref[...] + acc_ref[...] + bd_ref[...].astype(f32)).astype(bf16)
        gh = gh_ref[...]
        n = n_ref[...]
        cf = cot.astype(f32)
        vec_ref[0:1, :] = jnp.sum(gh * n, axis=0, keepdims=True)
        vec_ref[1:2, :] = jnp.sum(gh, axis=0, keepdims=True)
        vec_ref[2:3, :] = jnp.sum(cf, axis=0, keepdims=True)
        one = cf + norm_back(gh, n, r_ref[...], gain_ref[...].astype(f32))
        one_ref[...] = one
        ol = one.astype(bf16)
        gm_ref[...] = nt(ol, wo_ref[...])
        go = tn(att_ref[...], ol).astype(bf16)
        for q in range(4):
            gout_ref[q] = go[:, q * cols : (q + 1) * cols]


def middle(att, tok, cot, wo, up, dn, bu, bd, gain, shift):
    seg, width = tok.shape
    ff = up.shape[1]
    blk = 512
    per = ff // 4 // blk
    once = dict(pipeline_mode=pl.Buffered(1))
    whole = pl.BlockSpec((seg, width), lambda j: (0, 0), **once)
    vec = pl.BlockSpec((1, width), lambda j: (0, 0))
    q4 = width // 4
    return pl.pallas_call(
        middle_kernel,
        grid=(ff // blk,),
        in_specs=[whole, whole, whole, pl.BlockSpec((width, width), lambda j: (0, 0), **once),
                  pl.BlockSpec((width, blk), lambda j: (0, j)), pl.BlockSpec((blk, width), lambda j: (j, 0)),
                  pl.BlockSpec((1, blk), lambda j: (0, j)), vec, vec, vec],
        out_specs=[whole, whole, whole,
                   pl.BlockSpec((None, width, blk), lambda j: (j // per, 0, j % per)),
                   pl.BlockSpec((4, blk, q4), lambda j: (0, j, 0)),
                   pl.BlockSpec((4, width, q4), lambda j: (0, 0, 0), **once),
                   pl.BlockSpec((1, blk), lambda j: (0, j)),
                   pl.BlockSpec((8, width), lambda j: (0, 0))],
        out_shape=[jax.ShapeDtypeStruct((seg, width), bf16), jax.ShapeDtypeStruct((seg, width), f32), jax.ShapeDtypeStruct((seg, width), f32),
                   jax.ShapeDtypeStruct((4, width, ff // 4), bf16), jax.ShapeDtypeStruct((4, ff, q4), bf16), jax.ShapeDtypeStruct((4, width, q4), bf16),
                   jax.ShapeDtypeStruct((1, ff), f32), jax.ShapeDtypeStruct((8, width), f32)],
        scratch_shapes=[pltpu.VMEM((seg, width), f32)] * 2 + [pltpu.VMEM((seg, width), bf16), pltpu.VMEM((seg, 1), f32)] + [pltpu.VMEM((seg, width), f32)] * 2,
        compiler_params=pltpu.CompilerParams(vmem_limit_bytes=56 << 20),
        cost_estimate=pl.CostEstimate(flops=2 * seg * width * (6 * ff + 3 * width), bytes_accessed=8 * width * ff + 16 * seg * width, transcendentals=seg * ff),
    )(att, tok, cot, wo, up, dn, bu, bd, gain, shift)


def back_kernel(d_ref, w_ref, o_ref, acc_ref):
    j = pl.program_id(0)
    g = nt(d_ref[...], w_ref[...])

    @pl.when(j == 0)
    def _():
        acc_ref[...] = g

    @pl.when(j > 0)
    def _():
        acc_ref[...] += g

    @pl.when(j == pl.num_programs(0) - 1)
    def _():
        o_ref[...] = acc_ref[...].astype(bf16)


def before_grad(d_prev, w):
    _, seg, width = d_prev.shape
    blk = 512
    per = width // blk
    return pl.pallas_call(
        back_kernel,
        grid=(2 * per,),
        in_specs=[pl.BlockSpec((None, seg, blk), lambda j: (j // per, 0, j % per)), pl.BlockSpec((width, blk), lambda j: (0, per + j))],
        out_specs=pl.BlockSpec((seg, width), lambda j: (0, 0)),
        out_shape=jax.ShapeDtypeStruct((seg, width), bf16),
        scratch_shapes=[pltpu.VMEM((seg, width), f32)],
        compiler_params=pltpu.CompilerParams(vmem_limit_bytes=32 << 20),
        cost_estimate=pl.CostEstimate(flops=4 * seg * width * width, bytes_accessed=4 * width * width, transcendentals=0),
    )(d_prev, w)


def tail_kernel(dc_ref, dp_ref, nc_ref, np_ref, w_ref, g_ref, h_ref):
    j = pl.program_id(0)
    per = pl.num_programs(0) // 3
    dc = dc_ref[...]
    h = nt(dc, w_ref[...])

    @pl.when(j == 0)
    def _():
        h_ref[...] = h

    @pl.when(j > 0)
    def _():
        h_ref[...] += h

    @pl.when(j < per)
    def _():
        g_ref[...] = tn(nc_ref[...], dc).astype(bf16)

    @pl.when(j >= per)
    def _():
        g_ref[...] = (tn(nc_ref[...], dc) + tn(np_ref[...], dp_ref[...])).astype(bf16)


def qkv_back(d_cur, d_prev, n_cur, n_prev, w):
    _, seg, width = d_cur.shape
    blk = 256
    per = width // blk
    quarter = 3 * width // 4
    pq = quarter // blk
    whole = pl.BlockSpec((seg, width), lambda j: (0, 0))
    return pl.pallas_call(
        tail_kernel,
        grid=(3 * per,),
        in_specs=[pl.BlockSpec((None, seg, blk), lambda j: (j // per, 0, j % per)),
                  pl.BlockSpec((None, seg, blk), lambda j: (jnp.maximum(j // per - 1, 0), 0, jnp.where(j < per, 0, j % per))),
                  whole, whole, pl.BlockSpec((width, blk), lambda j: (0, j))],
        out_specs=[pl.BlockSpec((None, width, blk), lambda j: (j // pq, 0, j % pq)), whole],
        out_shape=[jax.ShapeDtypeStruct((4, width, quarter), bf16), jax.ShapeDtypeStruct((seg, width), f32)],
        compiler_params=pltpu.CompilerParams(vmem_limit_bytes=40 << 20),
        cost_estimate=pl.CostEstimate(flops=2 * seg * width * width * 8, bytes_accessed=12 * width * width + 16 * seg * width, transcendentals=0),
    )(d_cur, d_prev, n_cur, n_prev, w)


def last_kernel(h_ref, back_ref, tok_ref, one_ref, gain_ref, out_ref, vec_ref):
    h = h_ref[...] + back_ref[...].astype(f32)
    n, r = norm_stats(tok_ref[...].astype(f32))
    vec_ref[0:1, :] = jnp.sum(h * n, axis=0, keepdims=True)
    vec_ref[1:2, :] = jnp.sum(h, axis=0, keepdims=True)
    out_ref[...] = one_ref[...] + norm_back(h, n, r, gain_ref[...].astype(f32))


def finish(h, back, tok, one, gain):
    seg, width = tok.shape
    return pl.pallas_call(
        last_kernel,
        out_shape=[jax.ShapeDtypeStruct((seg, width), f32), jax.ShapeDtypeStruct((8, width), f32)],
        compiler_params=pltpu.CompilerParams(vmem_limit_bytes=40 << 20),
        cost_estimate=pl.CostEstimate(flops=20 * seg * width, bytes_accessed=16 * seg * width, transcendentals=0),
    )(h, back, tok, one, gain)


def qkv_kernel(xp_ref, xc_ref, gain_ref, shift_ref, w_ref, q_ref, kp_ref, kc_ref, vp_ref, vc_ref, rq_ref, rkp_ref, rkc_ref, np_ref, nc_ref, x_ref, *, dh):
    i = pl.program_id(0)
    per = pl.num_programs(0) // 3
    seg = xc_ref.shape[0]

    @pl.when(i == 0)
    def _():
        gain = gain_ref[...].astype(f32)
        shift = shift_ref[...].astype(f32)
        for src, dst, at in ((xp_ref, np_ref, 0), (xc_ref, nc_ref, seg)):
            n, r = norm_stats(src[...].astype(f32))
            low = (n * gain + shift).astype(bf16)
            x_ref[at : at + seg, :] = low
            dst[...] = low

    def unit(y, out_ref, r_ref):
        for k in range(y.shape[1] // dh):
            part = y[:, k * dh : (k + 1) * dh]
            r = lax.rsqrt(jnp.sum(part * part, axis=1, keepdims=True) + 1e-06)
            out_ref[:, k * dh : (k + 1) * dh] = (part * r).astype(bf16)
            r_ref[k] = r

    w = w_ref[...]

    @pl.when(i < per)
    def _():
        unit(nn(x_ref[seg:, :], w), q_ref, rq_ref)

    @pl.when((i >= per) & (i < 2 * per))
    def _():
        unit(nn(x_ref[:seg, :], w), kp_ref, rkp_ref)
        unit(nn(x_ref[seg:, :], w), kc_ref, rkc_ref)

    @pl.when(i >= 2 * per)
    def _():
        vp_ref[...] = nn(x_ref[:seg, :], w).astype(bf16)
        vc_ref[...] = nn(x_ref[seg:, :], w).astype(bf16)


def project_qkv(xp, xc, gain, shift, w, heads):
    seg, width = xc.shape
    dh = width // heads
    two = 2 * dh
    per = width // two
    whole = pl.BlockSpec((seg, width), lambda i: (0, 0))
    vec = pl.BlockSpec((1, width), lambda i: (0, 0))
    at = lambda s: (lambda i: (0, jnp.clip(i - s * per, 0, per - 1)))
    at3 = lambda s: (lambda i: (jnp.clip(i - s * per, 0, per - 1), 0, 0))
    cols = lambda s: pl.BlockSpec((seg, two), at(s))
    rs = lambda s: pl.BlockSpec((2, seg, 1), at3(s))
    low = jax.ShapeDtypeStruct((seg, width), bf16)
    rr = jax.ShapeDtypeStruct((heads, seg, 1), f32)
    return pl.pallas_call(
        functools.partial(qkv_kernel, dh=dh),
        grid=(3 * per,),
        in_specs=[whole, whole, vec, vec, pl.BlockSpec((width, two), lambda i: (0, i))],
        out_specs=[cols(0), cols(1), cols(1), cols(2), cols(2), rs(0), rs(1), rs(1), whole, whole],
        out_shape=[low] * 5 + [rr] * 3 + [low] * 2,
        scratch_shapes=[pltpu.VMEM((2 * seg, width), bf16)],
        compiler_params=pltpu.CompilerParams(vmem_limit_bytes=48 << 20),
        cost_estimate=pl.CostEstimate(flops=2 * seg * width * width * 5, bytes_accessed=3 * width * width * 2 + 9 * seg * width * 2, transcendentals=0),
    )(xp, xc, gain, shift, w)


def gather_weights(ws):
    n = lax.axis_size("fsdp")
    if n > 16 or any(w.shape[0] % 16 for w in ws):
        return [lax.all_gather(w, "fsdp", axis=0, tiled=True) for w in ws]
    outs, gate = [], None
    for w in ws:
        got = gather_start(w, gate)
        gate = got[1:]
        outs.append(assemble(gather_rest(got)))
    return outs


def scatter_weights(gs):
    n = lax.axis_size("fsdp")
    if n > 16:
        whole = [jnp.concatenate([g[q] for q in range(4)], axis=1) for g in gs]
        got = [lax.psum_scatter(g, "fsdp", scatter_dimension=0, tiled=True) for g in whole]
        return [g.astype(f32) for g in lax.psum(got, "stream")]
    return [scatter([g[q] for q in range(4)]) for g in gs]


def summed_everywhere(v):
    bit = 1
    while bit < lax.axis_size("fsdp"):
        v = v + lax.ppermute(v, "fsdp", xor_perm(bit, lax.axis_size("fsdp")))
        bit *= 2
    return v + send_x(v)


def local(
    tokens, resets, retrieved, memory_keys, memory_values, qkv_weight, out_weight, up_weight, up_bias,
    down_weight, down_bias, attn_gain, attn_shift, ffn_gain, ffn_shift, position_bias, memory_gate, cotangent,
):
    heads = memory_gate.shape[0]
    seg, width = tokens.shape[1:]
    dh = width // heads
    mem_rows = memory_keys.shape[1]
    shards = lax.axis_size("fsdp")
    mem = mem_rows * shards
    part = width // shards
    bias_part = up_bias.shape[0]
    pos_part = position_bias.shape[0]
    keys = memory_keys[0].astype(f32).reshape(mem_rows, heads, dh)
    keys = keys * lax.rsqrt(jnp.sum(keys * keys, axis=-1, keepdims=True) + 1e-06)
    small = jnp.concatenate([up_bias, down_bias, attn_gain, attn_shift, ffn_gain, ffn_shift, position_bias])
    small = jnp.pad(small, (0, width - small.shape[0]))[None]
    pack = jnp.concatenate([keys.reshape(mem_rows, width).astype(bf16), memory_values[0], jnp.pad(small, ((0, 15), (0, 0)))], axis=0)
    pack = lax.all_gather(pack, "fsdp", axis=0)
    mk = pack[:, :mem_rows].reshape(mem, width)
    mv = pack[:, mem_rows : 2 * mem_rows].reshape(mem, width)
    small = pack[:, 2 * mem_rows]
    b_up = small[:, :bias_part].reshape(-1)
    vecs = [small[:, bias_part + k * part : bias_part + (k + 1) * part].reshape(1, -1) for k in range(5)]
    b_down, gain_one, shift_one, gain_two, shift_two = vecs
    table = small[:, bias_part + 5 * part : bias_part + 5 * part + pos_part].reshape(heads, -1).astype(f32)
    w_qkv, w_out, w_up, w_down = gather_weights((qkv_weight, out_weight, up_weight, down_weight))
    before = passed_along(tokens[0], "fsdp", 1)
    mask = picked_masks(retrieved[0].transpose(1, 0, 2), mem)
    hot, rel = bucket_hot(seg)
    base = diagonal_bias(table, hot, rel)
    gate = jax.nn.sigmoid(memory_gate.astype(f32))
    reset = resets[0]
    q, kp, kc, vp, vc, rq, rkp, rkc, n_prev, n_cur = project_qkv(before, tokens[0], gain_one, shift_one, w_qkv, heads)
    attn_in, loc, rem = attn_fwd(gate, reset, q, kp, kc, vp, vc, base, mk, mv, mask)
    output, grad_one, gm, up_g, down_g, out_g, up_bias_g, vec_two = middle(
        attn_in, tokens[0], cotangent[0], w_out, w_up, w_down, b_up.reshape(1, -1), b_down, gain_two, shift_two)
    up_t, down_t, out_t = scatter_weights((up_g, down_g, out_g))
    d_cur, d_prev, diag, dgate = attn_bwd(gate, reset, q, kp, kc, vp, vc, rq, rkp, rkc, base, mk, mv, mask, loc, rem, gm)
    gate_g = dgate[:, 0, 0]
    table_g = jnp.dot(diag[:, 0], hot.T, precision=lax.Precision.HIGHEST)
    back = passed_along(before_grad(d_prev, w_qkv), "fsdp", -1)
    qkv_g, grad_h1 = qkv_back(d_cur, d_prev, n_cur, n_prev, w_qkv)
    (qkv_t,) = scatter_weights((qkv_g,))
    token_grad, vec_one = finish(grad_h1, back, tokens[0], grad_one, gain_one)
    gain_two_g, shift_two_g, down_bias_g = vec_two[0], vec_two[1], vec_two[2]
    gain_one_g, shift_one_g = vec_one[0], vec_one[1]
    small_g = jnp.concatenate(
        [up_bias_g.reshape(shards, -1)]
        + [v.reshape(shards, -1) for v in (down_bias_g, gain_one_g, shift_one_g, gain_two_g, shift_two_g, table_g)]
        + [jnp.broadcast_to(gate_g[None], (shards, heads))],
        axis=1,
    )
    small_g = summed_everywhere(small_g)
    small_g = lax.dynamic_index_in_dim(small_g, lax.axis_index("fsdp"), 0, keepdims=False)
    cuts = [bias_part] + [part] * 5 + [pos_part, heads]
    at = 0
    outs = []
    for c in cuts:
        outs.append(small_g[at : at + c])
        at += c
    ub, db, g1, s1, g2, s2, pg, gg = outs
    return output[None], token_grad[None], qkv_t, out_t, up_t, ub, down_t, db, g1, s1, g2, s2, pg, gg


def solution(mesh):
    row = P("stream", "fsdp", None)
    return jax.shard_map(
        local,
        mesh=mesh,
        in_specs=(
            row, P("stream", "fsdp"), P("stream", "fsdp", None, None), row, row, P("fsdp", None), P("fsdp", None),
            P("fsdp", None), P("fsdp"), P("fsdp", None), P("fsdp"), P("fsdp"), P("fsdp"), P("fsdp"), P("fsdp"),
            P("fsdp"), P(), row,
        ),
        out_specs=(
            row, row, P("fsdp", None), P("fsdp", None), P("fsdp", None), P("fsdp"), P("fsdp", None), P("fsdp"),
            P("fsdp"), P("fsdp"), P("fsdp"), P("fsdp"), P("fsdp"), P(),
        ),
        check_vma=False,
    )
```

```python
import functools
import math
import jax, jax.numpy as jnp
from jax import lax
from jax.experimental import pallas as pl
from jax.experimental.pallas import tpu as pltpu
f32=jnp.float32; bf16=jnp.bfloat16
LOG2E=math.log2(math.e)
NEG=-1e30

def nt(a,b): return lax.dot_general(a,b,(((1,),(1,)),((),())),preferred_element_type=f32)
def nn(a,b): return lax.dot_general(a,b,(((1,),(0,)),((),())),preferred_element_type=f32)
def tn(a,b): return lax.dot_general(a,b,(((0,),(0,)),((),())),preferred_element_type=f32)

from jax.experimental.layout import Layout, with_layout_constraint
from jax.sharding import PartitionSpec as P


def xor_perm(bit, n):
    return [(i, i ^ bit) for i in range(n)]


def places():
    n = lax.axis_size("fsdp")
    i = lax.axis_index("fsdp")
    return n // 4, i // 4, (i // 2) % 2, i % 2, lax.axis_index("stream")


def send_core(v):
    return lax.ppermute(v, "fsdp", xor_perm(1, lax.axis_size("fsdp")))


def send_y(v):
    return lax.ppermute(v, "fsdp", xor_perm(2, lax.axis_size("fsdp")))


def send_z(v, k):
    return lax.ppermute(v, "fsdp", xor_perm(4 * k, lax.axis_size("fsdp")))


def send_x(v):
    return lax.ppermute(v, "stream", [(0, 1), (1, 0)])


def gather_small(memory_keys, memory_values, vectors, heads):
    mem_rows, width = memory_keys.shape[1:]
    keys = memory_keys[0].astype(f32).reshape(mem_rows, heads, width // heads)
    keys = keys * lax.rsqrt(jnp.sum(keys * keys, axis=-1, keepdims=True) + 1e-06)
    small = jnp.concatenate(vectors)
    small = jnp.pad(small[None], ((0, 15), (0, width - small.shape[0])))
    pack = jnp.concatenate([keys.reshape(mem_rows, width).astype(bf16), memory_values[0], small], axis=0)
    pack = lax.all_gather(pack, "fsdp", axis=0)
    return pack[:, 2 * mem_rows], pack[:, :mem_rows].reshape(-1, width), pack[:, mem_rows : 2 * mem_rows].reshape(-1, width)


def scatter_weights(gs):
    whole = [jnp.concatenate([g[q] for q in range(4)], axis=1) for g in gs]
    got = [lax.psum_scatter(g, "fsdp", scatter_dimension=0, tiled=True) for g in whole]
    return [g.astype(f32) for g in lax.psum(got, "stream")]


def summed_everywhere(v):
    bit = 1
    while bit < lax.axis_size("fsdp"):
        v = v + lax.ppermute(v, "fsdp", xor_perm(bit, lax.axis_size("fsdp")))
        bit *= 2
    return v + send_x(v)


def passed_along(block, axis, distance):
    devices = range(lax.axis_size(axis))
    return lax.ppermute(block, axis, [(i - distance, i) for i in devices if i - distance in devices])


def norm_stats(x):
    center = x - jnp.mean(x, axis=-1, keepdims=True)
    spread_sq = jnp.mean(center * center, axis=-1, keepdims=True)
    r = lax.rsqrt(spread_sq + 1e-05)
    return center * r, r


def norm_back(grad, n, r, gain):
    gn = grad * gain
    return r * (gn - jnp.mean(gn, axis=-1, keepdims=True) - n * jnp.mean(gn * n, axis=-1, keepdims=True))


def mask_kernel(p_ref, o_ref, *, rows):
    n, k = p_ref.shape
    mem = o_ref.shape[1]
    for r in range(0, n, rows):
        p = p_ref[r:r+rows, :]
        ids = lax.broadcasted_iota(jnp.int32, (rows, mem), 1)
        hit = p[:, 0:1] == ids
        for t in range(1, k):
            hit = hit | (p[:, t:t+1] == ids)
        o_ref[r:r+rows, :] = jnp.where(hit, 1.0, 0.0).astype(bf16)

def picked_masks(picked, mem, interpret=False):
    h, n, k = picked.shape
    return pl.pallas_call(
        functools.partial(mask_kernel, rows=32),
        grid=(h,),
        in_specs=[pl.BlockSpec((None, n, k), lambda i: (i,0,0))],
        out_specs=pl.BlockSpec((None, n, mem), lambda i: (i,0,0)),
        out_shape=jax.ShapeDtypeStruct((h,n,mem), bf16),
        cost_estimate=pl.CostEstimate(flops=2*h*n*k*mem, bytes_accessed=h*n*(mem*2+512), transcendentals=0),
        interpret=interpret,
    )(picked)

def spread(base, blk):
    w = base.shape[1]
    x = jnp.broadcast_to(base, (8, w))
    r = lax.broadcasted_iota(jnp.int32, (8, w), 0)
    for b in (1, 2, 4):
        x = jnp.where((r & b) != 0, pltpu.roll(x, b, 1), x)
    size = 8
    while size < blk:
        x = jnp.concatenate([x, pltpu.roll(x, size, 1)], axis=0)
        size *= 2
    return x

def gather_diagonals(g):
    size, w = g.shape
    while size > 8:
        half = size // 2
        g = g[:half] + pltpu.roll(g[half:], w - half, 1)
        size = half
    r = lax.broadcasted_iota(jnp.int32, (8, w), 0)
    for b in (4, 2, 1):
        g = jnp.where((r & b) != 0, pltpu.roll(g, w - b, 1), g)
    return jnp.sum(g, axis=0, keepdims=True)

BLK = 128

def unit_back(g, u, r):
    u = u.astype(f32)
    return (r * (g - u * jnp.sum(g * u, axis=1, keepdims=True))).astype(bf16)

edges=[b for b in range(1,16)]+[int(math.ceil(16.0*8.0**((b-16)/16.0))) for b in range(16,32)]
def diagonal_rel(seg):
    wt = 2*seg + seg - BLK + BLK
    k = jnp.arange(wt, dtype=jnp.int32)
    top = 2*seg - BLK
    return jnp.where(k > wt - BLK, top - (k - wt), top - k)

def bucket_hot(seg):
    rel = diagonal_rel(seg)
    counts = jnp.zeros_like(rel)
    for e in edges: counts = counts + (rel >= e).astype(jnp.int32)
    hot = (counts[None,:] == jnp.arange(len(edges)+1)[:,None]) & (rel >= 0)[None,:]
    return hot.astype(f32), rel
def diagonal_bias(table, hot, rel):
    v = jnp.dot(table, hot, precision=lax.Precision.HIGHEST) * LOG2E
    return jnp.where(rel[None,:] >= 0, v, NEG)[:, None, :]


def wide_fwd_kernel(gate_ref, reset_ref, q_ref, kp_ref, kc_ref, vp_ref, vc_ref, base_ref, mk_ref, mv_ref, mask_ref,
                    mix_ref, loc_ref, rem_ref, t_ref):
    seg = q_ref.shape[0]
    h = pl.program_id(0)
    s = gate_ref[h]
    keep = jnp.where(reset_ref[0] == 0, 1.0, 0.0).astype(f32)
    t_ref[...] = spread(base_ref[...], BLK)
    heat = 16.0 * LOG2E
    nb = seg // BLK
    vp = vp_ref[...] * keep.astype(bf16)
    mk = mk_ref[...]; mv = mv_ref[...]
    for i in range(nb):
        rows = slice(i*BLK, (i+1)*BLK)
        q = q_ref[rows, :]
        off = (nb-1-i)*BLK
        cw = (i+1)*BLK
        ep = jnp.exp2(nt(q, kp_ref[...]) * heat + t_ref[:, off:off+seg])
        ec = jnp.exp2(nt(q, kc_ref[:cw, :]) * heat + t_ref[:, off+seg:off+seg+cw])
        il = 1.0 / (keep * jnp.sum(ep, axis=1, keepdims=True) + jnp.sum(ec, axis=1, keepdims=True))
        o = nn((ep * il).astype(bf16), vp) + nn((ec * il).astype(bf16), vc_ref[:cw, :])
        em = jnp.exp2(nt(q, mk) * heat) * mask_ref[rows, :].astype(f32)
        em = em * (1.0 / jnp.sum(em, axis=1, keepdims=True))
        om = nn(em.astype(bf16), mv)
        loc_ref[rows, :] = o.astype(bf16)
        rem_ref[rows, :] = om.astype(bf16)
        mix_ref[rows, :] = (s*om + (1.0-s)*o).astype(bf16)

def attn_fwd(gate, reset, q, kp, kc, vp, vc, base, mk, mv, mask, interpret=False):
    seg, width = q.shape
    heads = base.shape[0]
    dh = width // heads
    mem = mk.shape[0]
    col = lambda n: pl.BlockSpec((n, dh), lambda h, *_: (0, h))
    full = jax.ShapeDtypeStruct((seg, width), bf16)
    wt = base.shape[2]
    return pl.pallas_call(
        wide_fwd_kernel,
        grid_spec=pltpu.PrefetchScalarGridSpec(
            num_scalar_prefetch=2, grid=(heads,),
            in_specs=[col(seg), col(seg), col(seg), col(seg), col(seg),
                      pl.BlockSpec((None,1,wt), lambda h,*_: (h,0,0)), col(mem), col(mem),
                      pl.BlockSpec((None,seg,mem), lambda h,*_: (h,0,0))],
            out_specs=[col(seg), col(seg), col(seg)],
            scratch_shapes=[pltpu.VMEM((BLK, wt), f32)]),
        out_shape=[full, full, full],
        compiler_params=pltpu.CompilerParams(vmem_limit_bytes=48<<20),
        cost_estimate=pl.CostEstimate(flops=heads*seg*(2*seg+mem)*4*dh, bytes_accessed=8*seg*width*2+heads*seg*mem*2, transcendentals=heads*seg*(2*seg+mem)),
        interpret=interpret,
    )(gate, reset, q, kp, kc, vp, vc, base, mk, mv, mask)

def wide_bwd_kernel(gate_ref, reset_ref, q_ref, kp_ref, kc_ref, vp_ref, vc_ref, base_ref, mk_ref, mv_ref, mask_ref,
                    loc_ref, rem_ref, gm_ref, rq_ref, rkp_ref, rkc_ref,
                    dc_ref, dp_ref, diag_ref, dgate_ref, t_ref, g_ref, akp, akc, avp, avc):
    seg = q_ref.shape[0]
    h = pl.program_id(0)
    s = gate_ref[h]
    keep = jnp.where(reset_ref[0] == 0, 1.0, 0.0).astype(f32)
    t_ref[...] = spread(base_ref[...], BLK)
    g_ref[...] = jnp.zeros_like(g_ref)
    heat = 16.0 * LOG2E
    nb = seg // BLK
    mk = mk_ref[...]; mv = mv_ref[...]
    dg = jnp.zeros((BLK, 1), f32)
    for i in range(nb):
        rows = slice(i*BLK, (i+1)*BLK)
        q = q_ref[rows, :]
        gm = gm_ref[rows, :]
        off = (nb-1-i)*BLK
        cw = (i+1)*BLK
        al = jnp.sum(gm * loc_ref[rows, :].astype(f32), axis=1, keepdims=True)
        ar = jnp.sum(gm * rem_ref[rows, :].astype(f32), axis=1, keepdims=True)
        dg = dg + (ar - al)
        gl = ((1.0-s)*gm).astype(bf16)
        gr = (s*gm).astype(bf16)
        ep = jnp.exp2(nt(q, kp_ref[...]) * heat + t_ref[:, off:off+seg])
        ec = jnp.exp2(nt(q, kc_ref[:cw, :]) * heat + t_ref[:, off+seg:off+seg+cw])
        l = keep * jnp.sum(ep, axis=1, keepdims=True) + jnp.sum(ec, axis=1, keepdims=True)
        il = 1.0 / l
        ilp = il * keep
        pp = ep * ilp
        pc = ec * il
        wp = pp * nt(gl, vp_ref[...])
        wc = pc * nt(gl, vc_ref[:cw, :])
        dl = jnp.sum(wp, axis=1, keepdims=True) + jnp.sum(wc, axis=1, keepdims=True)
        dsp = (wp - pp * dl).astype(bf16); dsc = (wc - pc * dl).astype(bf16)
        g_ref[:, off:off+seg] += dsp.astype(f32)
        g_ref[:, off+seg:off+seg+cw] += dsc.astype(f32)
        dq = nn(dsp, kp_ref[...]) + nn(dsc, kc_ref[:cw, :])
        ppb = pp.astype(bf16); pcb = pc.astype(bf16)
        dkp = tn(dsp, q); dvp = tn(ppb, gl)
        dkc = tn(dsc, q); dvc = tn(pcb, gl)
        if i == 0:
            akp[...] = dkp; avp[...] = dvp
            akc[...] = jnp.zeros_like(akc); avc[...] = jnp.zeros_like(avc)
            akc[:cw, :] = dkc; avc[:cw, :] = dvc
        else:
            akp[...] += dkp; avp[...] += dvp
            akc[:cw, :] += dkc; avc[:cw, :] += dvc
        em = jnp.exp2(nt(q, mk) * heat) * mask_ref[rows, :].astype(f32)
        ilm = 1.0 / jnp.sum(em, axis=1, keepdims=True)
        em = em * ilm
        gw = nt(gr, mv)
        dsm = em * (gw - jnp.sum(em * gw, axis=1, keepdims=True))
        dq = dq + nn(dsm.astype(bf16), mk)
        dc_ref[0, rows, :] = unit_back(16.0 * dq, q, rq_ref[rows, :])
    dp_ref[0] = unit_back(16.0 * akp[...], kp_ref[...], rkp_ref[...])
    dc_ref[1] = unit_back(16.0 * akc[...], kc_ref[...], rkc_ref[...])
    dp_ref[1] = avp[...].astype(bf16)
    dc_ref[2] = avc[...].astype(bf16)
    diag_ref[...] = gather_diagonals(g_ref[...])
    dgate_ref[...] = jnp.broadcast_to(jnp.sum(dg) * s * (1.0-s), dgate_ref.shape)

def attn_bwd(gate, reset, q, kp, kc, vp, vc, rq, rkp, rkc, base, mk, mv, mask, loc, rem, gm, interpret=False):
    seg, width = q.shape
    heads = base.shape[0]
    dh = width // heads
    mem = mk.shape[0]
    wt = base.shape[2]
    col = lambda n: pl.BlockSpec((n, dh), lambda h, *_: (0, h))
    row = lambda w: pl.BlockSpec((None,1,w), lambda h,*_: (h,0,0))
    rcol = pl.BlockSpec((None,seg,1), lambda h,*_: (h,0,0))
    fb = jax.ShapeDtypeStruct((seg, width), bf16)
    return pl.pallas_call(
        wide_bwd_kernel,
        grid_spec=pltpu.PrefetchScalarGridSpec(
            num_scalar_prefetch=2, grid=(heads,),
            in_specs=[col(seg)]*5 + [row(wt), col(mem), col(mem),
                      pl.BlockSpec((None,seg,mem), lambda h,*_: (h,0,0)), col(seg), col(seg), col(seg), rcol, rcol, rcol],
            out_specs=[pl.BlockSpec((3,seg,dh), lambda h,*_: (0,0,h)), pl.BlockSpec((2,seg,dh), lambda h,*_: (0,0,h)), row(wt), row(128)],
            scratch_shapes=[pltpu.VMEM((BLK, wt), f32)]*2 + [pltpu.VMEM((seg, dh), f32)]*4),
        out_shape=[jax.ShapeDtypeStruct((3,seg,width),bf16), jax.ShapeDtypeStruct((2,seg,width),bf16), jax.ShapeDtypeStruct((heads,1,wt), f32), jax.ShapeDtypeStruct((heads,1,128), f32)],
        compiler_params=pltpu.CompilerParams(vmem_limit_bytes=48<<20),
        cost_estimate=pl.CostEstimate(flops=heads*seg*(2*seg+mem)*10*dh, bytes_accessed=20*seg*width*2+heads*seg*mem*2, transcendentals=heads*seg*(2*seg+mem)),
        interpret=interpret,
    )(gate, reset, q, kp, kc, vp, vc, base, mk, mv, mask, loc, rem, gm, rq, rkp, rkc)


def wide_qkv_kernel(xp_ref, xc_ref, gain_ref, shift_ref, w_ref, q_ref, kp_ref, kc_ref, vp_ref, vc_ref, rq_ref, rkp_ref, rkc_ref, np_ref, nc_ref, x_ref, *, dh):
    i = pl.program_id(0)
    per = pl.num_programs(0) // 3
    seg = xc_ref.shape[0]

    @pl.when(i == 0)
    def _():
        gain = gain_ref[...].astype(f32)
        shift = shift_ref[...].astype(f32)
        for src, dst, at in ((xp_ref, np_ref, 0), (xc_ref, nc_ref, seg)):
            n, r = norm_stats(src[...].astype(f32))
            low = (n * gain + shift).astype(bf16)
            x_ref[at : at + seg, :] = low
            dst[...] = low

    def unit(y, out_ref, r_ref):
        for k in range(y.shape[1] // dh):
            part = y[:, k * dh : (k + 1) * dh]
            r = lax.rsqrt(jnp.sum(part * part, axis=1, keepdims=True) + 1e-06)
            out_ref[:, k * dh : (k + 1) * dh] = (part * r).astype(bf16)
            r_ref[k] = r

    w = w_ref[...]

    @pl.when(i < per)
    def _():
        unit(nn(x_ref[seg:, :], w), q_ref, rq_ref)

    @pl.when((i >= per) & (i < 2 * per))
    def _():
        unit(nn(x_ref[:seg, :], w), kp_ref, rkp_ref)
        unit(nn(x_ref[seg:, :], w), kc_ref, rkc_ref)

    @pl.when(i >= 2 * per)
    def _():
        vp_ref[...] = nn(x_ref[:seg, :], w).astype(bf16)
        vc_ref[...] = nn(x_ref[seg:, :], w).astype(bf16)


def project_qkv(xp, xc, gain, shift, w, heads):
    seg, width = xc.shape
    dh = width // heads
    two = 2 * dh
    per = width // two
    whole = pl.BlockSpec((seg, width), lambda i: (0, 0))
    vec = pl.BlockSpec((1, width), lambda i: (0, 0))
    at = lambda s: (lambda i: (0, jnp.clip(i - s * per, 0, per - 1)))
    at3 = lambda s: (lambda i: (jnp.clip(i - s * per, 0, per - 1), 0, 0))
    cols = lambda s: pl.BlockSpec((seg, two), at(s))
    rs = lambda s: pl.BlockSpec((2, seg, 1), at3(s))
    low = jax.ShapeDtypeStruct((seg, width), bf16)
    rr = jax.ShapeDtypeStruct((heads, seg, 1), f32)
    return pl.pallas_call(
        functools.partial(wide_qkv_kernel, dh=dh),
        grid=(3 * per,),
        in_specs=[whole, whole, vec, vec, pl.BlockSpec((width, two), lambda i: (0, i))],
        out_specs=[cols(0), cols(1), cols(1), cols(2), cols(2), rs(0), rs(1), rs(1), whole, whole],
        out_shape=[low] * 5 + [rr] * 3 + [low] * 2,
        scratch_shapes=[pltpu.VMEM((2 * seg, width), bf16)],
        compiler_params=pltpu.CompilerParams(vmem_limit_bytes=48 << 20),
        cost_estimate=pl.CostEstimate(flops=2 * seg * width * width * 5, bytes_accessed=3 * width * width * 2 + 9 * seg * width * 2, transcendentals=0),
    )(xp, xc, gain, shift, w)


def middle_kernel(att_ref, tok_ref, cot_ref, wo_ref, up_ref, dn_ref, bu_ref, bd_ref, gain_ref, shift_ref,
                  out_ref, one_ref, gm_ref, gup_ref, gdn_ref, gout_ref, gbu_ref, vec_ref,
                  res_ref, n_ref, low_ref, r_ref, acc_ref, gh_ref):
    j = pl.program_id(0)
    last = pl.num_programs(0) - 1
    width = tok_ref.shape[1]

    @pl.when(j == 0)
    def _():
        res = tok_ref[...].astype(f32) + nn(att_ref[...], wo_ref[...])
        res_ref[...] = res
        n, r = norm_stats(res)
        n_ref[...] = n
        r_ref[...] = r
        low_ref[...] = (n * gain_ref[...].astype(f32) + shift_ref[...].astype(f32)).astype(bf16)

    low = low_ref[...]
    cot = cot_ref[...]
    up = up_ref[...]
    dn = dn_ref[...]
    p = nn(low, up) + bu_ref[...].astype(f32)
    ga = nt(cot, dn)
    k0 = math.sqrt(2.0 / math.pi)
    p2 = p * p
    t = jnp.tanh(p * (k0 + (k0 * 0.044715) * p2))
    half = 0.5 * (1.0 + t)
    act = (p * half).astype(bf16)
    slope = half + 0.5 * p * (1.0 - t * t) * (k0 + (3.0 * k0 * 0.044715) * p2)
    gp = (ga * slope).astype(bf16)
    o = nn(act, dn)
    g = nt(gp, up)
    gup_ref[...] = tn(low, gp).astype(bf16)
    gd = tn(act, cot).astype(bf16)
    cols = width // 4
    for q in range(4):
        gdn_ref[q] = gd[:, q * cols : (q + 1) * cols]
    gbu_ref[...] = jnp.sum(gp.astype(f32), axis=0, keepdims=True)

    @pl.when(j == 0)
    def _():
        acc_ref[...] = o
        gh_ref[...] = g

    @pl.when(j > 0)
    def _():
        acc_ref[...] += o
        gh_ref[...] += g

    @pl.when(j == last)
    def _():
        out_ref[...] = (res_ref[...] + acc_ref[...] + bd_ref[...].astype(f32)).astype(bf16)
        gh = gh_ref[...]
        n = n_ref[...]
        cf = cot.astype(f32)
        vec_ref[0:1, :] = jnp.sum(gh * n, axis=0, keepdims=True)
        vec_ref[1:2, :] = jnp.sum(gh, axis=0, keepdims=True)
        vec_ref[2:3, :] = jnp.sum(cf, axis=0, keepdims=True)
        one = cf + norm_back(gh, n, r_ref[...], gain_ref[...].astype(f32))
        one_ref[...] = one
        ol = one.astype(bf16)
        gm_ref[...] = nt(ol, wo_ref[...])
        go = tn(att_ref[...], ol).astype(bf16)
        for q in range(4):
            gout_ref[q] = go[:, q * cols : (q + 1) * cols]


def middle(att, tok, cot, wo, up, dn, bu, bd, gain, shift):
    seg, width = tok.shape
    ff = up.shape[1]
    blk = 512
    per = ff // 4 // blk
    once = dict(pipeline_mode=pl.Buffered(1))
    whole = pl.BlockSpec((seg, width), lambda j: (0, 0), **once)
    vec = pl.BlockSpec((1, width), lambda j: (0, 0))
    q4 = width // 4
    return pl.pallas_call(
        middle_kernel,
        grid=(ff // blk,),
        in_specs=[whole, whole, whole, pl.BlockSpec((width, width), lambda j: (0, 0), **once),
                  pl.BlockSpec((width, blk), lambda j: (0, j)), pl.BlockSpec((blk, width), lambda j: (j, 0)),
                  pl.BlockSpec((1, blk), lambda j: (0, j)), vec, vec, vec],
        out_specs=[whole, whole, whole,
                   pl.BlockSpec((None, width, blk), lambda j: (j // per, 0, j % per)),
                   pl.BlockSpec((4, blk, q4), lambda j: (0, j, 0)),
                   pl.BlockSpec((4, width, q4), lambda j: (0, 0, 0), **once),
                   pl.BlockSpec((1, blk), lambda j: (0, j)),
                   pl.BlockSpec((8, width), lambda j: (0, 0))],
        out_shape=[jax.ShapeDtypeStruct((seg, width), bf16), jax.ShapeDtypeStruct((seg, width), f32), jax.ShapeDtypeStruct((seg, width), f32),
                   jax.ShapeDtypeStruct((4, width, ff // 4), bf16), jax.ShapeDtypeStruct((4, ff, q4), bf16), jax.ShapeDtypeStruct((4, width, q4), bf16),
                   jax.ShapeDtypeStruct((1, ff), f32), jax.ShapeDtypeStruct((8, width), f32)],
        scratch_shapes=[pltpu.VMEM((seg, width), f32)] * 2 + [pltpu.VMEM((seg, width), bf16), pltpu.VMEM((seg, 1), f32)] + [pltpu.VMEM((seg, width), f32)] * 2,
        compiler_params=pltpu.CompilerParams(vmem_limit_bytes=56 << 20),
        cost_estimate=pl.CostEstimate(flops=2 * seg * width * (6 * ff + 3 * width), bytes_accessed=8 * width * ff + 16 * seg * width, transcendentals=seg * ff),
    )(att, tok, cot, wo, up, dn, bu, bd, gain, shift)


def wide_back_kernel(d_ref, w_ref, o_ref, acc_ref):
    j = pl.program_id(0)
    g = nt(d_ref[...], w_ref[...])

    @pl.when(j == 0)
    def _():
        acc_ref[...] = g

    @pl.when(j > 0)
    def _():
        acc_ref[...] += g

    @pl.when(j == pl.num_programs(0) - 1)
    def _():
        o_ref[...] = acc_ref[...].astype(bf16)


def wide_before_grad(d_prev, w):
    _, seg, width = d_prev.shape
    blk = 512
    per = width // blk
    return pl.pallas_call(
        wide_back_kernel,
        grid=(2 * per,),
        in_specs=[pl.BlockSpec((None, seg, blk), lambda j: (j // per, 0, j % per)), pl.BlockSpec((width, blk), lambda j: (0, per + j))],
        out_specs=pl.BlockSpec((seg, width), lambda j: (0, 0)),
        out_shape=jax.ShapeDtypeStruct((seg, width), bf16),
        scratch_shapes=[pltpu.VMEM((seg, width), f32)],
        compiler_params=pltpu.CompilerParams(vmem_limit_bytes=32 << 20),
        cost_estimate=pl.CostEstimate(flops=4 * seg * width * width, bytes_accessed=4 * width * width, transcendentals=0),
    )(d_prev, w)


def tail_kernel(dc_ref, dp_ref, nc_ref, np_ref, w_ref, g_ref, h_ref):
    j = pl.program_id(0)
    per = pl.num_programs(0) // 3
    dc = dc_ref[...]
    h = nt(dc, w_ref[...])

    @pl.when(j == 0)
    def _():
        h_ref[...] = h

    @pl.when(j > 0)
    def _():
        h_ref[...] += h

    @pl.when(j < per)
    def _():
        g_ref[...] = tn(nc_ref[...], dc).astype(bf16)

    @pl.when(j >= per)
    def _():
        g_ref[...] = (tn(nc_ref[...], dc) + tn(np_ref[...], dp_ref[...])).astype(bf16)


def qkv_back(d_cur, d_prev, n_cur, n_prev, w):
    _, seg, width = d_cur.shape
    blk = 256
    per = width // blk
    quarter = 3 * width // 4
    pq = quarter // blk
    whole = pl.BlockSpec((seg, width), lambda j: (0, 0))
    return pl.pallas_call(
        tail_kernel,
        grid=(3 * per,),
        in_specs=[pl.BlockSpec((None, seg, blk), lambda j: (j // per, 0, j % per)),
                  pl.BlockSpec((None, seg, blk), lambda j: (jnp.maximum(j // per - 1, 0), 0, jnp.where(j < per, 0, j % per))),
                  whole, whole, pl.BlockSpec((width, blk), lambda j: (0, j))],
        out_specs=[pl.BlockSpec((None, width, blk), lambda j: (j // pq, 0, j % pq)), whole],
        out_shape=[jax.ShapeDtypeStruct((4, width, quarter), bf16), jax.ShapeDtypeStruct((seg, width), f32)],
        compiler_params=pltpu.CompilerParams(vmem_limit_bytes=40 << 20),
        cost_estimate=pl.CostEstimate(flops=2 * seg * width * width * 8, bytes_accessed=12 * width * width + 16 * seg * width, transcendentals=0),
    )(d_cur, d_prev, n_cur, n_prev, w)


def last_kernel(h_ref, back_ref, tok_ref, one_ref, gain_ref, out_ref, vec_ref):
    h = h_ref[...] + back_ref[...].astype(f32)
    n, r = norm_stats(tok_ref[...].astype(f32))
    vec_ref[0:1, :] = jnp.sum(h * n, axis=0, keepdims=True)
    vec_ref[1:2, :] = jnp.sum(h, axis=0, keepdims=True)
    out_ref[...] = one_ref[...] + norm_back(h, n, r, gain_ref[...].astype(f32))


def finish(h, back, tok, one, gain):
    seg, width = tok.shape
    return pl.pallas_call(
        last_kernel,
        out_shape=[jax.ShapeDtypeStruct((seg, width), f32), jax.ShapeDtypeStruct((8, width), f32)],
        compiler_params=pltpu.CompilerParams(vmem_limit_bytes=40 << 20),
        cost_estimate=pl.CostEstimate(flops=20 * seg * width, bytes_accessed=16 * seg * width, transcendentals=0),
    )(h, back, tok, one, gain)


def local_wide(
    tokens, resets, retrieved, memory_keys, memory_values, qkv_weight, out_weight, up_weight, up_bias,
    down_weight, down_bias, attn_gain, attn_shift, ffn_gain, ffn_shift, position_bias, memory_gate, cotangent,
):
    heads = memory_gate.shape[0]
    seg, width = tokens.shape[1:]
    dh = width // heads
    mem_rows = memory_keys.shape[1]
    shards = lax.axis_size("fsdp")
    mem = mem_rows * shards
    part = width // shards
    bias_part = up_bias.shape[0]
    pos_part = position_bias.shape[0]
    small, mk, mv = gather_small(memory_keys, memory_values, [up_bias, down_bias, attn_gain, attn_shift, ffn_gain, ffn_shift, position_bias], heads)
    b_up = small[:, :bias_part].reshape(-1)
    vecs = [small[:, bias_part + k * part : bias_part + (k + 1) * part].reshape(1, -1) for k in range(5)]
    b_down, gain_one, shift_one, gain_two, shift_two = vecs
    table = small[:, bias_part + 5 * part : bias_part + 5 * part + pos_part].reshape(heads, -1).astype(f32)
    w_qkv, w_out, w_up, w_down = [lax.all_gather(w, "fsdp", axis=0, tiled=True) for w in (qkv_weight, out_weight, up_weight, down_weight)]
    before = passed_along(tokens[0], "fsdp", 1)
    mask = picked_masks(retrieved[0].transpose(1, 0, 2), mem)
    hot, rel = bucket_hot(seg)
    base = diagonal_bias(table, hot, rel)
    gate = jax.nn.sigmoid(memory_gate.astype(f32))
    reset = resets[0]
    q, kp, kc, vp, vc, rq, rkp, rkc, n_prev, n_cur = project_qkv(before, tokens[0], gain_one, shift_one, w_qkv, heads)
    attn_in, loc, rem = attn_fwd(gate, reset, q, kp, kc, vp, vc, base, mk, mv, mask)
    output, grad_one, gm, up_g, down_g, out_g, up_bias_g, vec_two = middle(
        attn_in, tokens[0], cotangent[0], w_out, w_up, w_down, b_up.reshape(1, -1), b_down, gain_two, shift_two)
    up_t, down_t, out_t = scatter_weights((up_g, down_g, out_g))
    d_cur, d_prev, diag, dgate = attn_bwd(gate, reset, q, kp, kc, vp, vc, rq, rkp, rkc, base, mk, mv, mask, loc, rem, gm)
    gate_g = dgate[:, 0, 0]
    table_g = jnp.dot(diag[:, 0], hot.T, precision=lax.Precision.HIGHEST)
    back = passed_along(wide_before_grad(d_prev, w_qkv), "fsdp", -1)
    qkv_g, grad_h1 = qkv_back(d_cur, d_prev, n_cur, n_prev, w_qkv)
    (qkv_t,) = scatter_weights((qkv_g,))
    token_grad, vec_one = finish(grad_h1, back, tokens[0], grad_one, gain_one)
    gain_two_g, shift_two_g, down_bias_g = vec_two[0], vec_two[1], vec_two[2]
    gain_one_g, shift_one_g = vec_one[0], vec_one[1]
    small_g = jnp.concatenate(
        [up_bias_g.reshape(shards, -1)]
        + [v.reshape(shards, -1) for v in (down_bias_g, gain_one_g, shift_one_g, gain_two_g, shift_two_g, table_g)]
        + [jnp.broadcast_to(gate_g[None], (shards, heads))],
        axis=1,
    )
    small_g = summed_everywhere(small_g)
    small_g = lax.dynamic_index_in_dim(small_g, lax.axis_index("fsdp"), 0, keepdims=False)
    cuts = [bias_part] + [part] * 5 + [pos_part, heads]
    at = 0
    outs = []
    for c in cuts:
        outs.append(small_g[at : at + c])
        at += c
    ub, db, g1, s1, g2, s2, pg, gg = outs
    return output[None], token_grad[None], qkv_t, out_t, up_t, ub, down_t, db, g1, s1, g2, s2, pg, gg


def take(v, i, axis):
    return lax.dynamic_index_in_dim(v, i, axis, keepdims=False)


def fence(*trees):
    return lax.optimization_barrier(trees)


def major_first(v):
    return with_layout_constraint(v, Layout(tuple(range(v.ndim))))


def add_low(u, v):
    return (u.astype(f32) + v.astype(f32)).astype(bf16)


def hits_kernel(at_ref, p_ref, o_ref):
    slots, n = p_ref.shape
    mem = o_ref.shape[0]
    lane = 128
    ids = lax.broadcasted_iota(jnp.int32, (mem, lane), 0)
    rows = mem // 8
    chip = (((ids // rows) & 3) ^ at_ref[0]) * 2 + ((ids // (4 * rows)) ^ at_ref[1])
    ids = chip * rows + ids % rows
    for t in range(n // lane):
        cols = slice(t * lane, (t + 1) * lane)
        acc = jnp.zeros((mem, lane), f32)
        for s in range(slots):
            acc = jnp.where(ids == p_ref[s : s + 1, cols], 1.0, acc)
        o_ref[:, cols] = acc.astype(bf16)


def hit_masks(at, picked, mem):
    h, slots, n = picked.shape
    return pl.pallas_call(
        hits_kernel,
        grid_spec=pltpu.PrefetchScalarGridSpec(
            num_scalar_prefetch=1, grid=(h,),
            in_specs=[pl.BlockSpec((None, slots, n), lambda i, at: (i, 0, 0))],
            out_specs=pl.BlockSpec((None, mem, n), lambda i, at: (i, 0, 0))),
        out_shape=jax.ShapeDtypeStruct((h, mem, n), bf16),
        cost_estimate=pl.CostEstimate(flops=2 * h * n * slots * mem, bytes_accessed=h * n * mem * 2, transcendentals=0),
    )(at, picked)


def prep_kernel(at_ref, reset_ref, wq_ref, up_ref, dn_ref, wo_ref, mk_ref, mv_ref, *refs):
    vectors, (qo_ref, qs_ref, ro_ref, rs_ref, d1_ref) = refs[:-5], refs[-5:]
    r = wq_ref.shape[0]
    m = mk_ref.shape[0]
    c, x = at_ref[2], at_ref[3]
    width = wq_ref.shape[1] // 3
    lane = 128
    at = lambda col: pl.ds(pl.multiple_of(col, lane), lane)
    lanes = lambda k: slice(k * lane, (k + 1) * lane)
    for qd, rd, cc in ((qo_ref, ro_ref, c), (qs_ref, rs_ref, 1 - c)):
        for ab in range(2):
            for part in range(3):
                qd[ab * r : (ab + 1) * r, lanes(part)] = wq_ref[:, at(part * width + (4 * cc + 2 * x + ab) * lane)]
            for half in range(2):
                for yy in range(2):
                    col = ((2 * (2 * x + ab) + yy) * 2 + cc) * 2 * lane + half * lane
                    row = (half * 2 + ab) * r
                    rd[row : row + r, lanes(yy)] = up_ref[:, at(col)]
            rd[4 * r : 5 * r, lanes(ab)] = wo_ref[:, at((4 * cc + 2 * x + ab) * lane)]
        for kv, src in enumerate((mk_ref, mv_ref)):
            for h in range(4):
                row = 5 * r + (kv * 2 + h // 2) * m
                rd[row : row + m, lanes(h % 2)] = src[:, at((4 * cc + h) * lane)]
        qd[2 * r :, :] = jnp.zeros((8, 3 * lane), bf16)
        for k, v in enumerate(vectors):
            qd[2 * r + k : 2 * r + k + 1, : v.shape[1]] = v[...]
        qd[2 * r + 7 : 2 * r + 8, :lane] = jnp.broadcast_to(reset_ref[0, 0].astype(f32), (1, lane)).astype(bf16)
    for ab in range(2):
        for half in range(2):
            for yy in range(2):
                d1_ref[half, ab, :, lanes(yy)] = dn_ref[half * lane : (half + 1) * lane, at((2 * x + ab) * 2 * lane + yy * lane)]


def prepare(at, resets, wq, up, dn, wo, mk, mv, vectors):
    r, m = wq.shape[0], mk.shape[0]
    s = lambda *d: jax.ShapeDtypeStruct(d, bf16)
    return pl.pallas_call(
        prep_kernel,
        in_specs=[pl.BlockSpec(memory_space=pltpu.SMEM)] * 2 + [pl.BlockSpec(memory_space=pltpu.VMEM)] * (6 + len(vectors)),
        out_shape=[s(2 * r + 8, 384), s(2 * r + 8, 384), s(5 * r + 4 * m, 256), s(5 * r + 4 * m, 256), s(2, 2, 128, 256)],
    )(at, resets, wq, up, dn, wo, mk, mv, *[v.reshape(1, -1) for v in vectors])


def pack_kernel(at_ref, own_ref, got_ref, d_ref, f1_ref, f2_ref, *, m):
    c = at_ref[2]
    lane = 128

    def fill(r0, r1):
        for ab in range(2):
            a = 448 * ab
            f1_ref[a : a + 64, :] = r0[64 * ab : 64 * ab + 64, :]
            f1_ref[a + 64 : a + 128, :] = r1[64 * ab : 64 * ab + 64, :]
            f1_ref[a + 128 : a + 256, :] = d_ref[0, ab]
            f1_ref[a + 256 : a + 320, :lane] = r0[256:320, lane * ab : lane * ab + lane]
            f1_ref[a + 256 : a + 320, lane:] = r1[256:320, lane * ab : lane * ab + lane]
            b = 256 * ab
            f2_ref[b : b + 64, :] = r0[128 + 64 * ab : 192 + 64 * ab, :]
            f2_ref[b + 64 : b + 128, :] = r1[128 + 64 * ab : 192 + 64 * ab, :]
            f2_ref[b + 128 : b + 256, :] = d_ref[1, ab]
        for k in range(4):
            at = 320 + 2 * k * m
            f1_ref[at : at + m, :] = r0[320 + k * m : 320 + (k + 1) * m, :]
            f1_ref[at + m : at + 2 * m, :] = r1[320 + k * m : 320 + (k + 1) * m, :]

    @pl.when(c == 0)
    def _():
        fill(own_ref, got_ref)

    @pl.when(c == 1)
    def _():
        fill(got_ref, own_ref)


def pack_ffn(at, own, got, d, m):
    s = lambda *e: jax.ShapeDtypeStruct(e, bf16)
    return pl.pallas_call(
        functools.partial(pack_kernel, m=m),
        in_specs=[pl.BlockSpec(memory_space=pltpu.SMEM)] + [pl.BlockSpec(memory_space=pltpu.VMEM)] * 3,
        out_shape=[s(768, 256), s(512, 256)],
    )(at, own, got, d)


def piece_places(at_ref):
    z, y, x = at_ref[0], at_ref[1], at_ref[3]
    for kind in range(4):
        for i in range(2):
            for k in range(4):
                yy = (y ^ i) if kind < 2 else (y if kind == 2 else 1 - y)
                xx = (x if kind == 0 else 1 - x) if kind < 2 else (x ^ i)
                yield kind * 2 + i, k, (z ^ k) * 2 + yy, 2 * xx + kind // 2


def qkv_kernel(at_ref, tp_ref, own_ref, oth_ref, gain_ref, shift_ref, p0, p1, p2, p3, p4, p5, p6, p7,
               q_ref, k_ref, v_ref, rq_ref, rk_ref, xn_hbm, w_hbm, x_ref, w_ref, sem, osem):
    i = pl.program_id(0)
    seg = tp_ref.shape[0]
    dh = 128
    half = w_ref.shape[1] // 3
    outs = [pltpu.make_async_copy(x_ref, xn_hbm, osem.at[0]), pltpu.make_async_copy(w_ref, w_hbm, osem.at[1])]

    @pl.when(i == 0)
    def _():
        copies = []
        pieces = (p0, p1, p2, p3, p4, p5, p6, p7)
        for kind, slot, chip, quarter in piece_places(at_ref):
            for part in range(3):
                dst = w_ref.at[pl.ds(pl.multiple_of(chip * 128, 128), 128), pl.ds(pl.multiple_of(part * half + quarter * dh, dh), dh)]
                copies.append(pltpu.make_async_copy(pieces[kind].at[slot, pl.ds(0, 128), pl.ds(part * dh, dh)], dst, sem))
        for copy in copies:
            copy.start()
        gain = gain_ref[...].astype(f32)
        shift = shift_ref[...].astype(f32)
        for s, src in enumerate((tp_ref, own_ref, oth_ref)):
            first = 0 if s == 0 else seg * (1 + at_ref[2]) if s == 1 else seg * (2 - at_ref[2])
            for r0 in range(0, seg, 128):
                n, r = norm_stats(src[r0 : r0 + 128, :].astype(f32))
                x_ref[pl.ds(pl.multiple_of(first + r0, 128), 128), :] = (n * gain + shift).astype(bf16)
        for copy in copies:
            copy.wait()
        for copy in outs:
            copy.start()

    def unit(y, out_ref, r_ref):
        for k in range(2):
            part = y[:, k * dh : (k + 1) * dh]
            r = lax.rsqrt(jnp.sum(part * part, axis=1, keepdims=True) + 1e-06)
            out_ref[:, k * dh : (k + 1) * dh] = (part * r).astype(bf16)
            r_ref[k] = r

    w = w_ref[:, pl.ds(pl.multiple_of(i * 256, 256), 256)]

    @pl.when(i < 2)
    def _():
        unit(nn(x_ref[seg:, :], w), q_ref, rq_ref)

    @pl.when((i >= 2) & (i < 4))
    def _():
        unit(nn(x_ref[...], w), k_ref, rk_ref)

    @pl.when(i >= 4)
    def _():
        v_ref[...] = nn(x_ref[...], w).astype(bf16)

    @pl.when(i == 5)
    def _():
        for copy in outs:
            copy.wait()


def project_pair(at, tp, own, oth, gain, shift, pieces):
    seg, width = tp.shape
    half = width // 2
    once = dict(pipeline_mode=pl.Buffered(1))
    whole = pl.BlockSpec((seg, width), lambda i, *_: (0, 0), **once)
    vec = pl.BlockSpec((1, width), lambda i, *_: (0, 0))
    hbm = pl.BlockSpec(memory_space=pltpu.HBM)
    col = lambda n, s: pl.BlockSpec((n * seg, 256), lambda i, *_: (0, jnp.clip(i - s, 0, 1)))
    rs = lambda n, s: pl.BlockSpec((2, n * seg, 1), lambda i, *_: (jnp.clip(i - s, 0, 1), 0, 0))
    sd = jax.ShapeDtypeStruct
    return pl.pallas_call(
        qkv_kernel,
        grid_spec=pltpu.PrefetchScalarGridSpec(
            num_scalar_prefetch=1, grid=(6,),
            in_specs=[whole, whole, whole, vec, vec] + [hbm] * 8,
            out_specs=[col(2, 0), col(3, 2), col(3, 4), rs(2, 0), rs(3, 2), hbm, hbm],
            scratch_shapes=[pltpu.VMEM((3 * seg, width), bf16), pltpu.VMEM((width, 3 * half), bf16), pltpu.SemaphoreType.DMA, pltpu.SemaphoreType.DMA((2,))]),
        out_shape=[sd((2 * seg, half), bf16), sd((3 * seg, half), bf16), sd((3 * seg, half), bf16), sd((4, 2 * seg, 1), f32), sd((4, 3 * seg, 1), f32),
                   sd((3 * seg, width), bf16), sd((width, 3 * half), bf16)],
        compiler_params=pltpu.CompilerParams(vmem_limit_bytes=48 << 20),
        cost_estimate=pl.CostEstimate(flops=2 * seg * width * half * 8, bytes_accessed=20 << 20, transcendentals=0),
    )(at, tp, own, oth, gain, shift, *pieces)


def attn_fwd_kernel(gate_ref, reset_ref, at_ref, q_ref, k_ref, v_ref, base_ref, mk0_ref, mk1_ref, mv0_ref, mv1_ref, mask0_ref, mask1_ref, mix_ref, loc_ref, rem_ref, t_ref):
    seg = q_ref.shape[0] // 2
    s = gate_ref[pl.program_id(0)]
    t_ref[...] = spread(base_ref[...], BLK)
    heat = 16.0 * LOG2E
    nb = seg // BLK
    mk = jnp.concatenate([mk0_ref[...].reshape(-1, 128), mk1_ref[...].reshape(-1, 128)]).astype(f32)
    mk = (mk * lax.rsqrt(jnp.sum(mk * mk, axis=1, keepdims=True) + 1e-06)).astype(bf16)
    mv = jnp.concatenate([mv0_ref[...].reshape(-1, 128), mv1_ref[...].reshape(-1, 128)])
    for u in range(2):
        keep = jnp.where(reset_ref[u] == 0, 1.0, 0.0).astype(f32)
        kp = k_ref[u * seg : (u + 1) * seg, :]
        vp = v_ref[u * seg : (u + 1) * seg, :] * keep.astype(bf16)
        for i in range(nb):
            rows = slice(u * seg + i * BLK, u * seg + (i + 1) * BLK)
            q = q_ref[rows, :]
            off = (nb - 1 - i) * BLK
            cw = (i + 1) * BLK
            kc = k_ref[(u + 1) * seg : (u + 1) * seg + cw, :]
            vc = v_ref[(u + 1) * seg : (u + 1) * seg + cw, :]
            ep = jnp.exp2(nt(q, kp) * heat + t_ref[:, off : off + seg])
            ec = jnp.exp2(nt(q, kc) * heat + t_ref[:, off + seg : off + seg + cw])
            il = 1.0 / (keep * jnp.sum(ep, axis=1, keepdims=True) + jnp.sum(ec, axis=1, keepdims=True))
            o = nn((ep * il).astype(bf16), vp) + nn((ec * il).astype(bf16), vc)
            em = jnp.exp2(nt(mk, q) * heat) * (mask0_ref, mask1_ref)[u][:, i * BLK : (i + 1) * BLK].astype(f32)
            em = em * (1.0 / jnp.sum(em, axis=0, keepdims=True))
            om = tn(em.astype(bf16), mv)
            loc_ref[rows, :] = o.astype(bf16)
            rem_ref[rows, :] = om.astype(bf16)
            mix_ref[rows, :] = (s * om + (1.0 - s) * o).astype(bf16)


def head_specs(seg, mem, wt, head=lambda h: h):
    dh = 128
    col = lambda n: pl.BlockSpec((n, dh), lambda h, *_: (0, head(h)))
    own = lambda k: pl.BlockSpec((4, mem // 8, dh), lambda h, *_: (0, 10 + 2 * k + head(h) // 2, head(h) % 2))
    return [col(2 * seg), col(3 * seg), col(3 * seg), pl.BlockSpec((None, 1, wt), lambda h, *_: (head(h), 0, 0)), own(0), own(0), own(1), own(1)] + [pl.BlockSpec((None, mem, seg), lambda h, *_: (head(h), 0, 0))] * 2


def attend(gate, reset, at, q, k, v, base, pack, masks):
    seg = q.shape[0] // 2
    mem, wt = masks[0].shape[1], base.shape[2]
    col = pl.BlockSpec((2 * seg, 128), lambda h, *_: (0, h))
    full = jax.ShapeDtypeStruct(q.shape, bf16)
    return pl.pallas_call(
        attn_fwd_kernel,
        grid_spec=pltpu.PrefetchScalarGridSpec(
            num_scalar_prefetch=3, grid=(4,), in_specs=head_specs(seg, mem, wt), out_specs=[col] * 3, scratch_shapes=[pltpu.VMEM((BLK, wt), f32)]),
        out_shape=[full] * 3,
        compiler_params=pltpu.CompilerParams(vmem_limit_bytes=48 << 20),
        cost_estimate=pl.CostEstimate(flops=8 * seg * (2 * seg + mem) * 4 * 128, bytes_accessed=20 << 20, transcendentals=8 * seg * (2 * seg + mem)),
    )(gate, reset, at, q, k, v, base, *pack, *pack, *masks)


def attn_bwd_kernel(gate_ref, reset_ref, at_ref, q_ref, k_ref, v_ref, base_ref, mk0_ref, mk1_ref, mv0_ref, mv1_ref, mask0_ref, mask1_ref, loc_ref, rem_ref, ol_ref, ox_ref, wo_ref, rq_ref, rk_ref,
                    dq_ref, dk_ref, dv_ref, diag_ref, dgate_ref, t_ref, g_ref, ak, av, gm_ref, *, part):
    seg = q_ref.shape[0] // 2
    s = gate_ref[2 * pl.program_id(0) + part]
    t_ref[...] = spread(base_ref[...], BLK)
    g_ref[...] = jnp.zeros_like(g_ref)
    ak[...] = jnp.zeros_like(ak)
    av[...] = jnp.zeros_like(av)
    wo = wo_ref[...]
    gm_ref[pl.ds(pl.multiple_of(at_ref[2] * seg, seg), seg), :] = nt(ol_ref[...], wo)
    gm_ref[pl.ds(pl.multiple_of((1 - at_ref[2]) * seg, seg), seg), :] = nt(ox_ref[...], wo)
    heat = 16.0 * LOG2E
    nb = seg // BLK
    mk = jnp.concatenate([mk0_ref[...].reshape(-1, 128), mk1_ref[...].reshape(-1, 128)]).astype(f32)
    mk = (mk * lax.rsqrt(jnp.sum(mk * mk, axis=1, keepdims=True) + 1e-06)).astype(bf16)
    mv = jnp.concatenate([mv0_ref[...].reshape(-1, 128), mv1_ref[...].reshape(-1, 128)])
    dg = jnp.zeros((BLK, 1), f32)
    for u in range(2):
        keep = jnp.where(reset_ref[u] == 0, 1.0, 0.0).astype(f32)
        old = slice(u * seg, (u + 1) * seg)
        kp = k_ref[old, :]
        vp = v_ref[old, :]
        for i in range(nb):
            rows = slice(u * seg + i * BLK, u * seg + (i + 1) * BLK)
            q = q_ref[rows, :]
            gm = gm_ref[rows, :]
            off = (nb - 1 - i) * BLK
            cw = (i + 1) * BLK
            cur = slice((u + 1) * seg, (u + 1) * seg + cw)
            kc = k_ref[cur, :]
            vc = v_ref[cur, :]
            al = jnp.sum(gm * loc_ref[rows, :].astype(f32), axis=1, keepdims=True)
            ar = jnp.sum(gm * rem_ref[rows, :].astype(f32), axis=1, keepdims=True)
            dg = dg + (ar - al)
            gl = ((1.0 - s) * gm).astype(bf16)
            gr = (s * gm).astype(bf16)
            ep = jnp.exp2(nt(q, kp) * heat + t_ref[:, off : off + seg])
            ec = jnp.exp2(nt(q, kc) * heat + t_ref[:, off + seg : off + seg + cw])
            l = keep * jnp.sum(ep, axis=1, keepdims=True) + jnp.sum(ec, axis=1, keepdims=True)
            il = 1.0 / l
            pp = ep * (il * keep)
            pc = ec * il
            wp = pp * nt(gl, vp)
            wc = pc * nt(gl, vc)
            dl = jnp.sum(wp, axis=1, keepdims=True) + jnp.sum(wc, axis=1, keepdims=True)
            dsp = (wp - pp * dl).astype(bf16)
            dsc = (wc - pc * dl).astype(bf16)
            g_ref[:, off : off + seg] += dsp.astype(f32)
            g_ref[:, off + seg : off + seg + cw] += dsc.astype(f32)
            dq = nn(dsp, kp) + nn(dsc, kc)
            ak[old, :] += tn(dsp, q)
            ak[cur, :] += tn(dsc, q)
            av[old, :] += tn(pp.astype(bf16), gl)
            av[cur, :] += tn(pc.astype(bf16), gl)
            em = jnp.exp2(nt(mk, q) * heat) * (mask0_ref, mask1_ref)[u][:, i * BLK : (i + 1) * BLK].astype(f32)
            em = em * (1.0 / jnp.sum(em, axis=0, keepdims=True))
            gw = nt(mv, gr)
            dsm = em * (gw - jnp.sum(em * gw, axis=0, keepdims=True))
            dq = dq + tn(dsm.astype(bf16), mk)
            dq_ref[rows, :] = unit_back(16.0 * dq, q, rq_ref[rows, :])
    dk_ref[...] = unit_back(16.0 * ak[...], k_ref[...], rk_ref[...])
    dv_ref[...] = av[...].astype(bf16)
    diag_ref[...] = gather_diagonals(g_ref[...])
    dgate_ref[...] = jnp.broadcast_to(jnp.sum(dg) * s * (1.0 - s), dgate_ref.shape)


def attend_back(part, gate, reset, at, q, k, v, base, pack, masks, loc, rem, ol, ox, wo, rq, rk):
    seg, half = q.shape[0] // 2, q.shape[1]
    mem, wt = masks[0].shape[1], base.shape[2]
    width = ol.shape[1]
    col = lambda n: pl.BlockSpec((n * seg, 128), lambda h, *_: (0, h))
    head = lambda h: 2 * h + part
    col_in = lambda n: pl.BlockSpec((n * seg, 128), lambda h, *_: (0, head(h)))
    row = lambda w: pl.BlockSpec((None, 1, w), lambda h, *_: (h, 0, 0))
    rcol = lambda n: pl.BlockSpec((None, n * seg, 1), lambda h, *_: (head(h), 0, 0))
    sd = jax.ShapeDtypeStruct
    return pl.pallas_call(
        functools.partial(attn_bwd_kernel, part=part),
        grid_spec=pltpu.PrefetchScalarGridSpec(
            num_scalar_prefetch=3, grid=(2,),
            in_specs=head_specs(seg, mem, wt, head) + [col_in(2), col_in(2), pl.BlockSpec((seg, width), lambda h, *_: (0, 0), pipeline_mode=pl.Buffered(1)), pl.BlockSpec((seg, width), lambda h, *_: (0, 0), pipeline_mode=pl.Buffered(1)),
                      pl.BlockSpec((128, width), lambda h, g, r, at: (4 * at[2] + head(h), 0)), rcol(2), rcol(3)],
            out_specs=[col(2), col(3), col(3), row(wt), row(128)],
            scratch_shapes=[pltpu.VMEM((BLK, wt), f32)] * 2 + [pltpu.VMEM((3 * seg, 128), f32)] * 2 + [pltpu.VMEM((2 * seg, 128), f32)]),
        out_shape=[sd((2 * seg, half // 2), bf16), sd((3 * seg, half // 2), bf16), sd((3 * seg, half // 2), bf16), sd((2, 1, wt), f32), sd((2, 1, 128), f32)],
        compiler_params=pltpu.CompilerParams(vmem_limit_bytes=48 << 20),
        cost_estimate=pl.CostEstimate(flops=8 * seg * (2 * seg + mem) * 10 * 128, bytes_accessed=30 << 20, transcendentals=8 * seg * (2 * seg + mem)),
    )(gate, reset, at, q, k, v, base, *pack, *pack, *masks, loc, rem, ol, ox, wo, rq, rk)


def ffn_kernel(at_ref, *refs, first):
    refs = list(refs)
    if first:
        ao_ref, ax_ref, tok_ref, tokx_ref, gain_ref, shift_ref, other_ref = refs[:7]
        refs = refs[7:]
    else:
        lo_ref, oi_ref, gi_ref = refs[:3]
        refs = refs[3:]
    cot_ref, cotx_ref, bu_ref = refs[:3]
    pieces = refs[3:11]
    refs = refs[11:]
    if first:
        lowo_ref, res_ref, o_ref, g_ref, wout_ref = refs[:5]
        refs = refs[5:]
    else:
        oo_ref, ox_ref, go_ref, gx_ref = refs[:4]
        refs = refs[4:]
    oa_ref, xa_ref, ob_ref, yb_ref, gbu_ref, up_s, dn_s, low_s, cot_s, act_s, gp_s, sem, osem, tmp = refs[:14]
    i = pl.program_id(0)
    rb, width = cot_ref.shape
    rows = pl.ds(pl.multiple_of(i * rb, rb), rb)
    q4 = 256
    copies = []
    for kind, slot, chip, quarter in piece_places(at_ref):
        where = (pl.ds(pl.multiple_of(chip * 128, 128), 128), pl.ds(pl.multiple_of(quarter * q4, q4), q4))
        for w, dst in enumerate((up_s, dn_s)):
            copies.append(pltpu.make_async_copy(pieces[kind].at[slot, pl.ds(w * 128, 128)], dst.at[where], sem))
    outs = []
    if first:
        wout_s = refs[14]
        c = at_ref[2]
        for whose, cc in ((0, c), (1, 1 - c)):
            for kind, slot, chip, quarter in piece_places(at_ref):
                for core in range(2):
                    src = pieces[kind].at[slot, pl.ds(256, 64), pl.ds(core * 128, 128)] if whose == 0 else other_ref.at[kind * 4 + slot, :, pl.ds(core * 128, 128)]
                    dst = wout_s.at[pl.ds(pl.multiple_of(chip * 128 + core * 64, 64), 64), pl.ds(pl.multiple_of((4 * cc + quarter) * 128, 128), 128)]
                    outs.append(pltpu.make_async_copy(src, dst, osem.at[0]))
        keep = pltpu.make_async_copy(wout_s, wout_ref, osem.at[1])

    @pl.when(i == 0)
    def _():
        for copy in outs + copies:
            copy.start()
        for copy in outs:
            copy.wait()
        if first:
            keep.start()

    if first:
        half_w = ao_ref.shape[1]
        wrow = lambda cc: wout_s[pl.ds(pl.multiple_of(cc * half_w, half_w), half_w), :]
        res = jnp.where(i < 2, tok_ref[...].astype(f32), tokx_ref[...].astype(f32)) + nn(ao_ref[...], wrow(c)) + nn(ax_ref[...], wrow(1 - c))
        n, r = norm_stats(res)
        low = (n * gain_ref[...].astype(f32) + shift_ref[...].astype(f32)).astype(bf16)
        lowo_ref[...] = low

        @pl.when(i < 2)
        def _():
            res_ref[...] = res
    else:
        low = lo_ref[...]
    low_s[rows, :] = low
    cot = jnp.where(i < 2, cot_ref[...].astype(f32), cotx_ref[...].astype(f32)).astype(bf16)
    cot_s[rows, :] = cot

    @pl.when(i == 0)
    def _():
        for copy in copies:
            copy.wait()

    p = nn(low, up_s[...]) + bu_ref[...].astype(f32)
    ga = nt(cot, dn_s[...])
    k0 = math.sqrt(2.0 / math.pi)
    p2_ = p * p
    t = jnp.tanh(p * (k0 + (k0 * 0.044715) * p2_))
    half = 0.5 * (1.0 + t)
    act = (p * half).astype(bf16)
    slope = half + 0.5 * p * (1.0 - t * t) * (k0 + (3.0 * k0 * 0.044715) * p2_)
    gp = (ga * slope).astype(bf16)
    act_s[rows, :] = act
    gp_s[rows, :] = gp
    o = nn(act, dn_s[...])
    g = nt(gp, up_s[...])
    if first:
        o_ref[...] = o
        g_ref[...] = g
    else:
        o = o + oi_ref[...]
        g = g + gi_ref[...]

        @pl.when(i < 2)
        def _():
            oo_ref[...] = o
            go_ref[...] = g

        @pl.when(i >= 2)
        def _():
            ox_ref[...] = o.astype(bf16)
            gx_ref[...] = g.astype(bf16)

    @pl.when(i == pl.num_programs(0) - 1)
    def _():
        z, y, x = at_ref[0], at_ref[1], at_ref[3]
        for part in range(2):
            for xr in range(2):
                cols = pl.ds(pl.multiple_of((2 * (x ^ xr) + part) * q4, q4), q4)
                for w, (left, right) in enumerate(((low_s, gp_s), (act_s, cot_s))):
                    tmp[w] = tn(left[...], right[:, cols]).astype(bf16)
                    for yr in range(2):
                        dst = ((oa_ref, xa_ref)[xr], yr) if part == 0 else ((ob_ref, yb_ref)[yr], xr)
                        for k in range(4):
                            chip = (z ^ k) * 2 + (y ^ yr)
                            dst[0][dst[1], w, k] = tmp[w, pl.ds(pl.multiple_of(chip * 128, 128), 128), :]
        if first:
            keep.wait()
        gbu_ref[...] = jnp.broadcast_to(jnp.sum(gp_s[...].astype(f32), axis=0, keepdims=True), gbu_ref.shape)


def ffn_half(at, first, ins, cot, cotx, bu, pieces):
    seg, width = cot.shape
    pair = 2 * seg
    rb = 256
    once = dict(pipeline_mode=pl.Buffered(1))
    there = lambda w: pl.BlockSpec((rb, w), lambda i, at: ((i + 2 * at[2]) % 4, 0))
    here = lambda w: pl.BlockSpec((rb, w), lambda i, at: (i, 0))
    own = pl.BlockSpec((rb, width), lambda i, at: (jnp.minimum(i, 1), 0))
    other = pl.BlockSpec((rb, width), lambda i, at: (jnp.maximum(i - 2, 0), 0))
    vec = pl.BlockSpec((1, width), lambda i, at: (0, 0))
    hbm = pl.BlockSpec(memory_space=pltpu.HBM)
    sd = jax.ShapeDtypeStruct
    half = width // 2
    if first:
        in_specs = [there(half), there(half), own, other, vec, vec, hbm]
        out_specs = [here(width), own, here(width), here(width), hbm]
        out_shape = [sd((pair, width), bf16), sd((seg, width), f32), sd((pair, width), f32), sd((pair, width), f32), sd((width, width), bf16)]
    else:
        in_specs = [here(width)] * 3
        out_specs = [own, other, own, other]
        out_shape = [sd((seg, width), f32), sd((seg, width), bf16), sd((seg, width), f32), sd((seg, width), bf16)]
    ff = bu.shape[1]
    grads = pl.BlockSpec((2, 2, 4, 128, 256), lambda i, at: (0, 0, 0, 0, 0), **once)
    return pl.pallas_call(
        functools.partial(ffn_kernel, first=first),
        grid_spec=pltpu.PrefetchScalarGridSpec(
            num_scalar_prefetch=1, grid=(4,),
            in_specs=in_specs + [own, other, vec] + [hbm] * 8,
            out_specs=out_specs + [grads] * 4 + [pl.BlockSpec((8, ff), lambda i, at: (0, 0))],
            scratch_shapes=[pltpu.VMEM((width, ff), bf16)] * 2 + [pltpu.VMEM((pair, width), bf16)] * 2 + [pltpu.VMEM((pair, ff), bf16)] * 2 + [pltpu.SemaphoreType.DMA, pltpu.SemaphoreType.DMA((2,)), pltpu.VMEM((2, width, 256), bf16)]
            + ([pltpu.VMEM((width, width), bf16)] if first else [])),
        out_shape=out_shape + [sd((2, 2, 4, 128, 256), bf16)] * 4 + [sd((8, ff), f32)],
        compiler_params=pltpu.CompilerParams(vmem_limit_bytes=56 << 20),
        cost_estimate=pl.CostEstimate(flops=2 * pair * width * ff * 6, bytes_accessed=30 << 20, transcendentals=pair * ff),
    )(at, *ins, cot, cotx, bu, *pieces)


def rows_kernel(*refs):
    pieces, out, buf, sem, osem = refs[:8], refs[8], refs[9], refs[10], refs[11]
    n = out.shape[1]
    copies = [pltpu.make_async_copy(v.at[:, pl.ds(256, n)], buf.at[pl.ds(4 * k, 4)], sem) for k, v in enumerate(pieces)]
    for copy in copies:
        copy.start()
    for copy in copies:
        copy.wait()
    done = pltpu.make_async_copy(buf, out, osem)
    done.start()
    done.wait()


def out_rows_of(pieces):
    n, cols = min(v.shape[1] for v in pieces) - 256, pieces[0].shape[2]
    hbm = pl.BlockSpec(memory_space=pltpu.HBM)
    return pl.pallas_call(
        rows_kernel,
        in_specs=[hbm] * 8,
        out_specs=hbm,
        out_shape=jax.ShapeDtypeStruct((32, n, cols), bf16),
        scratch_shapes=[pltpu.VMEM((32, n, cols), bf16), pltpu.SemaphoreType.DMA, pltpu.SemaphoreType.DMA],
        cost_estimate=pl.CostEstimate(flops=0, bytes_accessed=2 << 20, transcendentals=0),
    )(*pieces)


def join_kernel(res_ref, oo_ref, ox_ref, go_ref, gx_ref, cot_ref, gain_ref, bd_ref, out_ref, one_ref, ol_ref, vec_ref):
    res = res_ref[...]
    out_ref[...] = (res + oo_ref[...] + ox_ref[...].astype(f32) + bd_ref[...].astype(f32)).astype(bf16)
    gh = go_ref[...] + gx_ref[...].astype(f32)
    n, r = norm_stats(res)
    cf = cot_ref[...].astype(f32)
    one = cf + norm_back(gh, n, r, gain_ref[...].astype(f32))
    one_ref[...] = one
    ol_ref[...] = one.astype(bf16)

    @pl.when(pl.program_id(0) == 0)
    def _():
        vec_ref[...] = jnp.zeros_like(vec_ref)

    vec_ref[0:1, :] += jnp.sum(gh * n, axis=0, keepdims=True)
    vec_ref[1:2, :] += jnp.sum(gh, axis=0, keepdims=True)
    vec_ref[2:3, :] += jnp.sum(cf, axis=0, keepdims=True)


def join(res, oo, ox, go, gx, cot, gain, bd):
    seg, width = res.shape
    blk = pl.BlockSpec((128, width), lambda i: (i, 0))
    vec = pl.BlockSpec((1, width), lambda i: (0, 0))
    sd = jax.ShapeDtypeStruct
    return pl.pallas_call(
        join_kernel,
        grid=(seg // 128,),
        in_specs=[blk] * 6 + [vec, vec],
        out_specs=[blk, blk, blk, pl.BlockSpec((8, width), lambda i: (0, 0))],
        out_shape=[sd((seg, width), bf16), sd((seg, width), f32), sd((seg, width), bf16), sd((8, width), f32)],
        cost_estimate=pl.CostEstimate(flops=40 * seg * width, bytes_accessed=24 * seg * width, transcendentals=0),
    )(res, oo, ox, go, gx, cot, gain, bd)


def rows_by_head(refs):
    a, b = refs[0][...], refs[1][...]
    return jnp.concatenate([a[:, :128], b[:, :128], a[:, 128:], b[:, 128:]], axis=1)


def before_kernel(ka_ref, kb_ref, va_ref, vb_ref, wk_ref, wv_ref, o_ref):
    o_ref[...] = (nt(rows_by_head((ka_ref, kb_ref)), wk_ref[...]) + nt(rows_by_head((va_ref, vb_ref)), wv_ref[...])).astype(bf16)


def before_grad(dk, dv, w):
    seg, half = dk[0].shape[0] // 3, dk[0].shape[1] * 2
    width = w.shape[0]
    rb = 256
    d = pl.BlockSpec((rb, half // 2), lambda i: (i, 0))
    wb = lambda k: pl.BlockSpec((width, half), lambda i: (0, k))
    return pl.pallas_call(
        before_kernel,
        grid=(seg // rb,),
        in_specs=[d] * 4 + [wb(1), wb(2)],
        out_specs=pl.BlockSpec((rb, width), lambda i: (i, 0)),
        out_shape=jax.ShapeDtypeStruct((seg, width), bf16),
        cost_estimate=pl.CostEstimate(flops=4 * seg * half * width, bytes_accessed=4 << 20, transcendentals=0),
        compiler_params=pltpu.CompilerParams(vmem_limit_bytes=32 << 20),
    )(*dk, *dv, w, w)


def wgrad_kernel(at_ref, x_ref, dq_ref, dk_ref, dv_ref, att_ref, attx_ref, ol_ref, olx_ref, oa_ref, xa_ref, ob_ref, yb_ref, tmp, ol_s, *, pair):
    seg = dk_ref.shape[0] // 3
    z, y, c, x = at_ref[0], at_ref[1], at_ref[2], at_ref[3]
    for xr in range(2):
        cols = pl.ds(pl.multiple_of((x ^ xr) * 128, 128), 128)
        tmp[:, :128] = tn(x_ref[seg:, :], dq_ref[:, cols]).astype(bf16)
        tmp[:, 128:384] = tn(x_ref[...], jnp.concatenate([dk_ref[:, cols], dv_ref[:, cols]], axis=1)).astype(bf16)
        ocols = pl.ds(pl.multiple_of((4 * c + 2 * (x ^ xr) + pair) * 128, 128), 128)
        ol_s[pl.ds(pl.multiple_of(c * seg, seg), seg), :] = ol_ref[:, ocols]
        ol_s[pl.ds(pl.multiple_of((1 - c) * seg, seg), seg), :] = olx_ref[:, ocols]
        half = att_ref.shape[1]
        tmp[pl.ds(pl.multiple_of(c * half, half), half), 384:] = tn(att_ref[...], ol_s[...]).astype(bf16)
        tmp[pl.ds(pl.multiple_of((1 - c) * half, half), half), 384:] = tn(attx_ref[...], ol_s[...]).astype(bf16)
        for part in range(2):
            for yr in range(2):
                dst = ((oa_ref, xa_ref)[xr], yr) if part == 0 else ((ob_ref, yb_ref)[yr], xr)
                for k in range(4):
                    row = ((z ^ k) * 2 + (y ^ yr)) * 128 + part * 64
                    dst[0][dst[1], 0, k] = tmp[pl.ds(pl.multiple_of(row, 64), 64), :]


def qkv_wgrad(pair, at, x, dq, dk, dv, att, attx, ol, olx):
    n, width = x.shape
    vm = pl.BlockSpec(memory_space=pltpu.VMEM)
    return pl.pallas_call(
        functools.partial(wgrad_kernel, pair=pair),
        in_specs=[pl.BlockSpec(memory_space=pltpu.SMEM)] + [vm] * 8,
        out_specs=[vm] * 4,
        out_shape=[jax.ShapeDtypeStruct((2, 1, 4, 64, 512), bf16)] * 4,
        scratch_shapes=[pltpu.VMEM((width, 512), bf16), pltpu.VMEM((att.shape[0], 128), bf16)],
        compiler_params=pltpu.CompilerParams(vmem_limit_bytes=32 << 20),
        cost_estimate=pl.CostEstimate(flops=2 * n * width * 768, bytes_accessed=12 << 20, transcendentals=0),
    )(at, x, dq, dk, dv, att, attx, ol, olx)


def hgrad_kernel(at_ref, qa_ref, qb_ref, ka_ref, kb_ref, va_ref, vb_ref, wq_ref, wk_ref, wv_ref, back_ref, ho_ref, hx_ref):
    i = pl.program_id(0)
    c = at_ref[2]
    g = nt(rows_by_head((qa_ref, qb_ref)), wq_ref[...]) + nt(rows_by_head((ka_ref, kb_ref)), wk_ref[...]) + nt(rows_by_head((va_ref, vb_ref)), wv_ref[...])
    mine = jnp.where((i + 2 * c) % 4 == 2 + c, 1.0, 0.0).astype(f32)
    g = g + mine * back_ref[...].astype(f32)

    @pl.when(i < 2)
    def _():
        ho_ref[...] = g

    @pl.when(i >= 2)
    def _():
        hx_ref[...] = g.astype(bf16)


def hgrad(at, dq, dk, dv, w, back):
    pair, half = dq[0].shape[0], dq[0].shape[1] * 2
    seg, width = pair // 2, w.shape[0]
    rb = 256
    once = dict(pipeline_mode=pl.Buffered(1))
    wb = lambda k: pl.BlockSpec((width, half), lambda i, at: (0, k), **once)
    sd = jax.ShapeDtypeStruct
    return pl.pallas_call(
        hgrad_kernel,
        grid_spec=pltpu.PrefetchScalarGridSpec(
            num_scalar_prefetch=1, grid=(4,),
            in_specs=[pl.BlockSpec((rb, half // 2), lambda i, at: ((i + 2 * at[2]) % 4, 0))] * 2 + [pl.BlockSpec((rb, half // 2), lambda i, at: (2 + (i + 2 * at[2]) % 4, 0))] * 4
            + [wb(0), wb(1), wb(2), pl.BlockSpec((rb, width), lambda i, at: (0, 0))],
            out_specs=[pl.BlockSpec((rb, width), lambda i, at: (jnp.minimum(i, 1), 0)), pl.BlockSpec((rb, width), lambda i, at: (jnp.maximum(i - 2, 0), 0))]),
        out_shape=[sd((seg, width), f32), sd((seg, width), bf16)],
        compiler_params=pltpu.CompilerParams(vmem_limit_bytes=32 << 20),
        cost_estimate=pl.CostEstimate(flops=6 * pair * half * width, bytes_accessed=12 << 20, transcendentals=0),
    )(at, *dq, *dk, *dv, w, w, w, back)


def gather_z(own, steps):
    return [send_z(own, k) for k in steps]


def columns(got, cuts):
    return [jnp.stack([g[lo:hi] for g in got]) for lo, hi in cuts]


def scatter_one(g):
    return send_x(g[1]), send_y(g[3])


def two_blocks(g, one):
    return add_low(g[0][1], one[0][1]), add_low(g[2][1], one[1][1])


def scatter_two(blocks):
    return send_y(blocks[0]), send_x(blocks[1])


def scatter_total(g, one, two):
    total = lambda u, v, w: (u.astype(f32) + v.astype(f32) + w.astype(f32)).astype(bf16)
    a, b = total(g[0][0], one[0][0], two[0]), total(g[2][0], one[1][0], two[1])
    return [jnp.stack([a[:, k], b[:, k]]) for k in range(4)]


def scatter_z(v):
    return [send_z(v[k], k) for k in range(1, 4)]


def z_sum(v, got):
    total = v[0].astype(f32)
    for g in got:
        total = total + g.astype(f32)
    return total.astype(bf16)


def scatter_x(total, other):
    x = lax.axis_index("stream")
    return jnp.concatenate([jnp.where(x == 0, total, other), jnp.where(x == 0, other, total)])


def local_pair(
    tokens, resets, retrieved, memory_keys, memory_values, qkv_weight, out_weight, up_weight, up_bias,
    down_weight, down_bias, attn_gain, attn_shift, ffn_gain, ffn_shift, position_bias, memory_gate, cotangent,
):
    heads = memory_gate.shape[0]
    seg, width = tokens.shape[1:]
    dh = width // heads
    shards = lax.axis_size("fsdp")
    chips = shards // 2
    mem_rows = memory_keys.shape[1]
    mem = mem_rows * shards
    nz, z, y, c, x = places()
    at = jnp.stack([z, y, c, x]).astype(jnp.int32)
    low_core = c == 0
    both = lambda own, other: (jnp.where(low_core, own, other), jnp.where(low_core, other, own))
    tok, cot = tokens[0], cotangent[0]
    part = width // shards
    vectors = [up_bias, down_bias, attn_gain, attn_shift, ffn_gain, ffn_shift, position_bias]
    sizes = [v.shape[0] for v in vectors]
    tok_other, cot_other = send_core(tok), send_core(cot)
    ret = jnp.transpose(retrieved[0], (1, 2, 0)).reshape(2, 4, retrieved.shape[3], seg)
    p0, p1 = both(take(ret, c, 0), send_core(take(ret, 1 - c, 0)))
    q_own, q_swap, r_own, r_swap, d_own = prepare(
        at, resets, qkv_weight, up_weight, down_weight, out_weight, memory_keys[0], memory_values[0], vectors)
    q_got, r_got = send_core(q_swap), send_core(r_swap)
    hot, rel = bucket_hot(seg)
    gate = lax.dynamic_slice_in_dim(jax.nn.sigmoid(memory_gate.astype(f32)), 4 * c, 4, 0)
    q0, q1 = both(q_own, q_got)
    own_qkv = jnp.concatenate([q0[:64], q1[:64], q0[128:], q1[128:], q0[64:128], q1[64:128]])
    reset = jnp.stack([q0[135, 0], q1[135, 0]]).astype(jnp.int32)
    second = jnp.where(low_core, tok_other, tok)
    own_qkv, r_got, tok, tok_other, cot_other, p0, p1 = fence(own_qkv, r_got, tok, tok_other, cot_other, p0, p1)
    g0 = [own_qkv] + gather_z(own_qkv, (1, 2, 3))
    ty = lax.ppermute(tok, "fsdp", [(i, i ^ 2) for i in range(1, shards, 2)])
    masks = (hit_masks(at, p0, mem), hit_masks(at, p1, mem))
    own_f1, own_f2 = pack_ffn(at, r_own, r_got, d_own, mem_rows)
    g0, masks, own_f1, own_f2, ty = fence(g0, masks, own_f1, own_f2, ty)
    a, b = columns(g0, ((0, 144), (144, 272)))
    a, b, ty = fence(a, b, ty)
    ya, xb, xa, yb = send_y(a), send_x(b), send_x(a), send_y(b)
    tz = lax.ppermute(ty, "fsdp", [(i, i + 4) for i in range(1, shards - 4, 4)])
    a, ya, xb, xa, yb, b, own_f1, ty, tz = fence(a, ya, xb, xa, yb, b, own_f1, ty, tz)
    tp = jnp.where(y == 0, tz, ty)
    tp = jnp.where(low_core, lax.ppermute(tp, "fsdp", [(i, i - 1) for i in range(1, shards, 2)]), tp)
    small = jnp.stack([a[:, 128:, :256], ya[:, 128:, :256]]).reshape(2, 2, 2, 16, 256)
    for axis, bit in enumerate((y, z // 2, z % 2)):
        small = jnp.where(bit == 1, jnp.flip(small, axis), small)
    small = jnp.transpose(small.reshape(2, 4, 16, 256), (1, 0, 2, 3)).reshape(shards, 8, 256)
    cols = [small[:, k, :s] for k, s in enumerate(sizes)]
    b_down, gain_one, shift_one, gain_two, shift_two = [v.reshape(1, -1) for v in cols[1:6]]
    b_up = take(cols[0].reshape(chips, 2, 2, 128), c, 1)
    b_up = [b_up[:, k].reshape(1, -1) for k in range(2)]
    table = lax.dynamic_slice_in_dim(cols[6].reshape(heads, -1).astype(f32), 4 * c, 4, 0)
    base = diagonal_bias(table, hot, rel)
    ya, xb, own_f1, tp, base, b_up, gain_one, shift_one, b_down, gain_two, shift_two = fence(
        ya, xb, own_f1, tp, base, b_up, gain_one, shift_one, b_down, gain_two, shift_two)
    g0 = [a, ya, xa, send_x(ya), b, xb, yb, send_y(xb)]
    f1 = [own_f1] + gather_z(own_f1, (1, 2, 3))
    g0, f1, own_f2, tp = fence(g0, f1, own_f2, tp)
    a, b = columns(f1, ((0, 448), (448, 768)))
    a, b, tp = fence(a, b, tp)
    ya, xb = send_y(a), send_x(b)
    f2 = [own_f2] + gather_z(own_f2, (1, 2))
    q, k, v, rq, rk, xn, w_qkv = project_pair(at, tp, tok, tok_other, gain_one, shift_one, g0)
    q, k, v, a, b, ya, xb, f2 = fence(q, k, v, a, b, ya, xb, f2)
    pack = (a, ya)
    xa, xra, q = fence(a[:, :320], ya[:, :320], q)
    f1 = [a, ya, send_x(xa), send_x(xra), b, xb, send_y(b), send_y(xb)]
    f2 = f2 + gather_z(f2[0], (3,))
    att, loc, rem = attend(gate, reset, at, q, k, v, base, pack, masks)
    att, f1, f2 = fence(att, f1, f2)
    att_other = send_core(att)
    out_other = out_rows_of(f1)
    a, b = columns(f2, ((0, 256), (256, 512)))
    att_other, out_other, a, b = fence(att_other, out_other, a, b)
    out_other = send_core(out_other)
    ya, xb = send_y(a), send_x(b)
    att_other, out_other, f1, a, b, ya, xb = fence(att_other, out_other, f1, a, b, ya, xb)
    f2 = [a, ya, send_x(a), send_x(ya), b, xb, send_y(b), send_y(xb)]
    low, res, o1, h1, w_out, *n1, gbu1 = ffn_half(at, True, (att, att_other, tok, tok_other, gain_two, shift_two, out_other), cot, cot_other, b_up[0], f1)
    low, o1, h1, n1, f2 = fence(low, o1, h1, n1, f2)
    s1 = scatter_one(n1)
    oo, ox, go, gx, *n2, gbu2 = ffn_half(at, False, (low, o1, h1), cot, cot_other, b_up[1], f2)
    gx, ox, s1, n2, oo, go = fence(gx, ox, s1, n2, oo, go)
    gx, ox, w1 = send_core(gx), send_core(ox), two_blocks(n1, s1)
    gx, ox, w1 = fence(gx, ox, w1)
    u1 = scatter_two(w1)
    output, one, ol, vec_two = join(res, oo, ox, go, gx, cot, gain_two, b_down)
    ol, u1 = fence(ol, u1)
    ol_other = send_core(ol)
    v1 = scatter_total(n1, s1, u1)
    ol_other, ol, v1, n2 = fence(ol_other, ol, v1, n2)
    s2 = scatter_one(n2)
    z1 = scatter_z(v1)
    dqa, dka, dva, diag_a, dgate_a = attend_back(0, gate, reset, at, q, k, v, base, pack, masks, loc, rem, ol, ol_other, w_out, rq, rk)
    dqa, dka, dva, s2, z1, ol, diag_a, dgate_a = fence(dqa, dka, dva, s2, z1, ol, diag_a, dgate_a)
    w2, dqa, ol = fence(two_blocks(n2, s2), dqa, ol)
    u2 = scatter_two(w2)
    na = qkv_wgrad(0, at, xn, dqa, dka, dva, att, att_other, ol, ol_other)
    na, u2, ol = fence(na, u2, ol)
    v2, ol = fence(scatter_total(n2, s2, u2), ol)
    sa = scatter_one(na)
    z2 = scatter_z(v2)
    dqb, dkb, dvb, diag_b, dgate_b = attend_back(1, gate, reset, at, q, k, v, base, pack, masks, loc, rem, ol, ol_other, w_out, rq, rk)
    dqb, dkb, dvb, sa, z2, diag_b, dgate_b = fence(dqb, dkb, dvb, sa, z2, diag_b, dgate_b)
    wa, dkb = fence(two_blocks(na, sa), dkb)
    ua = scatter_two(wa)
    nb = qkv_wgrad(1, at, xn, dqb, dkb, dvb, att, att_other, ol, ol_other)
    back = before_grad((dka, dkb), (dva, dvb), w_qkv).reshape(2, seg // 2, width)
    nb, back, ua, z1, z2 = fence(nb, back, ua, z1, z2)
    va, back_out, nb = fence(scatter_total(na, sa, ua), take(back, 1 - c, 0), nb)
    back_got = send_core(back_out)
    sb = scatter_one(nb)
    za = scatter_z(va)
    t1, t2 = z_sum(v1, z1), z_sum(v2, z2)
    sb, back_got, t1, t2, za = fence(sb, back_got, t1, t2, za)
    wb, back, t1, t2 = fence(two_blocks(nb, sb), add_low(take(back, c, 0), back_got), t1, t2)
    ub = scatter_two(wb)
    back = lax.ppermute(back, "fsdp", [(i, i - 2) for i in range(2, shards)])
    x1, x2 = send_x(t1), send_x(t2)
    ub, back, x1, x2 = fence(ub, back, x1, x2)
    vb, back = fence(scatter_total(nb, sb, ub), back)
    zb = scatter_z(vb)
    ho, hx = hgrad(at, (dqa, dqb), (dka, dkb), (dva, dvb), w_qkv, back)
    zb, hx, ho, diag_a, diag_b, dgate_a, dgate_b, gbu1, gbu2, vec_two = fence(zb, hx, ho, diag_a, diag_b, dgate_a, dgate_b, gbu1, gbu2, vec_two)
    t_ab = jnp.concatenate([z_sum(va, za), z_sum(vb, zb)], axis=1)
    t_ab, hx = fence(t_ab, hx)
    x_ab = send_x(t_ab)
    token_grad, vec_one = finish(ho, send_core(hx), tok, one, gain_one)
    t_f1, t_f2 = scatter_x(t1, x1), scatter_x(t2, x2)
    by_head = lambda a, b: jnp.stack([a, b], axis=1).reshape((4,) + a.shape[1:])
    diag, dgate = by_head(diag_a, diag_b), by_head(dgate_a, dgate_b)
    mine_core = jnp.arange(2) == c
    gbu = jnp.stack([gbu1[0].reshape(chips, 128), gbu2[0].reshape(chips, 128)], axis=1)
    gbu = jnp.where(mine_core[None, :, None, None], gbu[:, None], 0.0).reshape(shards, -1)
    table_g = jnp.dot(diag[:, 0], hot.T, precision=lax.Precision.HIGHEST)
    table_g = jnp.where(mine_core[:, None, None], table_g[None], 0.0).reshape(shards, -1)
    gate_g = jnp.where(mine_core[:, None], dgate[:, 0, 0][None], 0.0).reshape(1, heads)
    up_sum = jnp.stack([t_f1[:, 0], t_f2[:, 0]]).reshape(2, 4, 2, 64, 256)
    up_got = send_core(take(up_sum, 1 - c, 2))
    x_ab, vec_one, up_got = fence(x_ab, vec_one, up_got)
    t_qkv = jnp.transpose(scatter_x(t_ab, x_ab).reshape(2, 2, 2, 64, 512), (0, 2, 1, 3, 4))
    qkv_sum = t_qkv.reshape(4, 2, 64, 512)
    qkv_got = send_core(take(qkv_sum, 1 - c, 1))
    pack = [gbu] + [v.reshape(shards, -1) for v in (vec_two[2], vec_one[0], vec_one[1], vec_two[0], vec_two[1])] + [table_g, jnp.broadcast_to(gate_g, (shards, heads))]
    total = jnp.concatenate(pack, axis=1)
    total = total + send_core(total)
    diagonal = lax.ppermute(total, ("stream", "fsdp"), [(s * shards + i, (1 - s) * shards + (i ^ 2)) for s in range(2) for i in range(shards)])
    total = (total + send_y(total)) + (send_x(total) + diagonal)
    total = (total + send_z(total, 1)) + (send_z(total, 2) + send_z(total, 3))
    total = take(total, lax.axis_index("fsdp"), 0)
    up_all = jnp.stack(both(take(up_sum, c, 2), up_got)).astype(f32)
    up_t = jnp.concatenate([up_all[cc, hf, q_, :, yy * 128 : (yy + 1) * 128] for q_ in range(4) for yy in range(2) for cc in range(2) for hf in range(2)], axis=1)
    down_t = jnp.concatenate([jnp.concatenate([t[q_, 1] for q_ in range(4)], axis=1) for t in (t_f1, t_f2)], axis=0).astype(f32)
    qkv_all = jnp.stack(both(take(qkv_sum, c, 1), qkv_got)).astype(f32)
    qkv_t = jnp.concatenate([qkv_all[cc, h, :, p * dh : (p + 1) * dh] for p in range(3) for cc in range(2) for h in range(4)], axis=1)
    out_t = jnp.concatenate([qkv_all[cc, h, :, 3 * dh :] for cc in range(2) for h in range(4)], axis=1)
    outs, off = [], 0
    for s in sizes + [heads]:
        outs.append(total[off : off + s])
        off += s
    ub, db, ag, ash, fg, fs, pg, gg = outs
    return output[None], token_grad[None], qkv_t, out_t, up_t, ub, down_t, db, ag, ash, fg, fs, pg, gg


def solution(mesh):
    row = P("stream", "fsdp", None)
    return jax.shard_map(
        local_pair if mesh.shape["fsdp"] == 16 else local_wide,
        mesh=mesh,
        in_specs=(
            row, P("stream", "fsdp"), P("stream", "fsdp", None, None), row, row, P("fsdp", None), P("fsdp", None),
            P("fsdp", None), P("fsdp"), P("fsdp", None), P("fsdp"), P("fsdp"), P("fsdp"), P("fsdp"), P("fsdp"),
            P("fsdp"), P(), row,
        ),
        out_specs=(
            row, row, P("fsdp", None), P("fsdp", None), P("fsdp", None), P("fsdp"), P("fsdp", None), P("fsdp"),
            P("fsdp"), P("fsdp"), P("fsdp"), P("fsdp"), P("fsdp"), P(),
        ),
        check_vma=False,
    )
```

```python
import functools
import math
import jax, jax.numpy as jnp
from jax import lax
from jax.experimental import pallas as pl
from jax.experimental.pallas import tpu as pltpu
f32=jnp.float32; bf16=jnp.bfloat16
LOG2E=math.log2(math.e)
NEG=-1e30

def nt(a,b): return lax.dot_general(a,b,(((1,),(1,)),((),())),preferred_element_type=f32)
def nn(a,b): return lax.dot_general(a,b,(((1,),(0,)),((),())),preferred_element_type=f32)
def tn(a,b): return lax.dot_general(a,b,(((0,),(0,)),((),())),preferred_element_type=f32)

from jax.experimental.layout import Layout, with_layout_constraint
from jax.sharding import PartitionSpec as P


def xor_perm(bit, n):
    return [(i, i ^ bit) for i in range(n)]


def places():
    n = lax.axis_size("fsdp")
    i = lax.axis_index("fsdp")
    return n // 4, i // 4, (i // 2) % 2, i % 2, lax.axis_index("stream")


def send_core(v):
    return lax.ppermute(v, "fsdp", xor_perm(1, lax.axis_size("fsdp")))


def send_y(v):
    return lax.ppermute(v, "fsdp", xor_perm(2, lax.axis_size("fsdp")))


def send_z(v, k):
    return lax.ppermute(v, "fsdp", xor_perm(4 * k, lax.axis_size("fsdp")))


def send_x(v):
    return lax.ppermute(v, "stream", [(0, 1), (1, 0)])


def gather_small(memory_keys, memory_values, vectors, heads):
    mem_rows, width = memory_keys.shape[1:]
    keys = memory_keys[0].astype(f32).reshape(mem_rows, heads, width // heads)
    keys = keys * lax.rsqrt(jnp.sum(keys * keys, axis=-1, keepdims=True) + 1e-06)
    small = jnp.concatenate(vectors)
    small = jnp.pad(small[None], ((0, 15), (0, width - small.shape[0])))
    pack = jnp.concatenate([keys.reshape(mem_rows, width).astype(bf16), memory_values[0], small], axis=0)
    pack = lax.all_gather(pack, "fsdp", axis=0)
    return pack[:, 2 * mem_rows], pack[:, :mem_rows].reshape(-1, width), pack[:, mem_rows : 2 * mem_rows].reshape(-1, width)


def scatter_weights(gs):
    whole = [jnp.concatenate([g[q] for q in range(4)], axis=1) for g in gs]
    got = [lax.psum_scatter(g, "fsdp", scatter_dimension=0, tiled=True) for g in whole]
    return [g.astype(f32) for g in lax.psum(got, "stream")]


def summed_everywhere(v):
    bit = 1
    while bit < lax.axis_size("fsdp"):
        v = v + lax.ppermute(v, "fsdp", xor_perm(bit, lax.axis_size("fsdp")))
        bit *= 2
    return v + send_x(v)


def passed_along(block, axis, distance):
    devices = range(lax.axis_size(axis))
    return lax.ppermute(block, axis, [(i - distance, i) for i in devices if i - distance in devices])


def norm_stats(x):
    center = x - jnp.mean(x, axis=-1, keepdims=True)
    spread_sq = jnp.mean(center * center, axis=-1, keepdims=True)
    r = lax.rsqrt(spread_sq + 1e-05)
    return center * r, r


def norm_back(grad, n, r, gain):
    gn = grad * gain
    return r * (gn - jnp.mean(gn, axis=-1, keepdims=True) - n * jnp.mean(gn * n, axis=-1, keepdims=True))


def mask_kernel(p_ref, o_ref, *, rows):
    n, k = p_ref.shape
    mem = o_ref.shape[1]
    for r in range(0, n, rows):
        p = p_ref[r:r+rows, :]
        ids = lax.broadcasted_iota(jnp.int32, (rows, mem), 1)
        hit = p[:, 0:1] == ids
        for t in range(1, k):
            hit = hit | (p[:, t:t+1] == ids)
        o_ref[r:r+rows, :] = jnp.where(hit, 1.0, 0.0).astype(bf16)

def picked_masks(picked, mem, interpret=False):
    h, n, k = picked.shape
    return pl.pallas_call(
        functools.partial(mask_kernel, rows=32),
        grid=(h,),
        in_specs=[pl.BlockSpec((None, n, k), lambda i: (i,0,0))],
        out_specs=pl.BlockSpec((None, n, mem), lambda i: (i,0,0)),
        out_shape=jax.ShapeDtypeStruct((h,n,mem), bf16),
        cost_estimate=pl.CostEstimate(flops=2*h*n*k*mem, bytes_accessed=h*n*(mem*2+512), transcendentals=0),
        interpret=interpret,
    )(picked)

def spread(base, blk):
    w = base.shape[1]
    x = jnp.broadcast_to(base, (8, w))
    r = lax.broadcasted_iota(jnp.int32, (8, w), 0)
    for b in (1, 2, 4):
        x = jnp.where((r & b) != 0, pltpu.roll(x, b, 1), x)
    size = 8
    while size < blk:
        x = jnp.concatenate([x, pltpu.roll(x, size, 1)], axis=0)
        size *= 2
    return x

def gather_diagonals(g):
    size, w = g.shape
    while size > 8:
        half = size // 2
        g = g[:half] + pltpu.roll(g[half:], w - half, 1)
        size = half
    r = lax.broadcasted_iota(jnp.int32, (8, w), 0)
    for b in (4, 2, 1):
        g = jnp.where((r & b) != 0, pltpu.roll(g, w - b, 1), g)
    return jnp.sum(g, axis=0, keepdims=True)

BLK = 128

def unit_back(g, u, r):
    u = u.astype(f32)
    return (r * (g - u * jnp.sum(g * u, axis=1, keepdims=True))).astype(bf16)

edges=[b for b in range(1,16)]+[int(math.ceil(16.0*8.0**((b-16)/16.0))) for b in range(16,32)]
def diagonal_rel(seg):
    wt = 2*seg + seg - BLK + BLK
    k = jnp.arange(wt, dtype=jnp.int32)
    top = 2*seg - BLK
    return jnp.where(k > wt - BLK, top - (k - wt), top - k)

def bucket_hot(seg):
    rel = diagonal_rel(seg)
    counts = jnp.zeros_like(rel)
    for e in edges: counts = counts + (rel >= e).astype(jnp.int32)
    hot = (counts[None,:] == jnp.arange(len(edges)+1)[:,None]) & (rel >= 0)[None,:]
    return hot.astype(f32), rel
def diagonal_bias(table, hot, rel):
    v = jnp.dot(table, hot, precision=lax.Precision.HIGHEST) * LOG2E
    return jnp.where(rel[None,:] >= 0, v, NEG)[:, None, :]


def wide_fwd_kernel(gate_ref, reset_ref, q_ref, kp_ref, kc_ref, vp_ref, vc_ref, base_ref, mk_ref, mv_ref, mask_ref,
                    mix_ref, loc_ref, rem_ref, t_ref):
    seg = q_ref.shape[0]
    h = pl.program_id(0)
    s = gate_ref[h]
    keep = jnp.where(reset_ref[0] == 0, 1.0, 0.0).astype(f32)
    t_ref[...] = spread(base_ref[...], BLK)
    heat = 16.0 * LOG2E
    nb = seg // BLK
    vp = vp_ref[...] * keep.astype(bf16)
    mk = mk_ref[...]; mv = mv_ref[...]
    for i in range(nb):
        rows = slice(i*BLK, (i+1)*BLK)
        q = q_ref[rows, :]
        off = (nb-1-i)*BLK
        cw = (i+1)*BLK
        ep = jnp.exp2(nt(q, kp_ref[...]) * heat + t_ref[:, off:off+seg])
        ec = jnp.exp2(nt(q, kc_ref[:cw, :]) * heat + t_ref[:, off+seg:off+seg+cw])
        il = 1.0 / (keep * jnp.sum(ep, axis=1, keepdims=True) + jnp.sum(ec, axis=1, keepdims=True))
        o = nn((ep * il).astype(bf16), vp) + nn((ec * il).astype(bf16), vc_ref[:cw, :])
        em = jnp.exp2(nt(q, mk) * heat) * mask_ref[rows, :].astype(f32)
        em = em * (1.0 / jnp.sum(em, axis=1, keepdims=True))
        om = nn(em.astype(bf16), mv)
        loc_ref[rows, :] = o.astype(bf16)
        rem_ref[rows, :] = om.astype(bf16)
        mix_ref[rows, :] = (s*om + (1.0-s)*o).astype(bf16)

def attn_fwd(gate, reset, q, kp, kc, vp, vc, base, mk, mv, mask, interpret=False):
    seg, width = q.shape
    heads = base.shape[0]
    dh = width // heads
    mem = mk.shape[0]
    col = lambda n: pl.BlockSpec((n, dh), lambda h, *_: (0, h))
    full = jax.ShapeDtypeStruct((seg, width), bf16)
    wt = base.shape[2]
    return pl.pallas_call(
        wide_fwd_kernel,
        grid_spec=pltpu.PrefetchScalarGridSpec(
            num_scalar_prefetch=2, grid=(heads,),
            in_specs=[col(seg), col(seg), col(seg), col(seg), col(seg),
                      pl.BlockSpec((None,1,wt), lambda h,*_: (h,0,0)), col(mem), col(mem),
                      pl.BlockSpec((None,seg,mem), lambda h,*_: (h,0,0))],
            out_specs=[col(seg), col(seg), col(seg)],
            scratch_shapes=[pltpu.VMEM((BLK, wt), f32)]),
        out_shape=[full, full, full],
        compiler_params=pltpu.CompilerParams(vmem_limit_bytes=48<<20),
        cost_estimate=pl.CostEstimate(flops=heads*seg*(2*seg+mem)*4*dh, bytes_accessed=8*seg*width*2+heads*seg*mem*2, transcendentals=heads*seg*(2*seg+mem)),
        interpret=interpret,
    )(gate, reset, q, kp, kc, vp, vc, base, mk, mv, mask)

def wide_bwd_kernel(gate_ref, reset_ref, q_ref, kp_ref, kc_ref, vp_ref, vc_ref, base_ref, mk_ref, mv_ref, mask_ref,
                    loc_ref, rem_ref, gm_ref, rq_ref, rkp_ref, rkc_ref,
                    dc_ref, dp_ref, diag_ref, dgate_ref, t_ref, g_ref, akp, akc, avp, avc):
    seg = q_ref.shape[0]
    h = pl.program_id(0)
    s = gate_ref[h]
    keep = jnp.where(reset_ref[0] == 0, 1.0, 0.0).astype(f32)
    t_ref[...] = spread(base_ref[...], BLK)
    g_ref[...] = jnp.zeros_like(g_ref)
    heat = 16.0 * LOG2E
    nb = seg // BLK
    mk = mk_ref[...]; mv = mv_ref[...]
    dg = jnp.zeros((BLK, 1), f32)
    for i in range(nb):
        rows = slice(i*BLK, (i+1)*BLK)
        q = q_ref[rows, :]
        gm = gm_ref[rows, :]
        off = (nb-1-i)*BLK
        cw = (i+1)*BLK
        al = jnp.sum(gm * loc_ref[rows, :].astype(f32), axis=1, keepdims=True)
        ar = jnp.sum(gm * rem_ref[rows, :].astype(f32), axis=1, keepdims=True)
        dg = dg + (ar - al)
        gl = ((1.0-s)*gm).astype(bf16)
        gr = (s*gm).astype(bf16)
        ep = jnp.exp2(nt(q, kp_ref[...]) * heat + t_ref[:, off:off+seg])
        ec = jnp.exp2(nt(q, kc_ref[:cw, :]) * heat + t_ref[:, off+seg:off+seg+cw])
        l = keep * jnp.sum(ep, axis=1, keepdims=True) + jnp.sum(ec, axis=1, keepdims=True)
        il = 1.0 / l
        ilp = il * keep
        pp = ep * ilp
        pc = ec * il
        wp = pp * nt(gl, vp_ref[...])
        wc = pc * nt(gl, vc_ref[:cw, :])
        dl = jnp.sum(wp, axis=1, keepdims=True) + jnp.sum(wc, axis=1, keepdims=True)
        dsp = (wp - pp * dl).astype(bf16); dsc = (wc - pc * dl).astype(bf16)
        g_ref[:, off:off+seg] += dsp.astype(f32)
        g_ref[:, off+seg:off+seg+cw] += dsc.astype(f32)
        dq = nn(dsp, kp_ref[...]) + nn(dsc, kc_ref[:cw, :])
        ppb = pp.astype(bf16); pcb = pc.astype(bf16)
        dkp = tn(dsp, q); dvp = tn(ppb, gl)
        dkc = tn(dsc, q); dvc = tn(pcb, gl)
        if i == 0:
            akp[...] = dkp; avp[...] = dvp
            akc[...] = jnp.zeros_like(akc); avc[...] = jnp.zeros_like(avc)
            akc[:cw, :] = dkc; avc[:cw, :] = dvc
        else:
            akp[...] += dkp; avp[...] += dvp
            akc[:cw, :] += dkc; avc[:cw, :] += dvc
        em = jnp.exp2(nt(q, mk) * heat) * mask_ref[rows, :].astype(f32)
        ilm = 1.0 / jnp.sum(em, axis=1, keepdims=True)
        em = em * ilm
        gw = nt(gr, mv)
        dsm = em * (gw - jnp.sum(em * gw, axis=1, keepdims=True))
        dq = dq + nn(dsm.astype(bf16), mk)
        dc_ref[0, rows, :] = unit_back(16.0 * dq, q, rq_ref[rows, :])
    dp_ref[0] = unit_back(16.0 * akp[...], kp_ref[...], rkp_ref[...])
    dc_ref[1] = unit_back(16.0 * akc[...], kc_ref[...], rkc_ref[...])
    dp_ref[1] = avp[...].astype(bf16)
    dc_ref[2] = avc[...].astype(bf16)
    diag_ref[...] = gather_diagonals(g_ref[...])
    dgate_ref[...] = jnp.broadcast_to(jnp.sum(dg) * s * (1.0-s), dgate_ref.shape)

def attn_bwd(gate, reset, q, kp, kc, vp, vc, rq, rkp, rkc, base, mk, mv, mask, loc, rem, gm, interpret=False):
    seg, width = q.shape
    heads = base.shape[0]
    dh = width // heads
    mem = mk.shape[0]
    wt = base.shape[2]
    col = lambda n: pl.BlockSpec((n, dh), lambda h, *_: (0, h))
    row = lambda w: pl.BlockSpec((None,1,w), lambda h,*_: (h,0,0))
    rcol = pl.BlockSpec((None,seg,1), lambda h,*_: (h,0,0))
    fb = jax.ShapeDtypeStruct((seg, width), bf16)
    return pl.pallas_call(
        wide_bwd_kernel,
        grid_spec=pltpu.PrefetchScalarGridSpec(
            num_scalar_prefetch=2, grid=(heads,),
            in_specs=[col(seg)]*5 + [row(wt), col(mem), col(mem),
                      pl.BlockSpec((None,seg,mem), lambda h,*_: (h,0,0)), col(seg), col(seg), col(seg), rcol, rcol, rcol],
            out_specs=[pl.BlockSpec((3,seg,dh), lambda h,*_: (0,0,h)), pl.BlockSpec((2,seg,dh), lambda h,*_: (0,0,h)), row(wt), row(128)],
            scratch_shapes=[pltpu.VMEM((BLK, wt), f32)]*2 + [pltpu.VMEM((seg, dh), f32)]*4),
        out_shape=[jax.ShapeDtypeStruct((3,seg,width),bf16), jax.ShapeDtypeStruct((2,seg,width),bf16), jax.ShapeDtypeStruct((heads,1,wt), f32), jax.ShapeDtypeStruct((heads,1,128), f32)],
        compiler_params=pltpu.CompilerParams(vmem_limit_bytes=48<<20),
        cost_estimate=pl.CostEstimate(flops=heads*seg*(2*seg+mem)*10*dh, bytes_accessed=20*seg*width*2+heads*seg*mem*2, transcendentals=heads*seg*(2*seg+mem)),
        interpret=interpret,
    )(gate, reset, q, kp, kc, vp, vc, base, mk, mv, mask, loc, rem, gm, rq, rkp, rkc)


def wide_qkv_kernel(xp_ref, xc_ref, gain_ref, shift_ref, w_ref, q_ref, kp_ref, kc_ref, vp_ref, vc_ref, rq_ref, rkp_ref, rkc_ref, np_ref, nc_ref, x_ref, *, dh):
    i = pl.program_id(0)
    per = pl.num_programs(0) // 3
    seg = xc_ref.shape[0]

    @pl.when(i == 0)
    def _():
        gain = gain_ref[...].astype(f32)
        shift = shift_ref[...].astype(f32)
        for src, dst, at in ((xp_ref, np_ref, 0), (xc_ref, nc_ref, seg)):
            n, r = norm_stats(src[...].astype(f32))
            low = (n * gain + shift).astype(bf16)
            x_ref[at : at + seg, :] = low
            dst[...] = low

    def unit(y, out_ref, r_ref):
        for k in range(y.shape[1] // dh):
            part = y[:, k * dh : (k + 1) * dh]
            r = lax.rsqrt(jnp.sum(part * part, axis=1, keepdims=True) + 1e-06)
            out_ref[:, k * dh : (k + 1) * dh] = (part * r).astype(bf16)
            r_ref[k] = r

    w = w_ref[...]

    @pl.when(i < per)
    def _():
        unit(nn(x_ref[seg:, :], w), q_ref, rq_ref)

    @pl.when((i >= per) & (i < 2 * per))
    def _():
        unit(nn(x_ref[:seg, :], w), kp_ref, rkp_ref)
        unit(nn(x_ref[seg:, :], w), kc_ref, rkc_ref)

    @pl.when(i >= 2 * per)
    def _():
        vp_ref[...] = nn(x_ref[:seg, :], w).astype(bf16)
        vc_ref[...] = nn(x_ref[seg:, :], w).astype(bf16)


def project_qkv(xp, xc, gain, shift, w, heads):
    seg, width = xc.shape
    dh = width // heads
    two = 2 * dh
    per = width // two
    whole = pl.BlockSpec((seg, width), lambda i: (0, 0))
    vec = pl.BlockSpec((1, width), lambda i: (0, 0))
    at = lambda s: (lambda i: (0, jnp.clip(i - s * per, 0, per - 1)))
    at3 = lambda s: (lambda i: (jnp.clip(i - s * per, 0, per - 1), 0, 0))
    cols = lambda s: pl.BlockSpec((seg, two), at(s))
    rs = lambda s: pl.BlockSpec((2, seg, 1), at3(s))
    low = jax.ShapeDtypeStruct((seg, width), bf16)
    rr = jax.ShapeDtypeStruct((heads, seg, 1), f32)
    return pl.pallas_call(
        functools.partial(wide_qkv_kernel, dh=dh),
        grid=(3 * per,),
        in_specs=[whole, whole, vec, vec, pl.BlockSpec((width, two), lambda i: (0, i))],
        out_specs=[cols(0), cols(1), cols(1), cols(2), cols(2), rs(0), rs(1), rs(1), whole, whole],
        out_shape=[low] * 5 + [rr] * 3 + [low] * 2,
        scratch_shapes=[pltpu.VMEM((2 * seg, width), bf16)],
        compiler_params=pltpu.CompilerParams(vmem_limit_bytes=48 << 20),
        cost_estimate=pl.CostEstimate(flops=2 * seg * width * width * 5, bytes_accessed=3 * width * width * 2 + 9 * seg * width * 2, transcendentals=0),
    )(xp, xc, gain, shift, w)


def middle_kernel(att_ref, tok_ref, cot_ref, wo_ref, up_ref, dn_ref, bu_ref, bd_ref, gain_ref, shift_ref,
                  out_ref, one_ref, gm_ref, gup_ref, gdn_ref, gout_ref, gbu_ref, vec_ref,
                  res_ref, n_ref, low_ref, r_ref, acc_ref, gh_ref):
    j = pl.program_id(0)
    last = pl.num_programs(0) - 1
    width = tok_ref.shape[1]

    @pl.when(j == 0)
    def _():
        res = tok_ref[...].astype(f32) + nn(att_ref[...], wo_ref[...])
        res_ref[...] = res
        n, r = norm_stats(res)
        n_ref[...] = n
        r_ref[...] = r
        low_ref[...] = (n * gain_ref[...].astype(f32) + shift_ref[...].astype(f32)).astype(bf16)

    low = low_ref[...]
    cot = cot_ref[...]
    up = up_ref[...]
    dn = dn_ref[...]
    p = nn(low, up) + bu_ref[...].astype(f32)
    ga = nt(cot, dn)
    k0 = math.sqrt(2.0 / math.pi)
    p2 = p * p
    t = jnp.tanh(p * (k0 + (k0 * 0.044715) * p2))
    half = 0.5 * (1.0 + t)
    act = (p * half).astype(bf16)
    slope = half + 0.5 * p * (1.0 - t * t) * (k0 + (3.0 * k0 * 0.044715) * p2)
    gp = (ga * slope).astype(bf16)
    o = nn(act, dn)
    g = nt(gp, up)
    gup_ref[...] = tn(low, gp).astype(bf16)
    gd = tn(act, cot).astype(bf16)
    cols = width // 4
    for q in range(4):
        gdn_ref[q] = gd[:, q * cols : (q + 1) * cols]
    gbu_ref[...] = jnp.sum(gp.astype(f32), axis=0, keepdims=True)

    @pl.when(j == 0)
    def _():
        acc_ref[...] = o
        gh_ref[...] = g

    @pl.when(j > 0)
    def _():
        acc_ref[...] += o
        gh_ref[...] += g

    @pl.when(j == last)
    def _():
        out_ref[...] = (res_ref[...] + acc_ref[...] + bd_ref[...].astype(f32)).astype(bf16)
        gh = gh_ref[...]
        n = n_ref[...]
        cf = cot.astype(f32)
        vec_ref[0:1, :] = jnp.sum(gh * n, axis=0, keepdims=True)
        vec_ref[1:2, :] = jnp.sum(gh, axis=0, keepdims=True)
        vec_ref[2:3, :] = jnp.sum(cf, axis=0, keepdims=True)
        one = cf + norm_back(gh, n, r_ref[...], gain_ref[...].astype(f32))
        one_ref[...] = one
        ol = one.astype(bf16)
        gm_ref[...] = nt(ol, wo_ref[...])
        go = tn(att_ref[...], ol).astype(bf16)
        for q in range(4):
            gout_ref[q] = go[:, q * cols : (q + 1) * cols]


def middle(att, tok, cot, wo, up, dn, bu, bd, gain, shift):
    seg, width = tok.shape
    ff = up.shape[1]
    blk = 512
    per = ff // 4 // blk
    once = dict(pipeline_mode=pl.Buffered(1))
    whole = pl.BlockSpec((seg, width), lambda j: (0, 0), **once)
    vec = pl.BlockSpec((1, width), lambda j: (0, 0))
    q4 = width // 4
    return pl.pallas_call(
        middle_kernel,
        grid=(ff // blk,),
        in_specs=[whole, whole, whole, pl.BlockSpec((width, width), lambda j: (0, 0), **once),
                  pl.BlockSpec((width, blk), lambda j: (0, j)), pl.BlockSpec((blk, width), lambda j: (j, 0)),
                  pl.BlockSpec((1, blk), lambda j: (0, j)), vec, vec, vec],
        out_specs=[whole, whole, whole,
                   pl.BlockSpec((None, width, blk), lambda j: (j // per, 0, j % per)),
                   pl.BlockSpec((4, blk, q4), lambda j: (0, j, 0)),
                   pl.BlockSpec((4, width, q4), lambda j: (0, 0, 0), **once),
                   pl.BlockSpec((1, blk), lambda j: (0, j)),
                   pl.BlockSpec((8, width), lambda j: (0, 0))],
        out_shape=[jax.ShapeDtypeStruct((seg, width), bf16), jax.ShapeDtypeStruct((seg, width), f32), jax.ShapeDtypeStruct((seg, width), f32),
                   jax.ShapeDtypeStruct((4, width, ff // 4), bf16), jax.ShapeDtypeStruct((4, ff, q4), bf16), jax.ShapeDtypeStruct((4, width, q4), bf16),
                   jax.ShapeDtypeStruct((1, ff), f32), jax.ShapeDtypeStruct((8, width), f32)],
        scratch_shapes=[pltpu.VMEM((seg, width), f32)] * 2 + [pltpu.VMEM((seg, width), bf16), pltpu.VMEM((seg, 1), f32)] + [pltpu.VMEM((seg, width), f32)] * 2,
        compiler_params=pltpu.CompilerParams(vmem_limit_bytes=56 << 20),
        cost_estimate=pl.CostEstimate(flops=2 * seg * width * (6 * ff + 3 * width), bytes_accessed=8 * width * ff + 16 * seg * width, transcendentals=seg * ff),
    )(att, tok, cot, wo, up, dn, bu, bd, gain, shift)


def wide_back_kernel(d_ref, w_ref, o_ref, acc_ref):
    j = pl.program_id(0)
    g = nt(d_ref[...], w_ref[...])

    @pl.when(j == 0)
    def _():
        acc_ref[...] = g

    @pl.when(j > 0)
    def _():
        acc_ref[...] += g

    @pl.when(j == pl.num_programs(0) - 1)
    def _():
        o_ref[...] = acc_ref[...].astype(bf16)


def wide_before_grad(d_prev, w):
    _, seg, width = d_prev.shape
    blk = 512
    per = width // blk
    return pl.pallas_call(
        wide_back_kernel,
        grid=(2 * per,),
        in_specs=[pl.BlockSpec((None, seg, blk), lambda j: (j // per, 0, j % per)), pl.BlockSpec((width, blk), lambda j: (0, per + j))],
        out_specs=pl.BlockSpec((seg, width), lambda j: (0, 0)),
        out_shape=jax.ShapeDtypeStruct((seg, width), bf16),
        scratch_shapes=[pltpu.VMEM((seg, width), f32)],
        compiler_params=pltpu.CompilerParams(vmem_limit_bytes=32 << 20),
        cost_estimate=pl.CostEstimate(flops=4 * seg * width * width, bytes_accessed=4 * width * width, transcendentals=0),
    )(d_prev, w)


def tail_kernel(dc_ref, dp_ref, nc_ref, np_ref, w_ref, g_ref, h_ref):
    j = pl.program_id(0)
    per = pl.num_programs(0) // 3
    dc = dc_ref[...]
    h = nt(dc, w_ref[...])

    @pl.when(j == 0)
    def _():
        h_ref[...] = h

    @pl.when(j > 0)
    def _():
        h_ref[...] += h

    @pl.when(j < per)
    def _():
        g_ref[...] = tn(nc_ref[...], dc).astype(bf16)

    @pl.when(j >= per)
    def _():
        g_ref[...] = (tn(nc_ref[...], dc) + tn(np_ref[...], dp_ref[...])).astype(bf16)


def qkv_back(d_cur, d_prev, n_cur, n_prev, w):
    _, seg, width = d_cur.shape
    blk = 256
    per = width // blk
    quarter = 3 * width // 4
    pq = quarter // blk
    whole = pl.BlockSpec((seg, width), lambda j: (0, 0))
    return pl.pallas_call(
        tail_kernel,
        grid=(3 * per,),
        in_specs=[pl.BlockSpec((None, seg, blk), lambda j: (j // per, 0, j % per)),
                  pl.BlockSpec((None, seg, blk), lambda j: (jnp.maximum(j // per - 1, 0), 0, jnp.where(j < per, 0, j % per))),
                  whole, whole, pl.BlockSpec((width, blk), lambda j: (0, j))],
        out_specs=[pl.BlockSpec((None, width, blk), lambda j: (j // pq, 0, j % pq)), whole],
        out_shape=[jax.ShapeDtypeStruct((4, width, quarter), bf16), jax.ShapeDtypeStruct((seg, width), f32)],
        compiler_params=pltpu.CompilerParams(vmem_limit_bytes=40 << 20),
        cost_estimate=pl.CostEstimate(flops=2 * seg * width * width * 8, bytes_accessed=12 * width * width + 16 * seg * width, transcendentals=0),
    )(d_cur, d_prev, n_cur, n_prev, w)


def last_kernel(h_ref, back_ref, tok_ref, one_ref, gain_ref, out_ref, vec_ref):
    h = h_ref[...] + back_ref[...].astype(f32)
    n, r = norm_stats(tok_ref[...].astype(f32))
    vec_ref[0:1, :] = jnp.sum(h * n, axis=0, keepdims=True)
    vec_ref[1:2, :] = jnp.sum(h, axis=0, keepdims=True)
    out_ref[...] = one_ref[...] + norm_back(h, n, r, gain_ref[...].astype(f32))


def finish(h, back, tok, one, gain):
    seg, width = tok.shape
    return pl.pallas_call(
        last_kernel,
        out_shape=[jax.ShapeDtypeStruct((seg, width), f32), jax.ShapeDtypeStruct((8, width), f32)],
        compiler_params=pltpu.CompilerParams(vmem_limit_bytes=40 << 20),
        cost_estimate=pl.CostEstimate(flops=20 * seg * width, bytes_accessed=16 * seg * width, transcendentals=0),
    )(h, back, tok, one, gain)


def local_wide(
    tokens, resets, retrieved, memory_keys, memory_values, qkv_weight, out_weight, up_weight, up_bias,
    down_weight, down_bias, attn_gain, attn_shift, ffn_gain, ffn_shift, position_bias, memory_gate, cotangent,
):
    heads = memory_gate.shape[0]
    seg, width = tokens.shape[1:]
    dh = width // heads
    mem_rows = memory_keys.shape[1]
    shards = lax.axis_size("fsdp")
    mem = mem_rows * shards
    part = width // shards
    bias_part = up_bias.shape[0]
    pos_part = position_bias.shape[0]
    small, mk, mv = gather_small(memory_keys, memory_values, [up_bias, down_bias, attn_gain, attn_shift, ffn_gain, ffn_shift, position_bias], heads)
    b_up = small[:, :bias_part].reshape(-1)
    vecs = [small[:, bias_part + k * part : bias_part + (k + 1) * part].reshape(1, -1) for k in range(5)]
    b_down, gain_one, shift_one, gain_two, shift_two = vecs
    table = small[:, bias_part + 5 * part : bias_part + 5 * part + pos_part].reshape(heads, -1).astype(f32)
    w_qkv, w_out, w_up, w_down = [lax.all_gather(w, "fsdp", axis=0, tiled=True) for w in (qkv_weight, out_weight, up_weight, down_weight)]
    before = passed_along(tokens[0], "fsdp", 1)
    mask = picked_masks(retrieved[0].transpose(1, 0, 2), mem)
    hot, rel = bucket_hot(seg)
    base = diagonal_bias(table, hot, rel)
    gate = jax.nn.sigmoid(memory_gate.astype(f32))
    reset = resets[0]
    q, kp, kc, vp, vc, rq, rkp, rkc, n_prev, n_cur = project_qkv(before, tokens[0], gain_one, shift_one, w_qkv, heads)
    attn_in, loc, rem = attn_fwd(gate, reset, q, kp, kc, vp, vc, base, mk, mv, mask)
    output, grad_one, gm, up_g, down_g, out_g, up_bias_g, vec_two = middle(
        attn_in, tokens[0], cotangent[0], w_out, w_up, w_down, b_up.reshape(1, -1), b_down, gain_two, shift_two)
    up_t, down_t, out_t = scatter_weights((up_g, down_g, out_g))
    d_cur, d_prev, diag, dgate = attn_bwd(gate, reset, q, kp, kc, vp, vc, rq, rkp, rkc, base, mk, mv, mask, loc, rem, gm)
    gate_g = dgate[:, 0, 0]
    table_g = jnp.dot(diag[:, 0], hot.T, precision=lax.Precision.HIGHEST)
    back = passed_along(wide_before_grad(d_prev, w_qkv), "fsdp", -1)
    qkv_g, grad_h1 = qkv_back(d_cur, d_prev, n_cur, n_prev, w_qkv)
    (qkv_t,) = scatter_weights((qkv_g,))
    token_grad, vec_one = finish(grad_h1, back, tokens[0], grad_one, gain_one)
    gain_two_g, shift_two_g, down_bias_g = vec_two[0], vec_two[1], vec_two[2]
    gain_one_g, shift_one_g = vec_one[0], vec_one[1]
    small_g = jnp.concatenate(
        [up_bias_g.reshape(shards, -1)]
        + [v.reshape(shards, -1) for v in (down_bias_g, gain_one_g, shift_one_g, gain_two_g, shift_two_g, table_g)]
        + [jnp.broadcast_to(gate_g[None], (shards, heads))],
        axis=1,
    )
    small_g = summed_everywhere(small_g)
    small_g = lax.dynamic_index_in_dim(small_g, lax.axis_index("fsdp"), 0, keepdims=False)
    cuts = [bias_part] + [part] * 5 + [pos_part, heads]
    at = 0
    outs = []
    for c in cuts:
        outs.append(small_g[at : at + c])
        at += c
    ub, db, g1, s1, g2, s2, pg, gg = outs
    return output[None], token_grad[None], qkv_t, out_t, up_t, ub, down_t, db, g1, s1, g2, s2, pg, gg


def take(v, i, axis):
    return lax.dynamic_index_in_dim(v, i, axis, keepdims=False)


def fence(*trees):
    return lax.optimization_barrier(trees)


def major_first(v):
    return with_layout_constraint(v, Layout(tuple(range(v.ndim))))


def add_low(u, v):
    return (u.astype(f32) + v.astype(f32)).astype(bf16)


def hits_kernel(at_ref, p_ref, o_ref):
    slots, n = p_ref.shape
    mem = o_ref.shape[0]
    lane = 128
    ids = lax.broadcasted_iota(jnp.int32, (mem, lane), 0)
    rows = mem // 8
    chip = (((ids // rows) & 3) ^ at_ref[0]) * 2 + ((ids // (4 * rows)) ^ at_ref[1])
    ids = chip * rows + ids % rows
    for t in range(n // lane):
        cols = slice(t * lane, (t + 1) * lane)
        acc = jnp.zeros((mem, lane), f32)
        for s in range(slots):
            acc = jnp.where(ids == p_ref[s : s + 1, cols], 1.0, acc)
        o_ref[:, cols] = acc.astype(bf16)


def hit_masks(at, picked, mem):
    h, slots, n = picked.shape
    return pl.pallas_call(
        hits_kernel,
        grid_spec=pltpu.PrefetchScalarGridSpec(
            num_scalar_prefetch=1, grid=(h,),
            in_specs=[pl.BlockSpec((None, slots, n), lambda i, at: (i, 0, 0))],
            out_specs=pl.BlockSpec((None, mem, n), lambda i, at: (i, 0, 0))),
        out_shape=jax.ShapeDtypeStruct((h, mem, n), bf16),
        cost_estimate=pl.CostEstimate(flops=2 * h * n * slots * mem, bytes_accessed=h * n * mem * 2, transcendentals=0),
    )(at, picked)


def prep_kernel(at_ref, reset_ref, wq_ref, up_ref, dn_ref, wo_ref, mk_ref, mv_ref, *refs):
    vectors, (qo_ref, qs_ref, ro_ref, rs_ref, d1_ref) = refs[:-5], refs[-5:]
    r = wq_ref.shape[0]
    m = mk_ref.shape[0]
    c, x = at_ref[2], at_ref[3]
    width = wq_ref.shape[1] // 3
    lane = 128
    at = lambda col: pl.ds(pl.multiple_of(col, lane), lane)
    lanes = lambda k: slice(k * lane, (k + 1) * lane)
    for qd, rd, cc in ((qo_ref, ro_ref, c), (qs_ref, rs_ref, 1 - c)):
        for ab in range(2):
            for part in range(3):
                qd[ab * r : (ab + 1) * r, lanes(part)] = wq_ref[:, at(part * width + (4 * cc + 2 * x + ab) * lane)]
            for half in range(2):
                for yy in range(2):
                    col = ((2 * (2 * x + ab) + yy) * 2 + cc) * 2 * lane + half * lane
                    row = (half * 2 + ab) * r
                    rd[row : row + r, lanes(yy)] = up_ref[:, at(col)]
            rd[4 * r : 5 * r, lanes(ab)] = wo_ref[:, at((4 * cc + 2 * x + ab) * lane)]
        for kv, src in enumerate((mk_ref, mv_ref)):
            for h in range(4):
                row = 5 * r + (kv * 2 + h // 2) * m
                rd[row : row + m, lanes(h % 2)] = src[:, at((4 * cc + h) * lane)]
        qd[2 * r :, :] = jnp.zeros((8, 3 * lane), bf16)
        for k, v in enumerate(vectors):
            qd[2 * r + k : 2 * r + k + 1, : v.shape[1]] = v[...]
        qd[2 * r + 7 : 2 * r + 8, :lane] = jnp.broadcast_to(reset_ref[0, 0].astype(f32), (1, lane)).astype(bf16)
    for ab in range(2):
        for half in range(2):
            for yy in range(2):
                d1_ref[half, ab, :, lanes(yy)] = dn_ref[half * lane : (half + 1) * lane, at((2 * x + ab) * 2 * lane + yy * lane)]


def prepare(at, resets, wq, up, dn, wo, mk, mv, vectors):
    r, m = wq.shape[0], mk.shape[0]
    s = lambda *d: jax.ShapeDtypeStruct(d, bf16)
    return pl.pallas_call(
        prep_kernel,
        in_specs=[pl.BlockSpec(memory_space=pltpu.SMEM)] * 2 + [pl.BlockSpec(memory_space=pltpu.VMEM)] * (6 + len(vectors)),
        out_shape=[s(2 * r + 8, 384), s(2 * r + 8, 384), s(5 * r + 4 * m, 256), s(5 * r + 4 * m, 256), s(2, 2, 128, 256)],
    )(at, resets, wq, up, dn, wo, mk, mv, *[v.reshape(1, -1) for v in vectors])


def pack_kernel(at_ref, own_ref, got_ref, d_ref, f1_ref, f2_ref, *, m):
    c = at_ref[2]
    lane = 128

    def fill(r0, r1):
        for ab in range(2):
            a = 448 * ab
            f1_ref[a : a + 64, :] = r0[64 * ab : 64 * ab + 64, :]
            f1_ref[a + 64 : a + 128, :] = r1[64 * ab : 64 * ab + 64, :]
            f1_ref[a + 128 : a + 256, :] = d_ref[0, ab]
            f1_ref[a + 256 : a + 320, :lane] = r0[256:320, lane * ab : lane * ab + lane]
            f1_ref[a + 256 : a + 320, lane:] = r1[256:320, lane * ab : lane * ab + lane]
            b = 256 * ab
            f2_ref[b : b + 64, :] = r0[128 + 64 * ab : 192 + 64 * ab, :]
            f2_ref[b + 64 : b + 128, :] = r1[128 + 64 * ab : 192 + 64 * ab, :]
            f2_ref[b + 128 : b + 256, :] = d_ref[1, ab]
        for k in range(4):
            at = 320 + 2 * k * m
            f1_ref[at : at + m, :] = r0[320 + k * m : 320 + (k + 1) * m, :]
            f1_ref[at + m : at + 2 * m, :] = r1[320 + k * m : 320 + (k + 1) * m, :]

    @pl.when(c == 0)
    def _():
        fill(own_ref, got_ref)

    @pl.when(c == 1)
    def _():
        fill(got_ref, own_ref)


def pack_ffn(at, own, got, d, m):
    s = lambda *e: jax.ShapeDtypeStruct(e, bf16)
    return pl.pallas_call(
        functools.partial(pack_kernel, m=m),
        in_specs=[pl.BlockSpec(memory_space=pltpu.SMEM)] + [pl.BlockSpec(memory_space=pltpu.VMEM)] * 3,
        out_shape=[s(768, 256), s(512, 256)],
    )(at, own, got, d)


def piece_places(at_ref):
    z, y, x = at_ref[0], at_ref[1], at_ref[3]
    for kind in range(4):
        for i in range(2):
            for k in range(4):
                yy = (y ^ i) if kind < 2 else (y if kind == 2 else 1 - y)
                xx = (x if kind == 0 else 1 - x) if kind < 2 else (x ^ i)
                yield kind * 2 + i, k, (z ^ k) * 2 + yy, 2 * xx + kind // 2


def qkv_kernel(at_ref, tp_ref, own_ref, oth_ref, gain_ref, shift_ref, p0, p1, p2, p3, p4, p5, p6, p7,
               q_ref, k_ref, v_ref, rq_ref, rk_ref, xn_hbm, w_hbm, x_ref, w_ref, sem, osem):
    i = pl.program_id(0)
    seg = tp_ref.shape[0]
    dh = 128
    half = w_ref.shape[1] // 3
    outs = [pltpu.make_async_copy(x_ref, xn_hbm, osem.at[0]), pltpu.make_async_copy(w_ref, w_hbm, osem.at[1])]

    @pl.when(i == 0)
    def _():
        copies = []
        pieces = (p0, p1, p2, p3, p4, p5, p6, p7)
        for kind, slot, chip, quarter in piece_places(at_ref):
            for part in range(3):
                dst = w_ref.at[pl.ds(pl.multiple_of(chip * 128, 128), 128), pl.ds(pl.multiple_of(part * half + quarter * dh, dh), dh)]
                copies.append(pltpu.make_async_copy(pieces[kind].at[slot, pl.ds(0, 128), pl.ds(part * dh, dh)], dst, sem))
        for copy in copies:
            copy.start()
        gain = gain_ref[...].astype(f32)
        shift = shift_ref[...].astype(f32)
        for s, src in enumerate((tp_ref, own_ref, oth_ref)):
            first = 0 if s == 0 else seg * (1 + at_ref[2]) if s == 1 else seg * (2 - at_ref[2])
            for r0 in range(0, seg, 128):
                n, r = norm_stats(src[r0 : r0 + 128, :].astype(f32))
                x_ref[pl.ds(pl.multiple_of(first + r0, 128), 128), :] = (n * gain + shift).astype(bf16)
        for copy in copies:
            copy.wait()
        for copy in outs:
            copy.start()

    def unit(y, out_ref, r_ref):
        for k in range(2):
            part = y[:, k * dh : (k + 1) * dh]
            r = lax.rsqrt(jnp.sum(part * part, axis=1, keepdims=True) + 1e-06)
            out_ref[:, k * dh : (k + 1) * dh] = (part * r).astype(bf16)
            r_ref[k] = r

    w = w_ref[:, pl.ds(pl.multiple_of(i * 256, 256), 256)]

    @pl.when(i < 2)
    def _():
        unit(nn(x_ref[seg:, :], w), q_ref, rq_ref)

    @pl.when((i >= 2) & (i < 4))
    def _():
        unit(nn(x_ref[...], w), k_ref, rk_ref)

    @pl.when(i >= 4)
    def _():
        v_ref[...] = nn(x_ref[...], w).astype(bf16)

    @pl.when(i == 5)
    def _():
        for copy in outs:
            copy.wait()


def project_pair(at, tp, own, oth, gain, shift, pieces):
    seg, width = tp.shape
    half = width // 2
    once = dict(pipeline_mode=pl.Buffered(1))
    whole = pl.BlockSpec((seg, width), lambda i, *_: (0, 0), **once)
    vec = pl.BlockSpec((1, width), lambda i, *_: (0, 0))
    hbm = pl.BlockSpec(memory_space=pltpu.HBM)
    col = lambda n, s: pl.BlockSpec((n * seg, 256), lambda i, *_: (0, jnp.clip(i - s, 0, 1)))
    rs = lambda n, s: pl.BlockSpec((2, n * seg, 1), lambda i, *_: (jnp.clip(i - s, 0, 1), 0, 0))
    sd = jax.ShapeDtypeStruct
    return pl.pallas_call(
        qkv_kernel,
        grid_spec=pltpu.PrefetchScalarGridSpec(
            num_scalar_prefetch=1, grid=(6,),
            in_specs=[whole, whole, whole, vec, vec] + [hbm] * 8,
            out_specs=[col(2, 0), col(3, 2), col(3, 4), rs(2, 0), rs(3, 2), hbm, hbm],
            scratch_shapes=[pltpu.VMEM((3 * seg, width), bf16), pltpu.VMEM((width, 3 * half), bf16), pltpu.SemaphoreType.DMA, pltpu.SemaphoreType.DMA((2,))]),
        out_shape=[sd((2 * seg, half), bf16), sd((3 * seg, half), bf16), sd((3 * seg, half), bf16), sd((4, 2 * seg, 1), f32), sd((4, 3 * seg, 1), f32),
                   sd((3 * seg, width), bf16), sd((width, 3 * half), bf16)],
        compiler_params=pltpu.CompilerParams(vmem_limit_bytes=48 << 20),
        cost_estimate=pl.CostEstimate(flops=2 * seg * width * half * 8, bytes_accessed=20 << 20, transcendentals=0),
    )(at, tp, own, oth, gain, shift, *pieces)


def attn_fwd_kernel(gate_ref, reset_ref, at_ref, q_ref, k_ref, v_ref, base_ref, mk0_ref, mk1_ref, mv0_ref, mv1_ref, mask0_ref, mask1_ref, mix_ref, loc_ref, rem_ref, t_ref):
    seg = q_ref.shape[0] // 2
    s = gate_ref[pl.program_id(0)]
    t_ref[...] = spread(base_ref[...], BLK)
    heat = 16.0 * LOG2E
    nb = seg // BLK
    mk = jnp.concatenate([mk0_ref[...].reshape(-1, 128), mk1_ref[...].reshape(-1, 128)]).astype(f32)
    mk = (mk * lax.rsqrt(jnp.sum(mk * mk, axis=1, keepdims=True) + 1e-06)).astype(bf16)
    mv = jnp.concatenate([mv0_ref[...].reshape(-1, 128), mv1_ref[...].reshape(-1, 128)])
    for u in range(2):
        keep = jnp.where(reset_ref[u] == 0, 1.0, 0.0).astype(f32)
        kp = k_ref[u * seg : (u + 1) * seg, :]
        vp = v_ref[u * seg : (u + 1) * seg, :] * keep.astype(bf16)
        for i in range(nb):
            rows = slice(u * seg + i * BLK, u * seg + (i + 1) * BLK)
            q = q_ref[rows, :]
            off = (nb - 1 - i) * BLK
            cw = (i + 1) * BLK
            kc = k_ref[(u + 1) * seg : (u + 1) * seg + cw, :]
            vc = v_ref[(u + 1) * seg : (u + 1) * seg + cw, :]
            ep = jnp.exp2(nt(q, kp) * heat + t_ref[:, off : off + seg])
            ec = jnp.exp2(nt(q, kc) * heat + t_ref[:, off + seg : off + seg + cw])
            il = 1.0 / (keep * jnp.sum(ep, axis=1, keepdims=True) + jnp.sum(ec, axis=1, keepdims=True))
            o = nn((ep * il).astype(bf16), vp) + nn((ec * il).astype(bf16), vc)
            em = jnp.exp2(nt(mk, q) * heat) * (mask0_ref, mask1_ref)[u][:, i * BLK : (i + 1) * BLK].astype(f32)
            em = em * (1.0 / jnp.sum(em, axis=0, keepdims=True))
            om = tn(em.astype(bf16), mv)
            loc_ref[rows, :] = o.astype(bf16)
            rem_ref[rows, :] = om.astype(bf16)
            mix_ref[rows, :] = (s * om + (1.0 - s) * o).astype(bf16)


def head_specs(seg, mem, wt, head=lambda h: h):
    dh = 128
    col = lambda n: pl.BlockSpec((n, dh), lambda h, *_: (0, head(h)))
    own = lambda k: pl.BlockSpec((4, mem // 8, dh), lambda h, *_: (0, 10 + 2 * k + head(h) // 2, head(h) % 2))
    return [col(2 * seg), col(3 * seg), col(3 * seg), pl.BlockSpec((None, 1, wt), lambda h, *_: (head(h), 0, 0)), own(0), own(0), own(1), own(1)] + [pl.BlockSpec((None, mem, seg), lambda h, *_: (head(h), 0, 0))] * 2


def attend(gate, reset, at, q, k, v, base, pack, masks):
    seg = q.shape[0] // 2
    mem, wt = masks[0].shape[1], base.shape[2]
    col = pl.BlockSpec((2 * seg, 128), lambda h, *_: (0, h))
    full = jax.ShapeDtypeStruct(q.shape, bf16)
    return pl.pallas_call(
        attn_fwd_kernel,
        grid_spec=pltpu.PrefetchScalarGridSpec(
            num_scalar_prefetch=3, grid=(4,), in_specs=head_specs(seg, mem, wt), out_specs=[col] * 3, scratch_shapes=[pltpu.VMEM((BLK, wt), f32)]),
        out_shape=[full] * 3,
        compiler_params=pltpu.CompilerParams(vmem_limit_bytes=48 << 20),
        cost_estimate=pl.CostEstimate(flops=8 * seg * (2 * seg + mem) * 4 * 128, bytes_accessed=20 << 20, transcendentals=8 * seg * (2 * seg + mem)),
    )(gate, reset, at, q, k, v, base, *pack, *pack, *masks)


def attn_bwd_kernel(gate_ref, reset_ref, at_ref, q_ref, k_ref, v_ref, base_ref, mk0_ref, mk1_ref, mv0_ref, mv1_ref, mask0_ref, mask1_ref, loc_ref, rem_ref, ol_ref, ox_ref, wo_ref, rq_ref, rk_ref,
                    dq_ref, dk_ref, dv_ref, diag_ref, dgate_ref, t_ref, g_ref, ak, av, gm_ref, *, part):
    seg = q_ref.shape[0] // 2
    s = gate_ref[2 * pl.program_id(0) + part]
    t_ref[...] = spread(base_ref[...], BLK)
    g_ref[...] = jnp.zeros_like(g_ref)
    ak[...] = jnp.zeros_like(ak)
    av[...] = jnp.zeros_like(av)
    wo = wo_ref[...]
    gm_ref[pl.ds(pl.multiple_of(at_ref[2] * seg, seg), seg), :] = nt(ol_ref[...], wo)
    gm_ref[pl.ds(pl.multiple_of((1 - at_ref[2]) * seg, seg), seg), :] = nt(ox_ref[...], wo)
    heat = 16.0 * LOG2E
    nb = seg // BLK
    mk = jnp.concatenate([mk0_ref[...].reshape(-1, 128), mk1_ref[...].reshape(-1, 128)]).astype(f32)
    mk = (mk * lax.rsqrt(jnp.sum(mk * mk, axis=1, keepdims=True) + 1e-06)).astype(bf16)
    mv = jnp.concatenate([mv0_ref[...].reshape(-1, 128), mv1_ref[...].reshape(-1, 128)])
    dg = jnp.zeros((BLK, 1), f32)
    for u in range(2):
        keep = jnp.where(reset_ref[u] == 0, 1.0, 0.0).astype(f32)
        old = slice(u * seg, (u + 1) * seg)
        kp = k_ref[old, :]
        vp = v_ref[old, :]
        for i in range(nb):
            rows = slice(u * seg + i * BLK, u * seg + (i + 1) * BLK)
            q = q_ref[rows, :]
            gm = gm_ref[rows, :]
            off = (nb - 1 - i) * BLK
            cw = (i + 1) * BLK
            cur = slice((u + 1) * seg, (u + 1) * seg + cw)
            kc = k_ref[cur, :]
            vc = v_ref[cur, :]
            al = jnp.sum(gm * loc_ref[rows, :].astype(f32), axis=1, keepdims=True)
            ar = jnp.sum(gm * rem_ref[rows, :].astype(f32), axis=1, keepdims=True)
            dg = dg + (ar - al)
            gl = ((1.0 - s) * gm).astype(bf16)
            gr = (s * gm).astype(bf16)
            ep = jnp.exp2(nt(q, kp) * heat + t_ref[:, off : off + seg])
            ec = jnp.exp2(nt(q, kc) * heat + t_ref[:, off + seg : off + seg + cw])
            l = keep * jnp.sum(ep, axis=1, keepdims=True) + jnp.sum(ec, axis=1, keepdims=True)
            il = 1.0 / l
            pp = ep * (il * keep)
            pc = ec * il
            wp = pp * nt(gl, vp)
            wc = pc * nt(gl, vc)
            dl = jnp.sum(wp, axis=1, keepdims=True) + jnp.sum(wc, axis=1, keepdims=True)
            dsp = (wp - pp * dl).astype(bf16)
            dsc = (wc - pc * dl).astype(bf16)
            g_ref[:, off : off + seg] += dsp.astype(f32)
            g_ref[:, off + seg : off + seg + cw] += dsc.astype(f32)
            dq = nn(dsp, kp) + nn(dsc, kc)
            ak[old, :] += tn(dsp, q)
            ak[cur, :] += tn(dsc, q)
            av[old, :] += tn(pp.astype(bf16), gl)
            av[cur, :] += tn(pc.astype(bf16), gl)
            em = jnp.exp2(nt(mk, q) * heat) * (mask0_ref, mask1_ref)[u][:, i * BLK : (i + 1) * BLK].astype(f32)
            em = em * (1.0 / jnp.sum(em, axis=0, keepdims=True))
            gw = nt(mv, gr)
            dsm = em * (gw - jnp.sum(em * gw, axis=0, keepdims=True))
            dq = dq + tn(dsm.astype(bf16), mk)
            dq_ref[rows, :] = unit_back(16.0 * dq, q, rq_ref[rows, :])
    dk_ref[...] = unit_back(16.0 * ak[...], k_ref[...], rk_ref[...])
    dv_ref[...] = av[...].astype(bf16)
    diag_ref[...] = gather_diagonals(g_ref[...])
    dgate_ref[...] = jnp.broadcast_to(jnp.sum(dg) * s * (1.0 - s), dgate_ref.shape)


def attend_back(part, gate, reset, at, q, k, v, base, pack, masks, loc, rem, ol, ox, wo, rq, rk):
    seg, half = q.shape[0] // 2, q.shape[1]
    mem, wt = masks[0].shape[1], base.shape[2]
    width = ol.shape[1]
    col = lambda n: pl.BlockSpec((n * seg, 128), lambda h, *_: (0, h))
    head = lambda h: 2 * h + part
    col_in = lambda n: pl.BlockSpec((n * seg, 128), lambda h, *_: (0, head(h)))
    row = lambda w: pl.BlockSpec((None, 1, w), lambda h, *_: (h, 0, 0))
    rcol = lambda n: pl.BlockSpec((None, n * seg, 1), lambda h, *_: (head(h), 0, 0))
    sd = jax.ShapeDtypeStruct
    return pl.pallas_call(
        functools.partial(attn_bwd_kernel, part=part),
        grid_spec=pltpu.PrefetchScalarGridSpec(
            num_scalar_prefetch=3, grid=(2,),
            in_specs=head_specs(seg, mem, wt, head) + [col_in(2), col_in(2), pl.BlockSpec((seg, width), lambda h, *_: (0, 0), pipeline_mode=pl.Buffered(1)), pl.BlockSpec((seg, width), lambda h, *_: (0, 0), pipeline_mode=pl.Buffered(1)),
                      pl.BlockSpec((128, width), lambda h, g, r, at: (4 * at[2] + head(h), 0)), rcol(2), rcol(3)],
            out_specs=[col(2), col(3), col(3), row(wt), row(128)],
            scratch_shapes=[pltpu.VMEM((BLK, wt), f32)] * 2 + [pltpu.VMEM((3 * seg, 128), f32)] * 2 + [pltpu.VMEM((2 * seg, 128), f32)]),
        out_shape=[sd((2 * seg, half // 2), bf16), sd((3 * seg, half // 2), bf16), sd((3 * seg, half // 2), bf16), sd((2, 1, wt), f32), sd((2, 1, 128), f32)],
        compiler_params=pltpu.CompilerParams(vmem_limit_bytes=48 << 20),
        cost_estimate=pl.CostEstimate(flops=8 * seg * (2 * seg + mem) * 10 * 128, bytes_accessed=30 << 20, transcendentals=8 * seg * (2 * seg + mem)),
    )(gate, reset, at, q, k, v, base, *pack, *pack, *masks, loc, rem, ol, ox, wo, rq, rk)


def ffn_kernel(at_ref, *refs, first):
    refs = list(refs)
    if first:
        ao_ref, ax_ref, tok_ref, tokx_ref, gain_ref, shift_ref, other_ref = refs[:7]
        refs = refs[7:]
    else:
        lo_ref, oi_ref, gi_ref = refs[:3]
        refs = refs[3:]
    cot_ref, cotx_ref, bu_ref = refs[:3]
    pieces = refs[3:11]
    refs = refs[11:]
    if first:
        lowo_ref, res_ref, o_ref, g_ref, wout_ref = refs[:5]
        refs = refs[5:]
    else:
        oo_ref, ox_ref, go_ref, gx_ref = refs[:4]
        refs = refs[4:]
    oa_ref, xa_ref, ob_ref, yb_ref, gbu_ref, up_s, dn_s, low_s, cot_s, act_s, gp_s, sem, osem, tmp = refs[:14]
    i = pl.program_id(0)
    rb, width = cot_ref.shape
    rows = pl.ds(pl.multiple_of(i * rb, rb), rb)
    q4 = 256
    copies = []
    for kind, slot, chip, quarter in piece_places(at_ref):
        where = (pl.ds(pl.multiple_of(chip * 128, 128), 128), pl.ds(pl.multiple_of(quarter * q4, q4), q4))
        for w, dst in enumerate((up_s, dn_s)):
            copies.append(pltpu.make_async_copy(pieces[kind].at[slot, pl.ds(w * 128, 128)], dst.at[where], sem))
    outs = []
    if first:
        wout_s = refs[14]
        c = at_ref[2]
        for whose, cc in ((0, c), (1, 1 - c)):
            for kind, slot, chip, quarter in piece_places(at_ref):
                for core in range(2):
                    src = pieces[kind].at[slot, pl.ds(256, 64), pl.ds(core * 128, 128)] if whose == 0 else other_ref.at[kind * 4 + slot, :, pl.ds(core * 128, 128)]
                    dst = wout_s.at[pl.ds(pl.multiple_of(chip * 128 + core * 64, 64), 64), pl.ds(pl.multiple_of((4 * cc + quarter) * 128, 128), 128)]
                    outs.append(pltpu.make_async_copy(src, dst, osem.at[0]))
        keep = pltpu.make_async_copy(wout_s, wout_ref, osem.at[1])

    @pl.when(i == 0)
    def _():
        for copy in outs + copies:
            copy.start()
        for copy in outs:
            copy.wait()
        if first:
            keep.start()

    if first:
        half_w = ao_ref.shape[1]
        wrow = lambda cc: wout_s[pl.ds(pl.multiple_of(cc * half_w, half_w), half_w), :]
        res = jnp.where(i < 2, tok_ref[...].astype(f32), tokx_ref[...].astype(f32)) + nn(ao_ref[...], wrow(c)) + nn(ax_ref[...], wrow(1 - c))
        n, r = norm_stats(res)
        low = (n * gain_ref[...].astype(f32) + shift_ref[...].astype(f32)).astype(bf16)
        lowo_ref[...] = low

        @pl.when(i < 2)
        def _():
            res_ref[...] = res
    else:
        low = lo_ref[...]
    low_s[rows, :] = low
    cot = jnp.where(i < 2, cot_ref[...].astype(f32), cotx_ref[...].astype(f32)).astype(bf16)
    cot_s[rows, :] = cot

    @pl.when(i == 0)
    def _():
        for copy in copies:
            copy.wait()

    p = nn(low, up_s[...]) + bu_ref[...].astype(f32)
    ga = nt(cot, dn_s[...])
    k0 = math.sqrt(2.0 / math.pi)
    p2_ = p * p
    t = jnp.tanh(p * (k0 + (k0 * 0.044715) * p2_))
    half = 0.5 * (1.0 + t)
    act = (p * half).astype(bf16)
    slope = half + 0.5 * p * (1.0 - t * t) * (k0 + (3.0 * k0 * 0.044715) * p2_)
    gp = (ga * slope).astype(bf16)
    act_s[rows, :] = act
    gp_s[rows, :] = gp
    o = nn(act, dn_s[...])
    g = nt(gp, up_s[...])
    if first:
        o_ref[...] = o
        g_ref[...] = g
    else:
        o = o + oi_ref[...]
        g = g + gi_ref[...]

        @pl.when(i < 2)
        def _():
            oo_ref[...] = o
            go_ref[...] = g

        @pl.when(i >= 2)
        def _():
            ox_ref[...] = o.astype(bf16)
            gx_ref[...] = g.astype(bf16)

    @pl.when(i == pl.num_programs(0) - 1)
    def _():
        z, y, x = at_ref[0], at_ref[1], at_ref[3]
        for part in range(2):
            for xr in range(2):
                cols = pl.ds(pl.multiple_of((2 * (x ^ xr) + part) * q4, q4), q4)
                for w, (left, right) in enumerate(((low_s, gp_s), (act_s, cot_s))):
                    tmp[w] = tn(left[...], right[:, cols]).astype(bf16)
                    for yr in range(2):
                        dst = ((oa_ref, xa_ref)[xr], yr) if part == 0 else ((ob_ref, yb_ref)[yr], xr)
                        for k in range(4):
                            chip = (z ^ k) * 2 + (y ^ yr)
                            dst[0][dst[1], w, k] = tmp[w, pl.ds(pl.multiple_of(chip * 128, 128), 128), :]
        if first:
            keep.wait()
        gbu_ref[...] = jnp.broadcast_to(jnp.sum(gp_s[...].astype(f32), axis=0, keepdims=True), gbu_ref.shape)


def ffn_half(at, first, ins, cot, cotx, bu, pieces):
    seg, width = cot.shape
    pair = 2 * seg
    rb = 256
    once = dict(pipeline_mode=pl.Buffered(1))
    there = lambda w: pl.BlockSpec((rb, w), lambda i, at: ((i + 2 * at[2]) % 4, 0))
    here = lambda w: pl.BlockSpec((rb, w), lambda i, at: (i, 0))
    own = pl.BlockSpec((rb, width), lambda i, at: (jnp.minimum(i, 1), 0))
    other = pl.BlockSpec((rb, width), lambda i, at: (jnp.maximum(i - 2, 0), 0))
    vec = pl.BlockSpec((1, width), lambda i, at: (0, 0))
    hbm = pl.BlockSpec(memory_space=pltpu.HBM)
    sd = jax.ShapeDtypeStruct
    half = width // 2
    if first:
        in_specs = [there(half), there(half), own, other, vec, vec, hbm]
        out_specs = [here(width), own, here(width), here(width), hbm]
        out_shape = [sd((pair, width), bf16), sd((seg, width), f32), sd((pair, width), f32), sd((pair, width), f32), sd((width, width), bf16)]
    else:
        in_specs = [here(width)] * 3
        out_specs = [own, other, own, other]
        out_shape = [sd((seg, width), f32), sd((seg, width), bf16), sd((seg, width), f32), sd((seg, width), bf16)]
    ff = bu.shape[1]
    grads = pl.BlockSpec((2, 2, 4, 128, 256), lambda i, at: (0, 0, 0, 0, 0), **once)
    return pl.pallas_call(
        functools.partial(ffn_kernel, first=first),
        grid_spec=pltpu.PrefetchScalarGridSpec(
            num_scalar_prefetch=1, grid=(4,),
            in_specs=in_specs + [own, other, vec] + [hbm] * 8,
            out_specs=out_specs + [grads] * 4 + [pl.BlockSpec((8, ff), lambda i, at: (0, 0))],
            scratch_shapes=[pltpu.VMEM((width, ff), bf16)] * 2 + [pltpu.VMEM((pair, width), bf16)] * 2 + [pltpu.VMEM((pair, ff), bf16)] * 2 + [pltpu.SemaphoreType.DMA, pltpu.SemaphoreType.DMA((2,)), pltpu.VMEM((2, width, 256), bf16)]
            + ([pltpu.VMEM((width, width), bf16)] if first else [])),
        out_shape=out_shape + [sd((2, 2, 4, 128, 256), bf16)] * 4 + [sd((8, ff), f32)],
        compiler_params=pltpu.CompilerParams(vmem_limit_bytes=56 << 20),
        cost_estimate=pl.CostEstimate(flops=2 * pair * width * ff * 6, bytes_accessed=30 << 20, transcendentals=pair * ff),
    )(at, *ins, cot, cotx, bu, *pieces)


def rows_kernel(*refs):
    pieces, out, buf, sem, osem = refs[:8], refs[8], refs[9], refs[10], refs[11]
    n = out.shape[1]
    copies = [pltpu.make_async_copy(v.at[:, pl.ds(256, n)], buf.at[pl.ds(4 * k, 4)], sem) for k, v in enumerate(pieces)]
    for copy in copies:
        copy.start()
    for copy in copies:
        copy.wait()
    done = pltpu.make_async_copy(buf, out, osem)
    done.start()
    done.wait()


def out_rows_of(pieces):
    n, cols = min(v.shape[1] for v in pieces) - 256, pieces[0].shape[2]
    hbm = pl.BlockSpec(memory_space=pltpu.HBM)
    return pl.pallas_call(
        rows_kernel,
        in_specs=[hbm] * 8,
        out_specs=hbm,
        out_shape=jax.ShapeDtypeStruct((32, n, cols), bf16),
        scratch_shapes=[pltpu.VMEM((32, n, cols), bf16), pltpu.SemaphoreType.DMA, pltpu.SemaphoreType.DMA],
        cost_estimate=pl.CostEstimate(flops=0, bytes_accessed=2 << 20, transcendentals=0),
    )(*pieces)


def join_kernel(res_ref, oo_ref, ox_ref, go_ref, gx_ref, cot_ref, gain_ref, bd_ref, out_ref, one_ref, ol_ref, vec_ref):
    res = res_ref[...]
    out_ref[...] = (res + oo_ref[...] + ox_ref[...].astype(f32) + bd_ref[...].astype(f32)).astype(bf16)
    gh = go_ref[...] + gx_ref[...].astype(f32)
    n, r = norm_stats(res)
    cf = cot_ref[...].astype(f32)
    one = cf + norm_back(gh, n, r, gain_ref[...].astype(f32))
    one_ref[...] = one
    ol_ref[...] = one.astype(bf16)

    @pl.when(pl.program_id(0) == 0)
    def _():
        vec_ref[...] = jnp.zeros_like(vec_ref)

    vec_ref[0:1, :] += jnp.sum(gh * n, axis=0, keepdims=True)
    vec_ref[1:2, :] += jnp.sum(gh, axis=0, keepdims=True)
    vec_ref[2:3, :] += jnp.sum(cf, axis=0, keepdims=True)


def join(res, oo, ox, go, gx, cot, gain, bd):
    seg, width = res.shape
    blk = pl.BlockSpec((128, width), lambda i: (i, 0))
    vec = pl.BlockSpec((1, width), lambda i: (0, 0))
    sd = jax.ShapeDtypeStruct
    return pl.pallas_call(
        join_kernel,
        grid=(seg // 128,),
        in_specs=[blk] * 6 + [vec, vec],
        out_specs=[blk, blk, blk, pl.BlockSpec((8, width), lambda i: (0, 0))],
        out_shape=[sd((seg, width), bf16), sd((seg, width), f32), sd((seg, width), bf16), sd((8, width), f32)],
        cost_estimate=pl.CostEstimate(flops=40 * seg * width, bytes_accessed=24 * seg * width, transcendentals=0),
    )(res, oo, ox, go, gx, cot, gain, bd)


def rows_by_head(refs):
    a, b = refs[0][...], refs[1][...]
    return jnp.concatenate([a[:, :128], b[:, :128], a[:, 128:], b[:, 128:]], axis=1)


def before_kernel(ka_ref, kb_ref, va_ref, vb_ref, wk_ref, wv_ref, o_ref):
    o_ref[...] = (nt(rows_by_head((ka_ref, kb_ref)), wk_ref[...]) + nt(rows_by_head((va_ref, vb_ref)), wv_ref[...])).astype(bf16)


def before_grad(dk, dv, w):
    seg, half = dk[0].shape[0] // 3, dk[0].shape[1] * 2
    width = w.shape[0]
    rb = 256
    d = pl.BlockSpec((rb, half // 2), lambda i: (i, 0))
    wb = lambda k: pl.BlockSpec((width, half), lambda i: (0, k))
    return pl.pallas_call(
        before_kernel,
        grid=(seg // rb,),
        in_specs=[d] * 4 + [wb(1), wb(2)],
        out_specs=pl.BlockSpec((rb, width), lambda i: (i, 0)),
        out_shape=jax.ShapeDtypeStruct((seg, width), bf16),
        cost_estimate=pl.CostEstimate(flops=4 * seg * half * width, bytes_accessed=4 << 20, transcendentals=0),
        compiler_params=pltpu.CompilerParams(vmem_limit_bytes=32 << 20),
    )(*dk, *dv, w, w)


def wgrad_kernel(at_ref, x_ref, dq_ref, dk_ref, dv_ref, att_ref, attx_ref, ol_ref, olx_ref, oa_ref, xa_ref, ob_ref, yb_ref, tmp, ol_s, *, pair):
    seg = dk_ref.shape[0] // 3
    z, y, c, x = at_ref[0], at_ref[1], at_ref[2], at_ref[3]
    for xr in range(2):
        cols = pl.ds(pl.multiple_of((x ^ xr) * 128, 128), 128)
        tmp[:, :128] = tn(x_ref[seg:, :], dq_ref[:, cols]).astype(bf16)
        tmp[:, 128:384] = tn(x_ref[...], jnp.concatenate([dk_ref[:, cols], dv_ref[:, cols]], axis=1)).astype(bf16)
        ocols = pl.ds(pl.multiple_of((4 * c + 2 * (x ^ xr) + pair) * 128, 128), 128)
        ol_s[pl.ds(pl.multiple_of(c * seg, seg), seg), :] = ol_ref[:, ocols]
        ol_s[pl.ds(pl.multiple_of((1 - c) * seg, seg), seg), :] = olx_ref[:, ocols]
        half = att_ref.shape[1]
        tmp[pl.ds(pl.multiple_of(c * half, half), half), 384:] = tn(att_ref[...], ol_s[...]).astype(bf16)
        tmp[pl.ds(pl.multiple_of((1 - c) * half, half), half), 384:] = tn(attx_ref[...], ol_s[...]).astype(bf16)
        for part in range(2):
            for yr in range(2):
                dst = ((oa_ref, xa_ref)[xr], yr) if part == 0 else ((ob_ref, yb_ref)[yr], xr)
                for k in range(4):
                    row = ((z ^ k) * 2 + (y ^ yr)) * 128 + part * 64
                    dst[0][dst[1], 0, k] = tmp[pl.ds(pl.multiple_of(row, 64), 64), :]


def qkv_wgrad(pair, at, x, dq, dk, dv, att, attx, ol, olx):
    n, width = x.shape
    vm = pl.BlockSpec(memory_space=pltpu.VMEM)
    return pl.pallas_call(
        functools.partial(wgrad_kernel, pair=pair),
        in_specs=[pl.BlockSpec(memory_space=pltpu.SMEM)] + [vm] * 8,
        out_specs=[vm] * 4,
        out_shape=[jax.ShapeDtypeStruct((2, 1, 4, 64, 512), bf16)] * 4,
        scratch_shapes=[pltpu.VMEM((width, 512), bf16), pltpu.VMEM((att.shape[0], 128), bf16)],
        compiler_params=pltpu.CompilerParams(vmem_limit_bytes=32 << 20),
        cost_estimate=pl.CostEstimate(flops=2 * n * width * 768, bytes_accessed=12 << 20, transcendentals=0),
    )(at, x, dq, dk, dv, att, attx, ol, olx)


def hgrad_kernel(at_ref, qa_ref, qb_ref, ka_ref, kb_ref, va_ref, vb_ref, wq_ref, wk_ref, wv_ref, back_ref, ho_ref, hx_ref):
    i = pl.program_id(0)
    c = at_ref[2]
    g = nt(rows_by_head((qa_ref, qb_ref)), wq_ref[...]) + nt(rows_by_head((ka_ref, kb_ref)), wk_ref[...]) + nt(rows_by_head((va_ref, vb_ref)), wv_ref[...])
    mine = jnp.where((i + 2 * c) % 4 == 2 + c, 1.0, 0.0).astype(f32)
    g = g + mine * back_ref[...].astype(f32)

    @pl.when(i < 2)
    def _():
        ho_ref[...] = g

    @pl.when(i >= 2)
    def _():
        hx_ref[...] = g.astype(bf16)


def hgrad(at, dq, dk, dv, w, back):
    pair, half = dq[0].shape[0], dq[0].shape[1] * 2
    seg, width = pair // 2, w.shape[0]
    rb = 256
    once = dict(pipeline_mode=pl.Buffered(1))
    wb = lambda k: pl.BlockSpec((width, half), lambda i, at: (0, k), **once)
    sd = jax.ShapeDtypeStruct
    return pl.pallas_call(
        hgrad_kernel,
        grid_spec=pltpu.PrefetchScalarGridSpec(
            num_scalar_prefetch=1, grid=(4,),
            in_specs=[pl.BlockSpec((rb, half // 2), lambda i, at: ((i + 2 * at[2]) % 4, 0))] * 2 + [pl.BlockSpec((rb, half // 2), lambda i, at: (2 + (i + 2 * at[2]) % 4, 0))] * 4
            + [wb(0), wb(1), wb(2), pl.BlockSpec((rb, width), lambda i, at: (0, 0))],
            out_specs=[pl.BlockSpec((rb, width), lambda i, at: (jnp.minimum(i, 1), 0)), pl.BlockSpec((rb, width), lambda i, at: (jnp.maximum(i - 2, 0), 0))]),
        out_shape=[sd((seg, width), f32), sd((seg, width), bf16)],
        compiler_params=pltpu.CompilerParams(vmem_limit_bytes=32 << 20),
        cost_estimate=pl.CostEstimate(flops=6 * pair * half * width, bytes_accessed=12 << 20, transcendentals=0),
    )(at, *dq, *dk, *dv, w, w, w, back)


def gather_z(own, steps):
    return [send_z(own, k) for k in steps]


def columns(got, cuts):
    return [jnp.stack([g[lo:hi] for g in got]) for lo, hi in cuts]


def scatter_one(g):
    return send_x(g[1]), send_y(g[3])


def two_blocks(g, one):
    return add_low(g[0][1], one[0][1]), add_low(g[2][1], one[1][1])


def scatter_two(blocks):
    return send_y(blocks[0]), send_x(blocks[1])


def scatter_total(g, one, two):
    total = lambda u, v, w: (u.astype(f32) + v.astype(f32) + w.astype(f32)).astype(bf16)
    a, b = total(g[0][0], one[0][0], two[0]), total(g[2][0], one[1][0], two[1])
    return [jnp.stack([a[:, k], b[:, k]]) for k in range(4)]


def scatter_z(v):
    return [send_z(v[k], k) for k in range(1, 4)]


def z_sum(v, got):
    total = v[0].astype(f32)
    for g in got:
        total = total + g.astype(f32)
    return total.astype(bf16)


def scatter_x(total, other):
    x = lax.axis_index("stream")
    return jnp.concatenate([jnp.where(x == 0, total, other), jnp.where(x == 0, other, total)])


def local_pair(
    tokens, resets, retrieved, memory_keys, memory_values, qkv_weight, out_weight, up_weight, up_bias,
    down_weight, down_bias, attn_gain, attn_shift, ffn_gain, ffn_shift, position_bias, memory_gate, cotangent,
):
    heads = memory_gate.shape[0]
    seg, width = tokens.shape[1:]
    dh = width // heads
    shards = lax.axis_size("fsdp")
    chips = shards // 2
    mem_rows = memory_keys.shape[1]
    mem = mem_rows * shards
    nz, z, y, c, x = places()
    at = jnp.stack([z, y, c, x]).astype(jnp.int32)
    low_core = c == 0
    both = lambda own, other: (jnp.where(low_core, own, other), jnp.where(low_core, other, own))
    tok, cot = tokens[0], cotangent[0]
    part = width // shards
    vectors = [up_bias, down_bias, attn_gain, attn_shift, ffn_gain, ffn_shift, position_bias]
    sizes = [v.shape[0] for v in vectors]
    tok_other, cot_other = send_core(tok), send_core(cot)
    ret = jnp.transpose(retrieved[0], (1, 2, 0)).reshape(2, 4, retrieved.shape[3], seg)
    p0, p1 = both(take(ret, c, 0), send_core(take(ret, 1 - c, 0)))
    q_own, q_swap, r_own, r_swap, d_own = prepare(
        at, resets, qkv_weight, up_weight, down_weight, out_weight, memory_keys[0], memory_values[0], vectors)
    q_got, r_got = send_core(q_swap), send_core(r_swap)
    hot, rel = bucket_hot(seg)
    gate = lax.dynamic_slice_in_dim(jax.nn.sigmoid(memory_gate.astype(f32)), 4 * c, 4, 0)
    q0, q1 = both(q_own, q_got)
    own_qkv = jnp.concatenate([q0[:64], q1[:64], q0[128:], q1[128:], q0[64:128], q1[64:128]])
    reset = jnp.stack([q0[135, 0], q1[135, 0]]).astype(jnp.int32)
    second = jnp.where(low_core, tok_other, tok)
    own_qkv, r_got, tok, tok_other, cot_other, p0, p1 = fence(own_qkv, r_got, tok, tok_other, cot_other, p0, p1)
    g0 = [own_qkv] + gather_z(own_qkv, (1, 2, 3))
    ty = lax.ppermute(tok, "fsdp", [(i, i ^ 2) for i in range(1, shards, 2)])
    masks = (hit_masks(at, p0, mem), hit_masks(at, p1, mem))
    own_f1, own_f2 = pack_ffn(at, r_own, r_got, d_own, mem_rows)
    g0, masks, own_f1, own_f2, ty = fence(g0, masks, own_f1, own_f2, ty)
    a, b = columns(g0, ((0, 144), (144, 272)))
    a, b, own_f1 = fence(a, b, own_f1)
    ya, xb, xa, yb = send_y(a), send_x(b), send_x(a), send_y(b)
    z2 = send_z(own_f1, 2)
    a, ya, xb, b, xa, yb, z2, own_f1, ty = fence(a, ya, xb, b, xa, yb, z2, own_f1, ty)
    g0 = [a, ya, xa, send_x(ya), b, xb, yb, send_y(xb)]
    f1 = [own_f1, send_z(own_f1, 1), z2, send_z(own_f1, 3)]
    tz = lax.ppermute(ty, "fsdp", [(i, i + 4) for i in range(1, shards - 4, 4)])
    small = jnp.stack([a[:, 128:, :256], ya[:, 128:, :256]]).reshape(2, 2, 2, 16, 256)
    for axis, bit in enumerate((y, z // 2, z % 2)):
        small = jnp.where(bit == 1, jnp.flip(small, axis), small)
    small = jnp.transpose(small.reshape(2, 4, 16, 256), (1, 0, 2, 3)).reshape(shards, 8, 256)
    cols = [small[:, k, :s] for k, s in enumerate(sizes)]
    b_down, gain_one, shift_one, gain_two, shift_two = [v.reshape(1, -1) for v in cols[1:6]]
    b_up = take(cols[0].reshape(chips, 2, 2, 128), c, 1)
    b_up = [b_up[:, k].reshape(1, -1) for k in range(2)]
    table = lax.dynamic_slice_in_dim(cols[6].reshape(heads, -1).astype(f32), 4 * c, 4, 0)
    base = diagonal_bias(table, hot, rel)
    g0, ty, tz, f1, own_f2, base, b_up, gain_one, shift_one, b_down, gain_two, shift_two = fence(
        g0, ty, tz, f1, own_f2, base, b_up, gain_one, shift_one, b_down, gain_two, shift_two)
    tp = jnp.where(y == 0, tz, ty)
    tp = jnp.where(low_core, lax.ppermute(tp, "fsdp", [(i, i - 1) for i in range(1, shards, 2)]), tp)
    a, b = columns(f1, ((0, 448), (448, 768)))
    a, b, tp = fence(a, b, tp)
    ya, xb = send_y(a), send_x(b)
    f2 = [own_f2] + gather_z(own_f2, (1, 2))
    q, k, v, rq, rk, xn, w_qkv = project_pair(at, tp, tok, tok_other, gain_one, shift_one, g0)
    q, k, v, a, b, ya, xb, f2 = fence(q, k, v, a, b, ya, xb, f2)
    pack = (a, ya)
    xa, xra, q = fence(a[:, :320], ya[:, :320], q)
    f1 = [a, ya, send_x(xa), send_x(xra), b, xb, send_y(b), send_y(xb)]
    f2 = f2 + gather_z(f2[0], (3,))
    att, loc, rem = attend(gate, reset, at, q, k, v, base, pack, masks)
    att, f1, f2 = fence(att, f1, f2)
    att_other = send_core(att)
    out_other = out_rows_of(f1)
    a, b = columns(f2, ((0, 256), (256, 512)))
    att_other, out_other, a, b = fence(att_other, out_other, a, b)
    out_other = send_core(out_other)
    ya, xb = send_y(a), send_x(b)
    att_other, out_other, f1, a, b, ya, xb = fence(att_other, out_other, f1, a, b, ya, xb)
    f2 = [a, ya, send_x(a), send_x(ya), b, xb, send_y(b), send_y(xb)]
    low, res, o1, h1, w_out, *n1, gbu1 = ffn_half(at, True, (att, att_other, tok, tok_other, gain_two, shift_two, out_other), cot, cot_other, b_up[0], f1)
    low, o1, h1, n1, f2 = fence(low, o1, h1, n1, f2)
    s1 = scatter_one(n1)
    oo, ox, go, gx, *n2, gbu2 = ffn_half(at, False, (low, o1, h1), cot, cot_other, b_up[1], f2)
    gx, ox, s1, n2, oo, go = fence(gx, ox, s1, n2, oo, go)
    gx, ox, w1 = send_core(gx), send_core(ox), two_blocks(n1, s1)
    gx, ox, w1 = fence(gx, ox, w1)
    u1 = scatter_two(w1)
    output, one, ol, vec_two = join(res, oo, ox, go, gx, cot, gain_two, b_down)
    ol, u1 = fence(ol, u1)
    ol_other = send_core(ol)
    v1 = scatter_total(n1, s1, u1)
    ol_other, ol, v1, n2 = fence(ol_other, ol, v1, n2)
    s2 = scatter_one(n2)
    z1 = scatter_z(v1)
    dqa, dka, dva, diag_a, dgate_a = attend_back(0, gate, reset, at, q, k, v, base, pack, masks, loc, rem, ol, ol_other, w_out, rq, rk)
    dqa, dka, dva, s2, z1, ol, diag_a, dgate_a = fence(dqa, dka, dva, s2, z1, ol, diag_a, dgate_a)
    w2, dqa, ol = fence(two_blocks(n2, s2), dqa, ol)
    u2 = scatter_two(w2)
    na = qkv_wgrad(0, at, xn, dqa, dka, dva, att, att_other, ol, ol_other)
    na, u2, ol = fence(na, u2, ol)
    v2, t1, ol = fence(scatter_total(n2, s2, u2), z_sum(v1, z1), ol)
    sa = scatter_one(na)
    z2 = scatter_z(v2)
    dqb, dkb, dvb, diag_b, dgate_b = attend_back(1, gate, reset, at, q, k, v, base, pack, masks, loc, rem, ol, ol_other, w_out, rq, rk)
    dqb, dkb, dvb, sa, z2, diag_b, dgate_b = fence(dqb, dkb, dvb, sa, z2, diag_b, dgate_b)
    wa, dkb, t1 = fence(two_blocks(na, sa), dkb, t1)
    ua = scatter_two(wa)
    x1 = send_x(t1)
    nb = qkv_wgrad(1, at, xn, dqb, dkb, dvb, att, att_other, ol, ol_other)
    back = before_grad((dka, dkb), (dva, dvb), w_qkv).reshape(2, seg // 2, width)
    nb, back, ua, x1, z2 = fence(nb, back, ua, x1, z2)
    va, back_out, nb = fence(scatter_total(na, sa, ua), take(back, 1 - c, 0), nb)
    back_got = send_core(back_out)
    sb = scatter_one(nb)
    za = scatter_z(va)
    t2 = z_sum(v2, z2)
    sb, back_got, t2, za = fence(sb, back_got, t2, za)
    wb, back, t2 = fence(two_blocks(nb, sb), add_low(take(back, c, 0), back_got), t2)
    ub = scatter_two(wb)
    back = lax.ppermute(back, "fsdp", [(i, i - 2) for i in range(2, shards)])
    ub, back, t2 = fence(ub, back, t2)
    vb, back, t2 = fence(scatter_total(nb, sb, ub), back, t2)
    zb = scatter_z(vb)
    x2 = send_x(t2)
    ho, hx = hgrad(at, (dqa, dqb), (dka, dkb), (dva, dvb), w_qkv, back)
    zb, x2, hx, ho, diag_a, diag_b, dgate_a, dgate_b, gbu1, gbu2, vec_two = fence(zb, x2, hx, ho, diag_a, diag_b, dgate_a, dgate_b, gbu1, gbu2, vec_two)
    t_ab = jnp.concatenate([z_sum(va, za), z_sum(vb, zb)], axis=1)
    t_ab, hx = fence(t_ab, hx)
    x_ab = send_x(t_ab)
    token_grad, vec_one = finish(ho, send_core(hx), tok, one, gain_one)
    t_f1, t_f2 = scatter_x(t1, x1), scatter_x(t2, x2)
    by_head = lambda a, b: jnp.stack([a, b], axis=1).reshape((4,) + a.shape[1:])
    diag, dgate = by_head(diag_a, diag_b), by_head(dgate_a, dgate_b)
    mine_core = jnp.arange(2) == c
    gbu = jnp.stack([gbu1[0].reshape(chips, 128), gbu2[0].reshape(chips, 128)], axis=1)
    gbu = jnp.where(mine_core[None, :, None, None], gbu[:, None], 0.0).reshape(shards, -1)
    table_g = jnp.dot(diag[:, 0], hot.T, precision=lax.Precision.HIGHEST)
    table_g = jnp.where(mine_core[:, None, None], table_g[None], 0.0).reshape(shards, -1)
    gate_g = jnp.where(mine_core[:, None], dgate[:, 0, 0][None], 0.0).reshape(1, heads)
    up_sum = jnp.stack([t_f1[:, 0], t_f2[:, 0]]).reshape(2, 4, 2, 64, 256)
    up_got = send_core(take(up_sum, 1 - c, 2))
    x_ab, vec_one, up_got = fence(x_ab, vec_one, up_got)
    t_qkv = jnp.transpose(scatter_x(t_ab, x_ab).reshape(2, 2, 2, 64, 512), (0, 2, 1, 3, 4))
    qkv_sum = t_qkv.reshape(4, 2, 64, 512)
    qkv_got = send_core(take(qkv_sum, 1 - c, 1))
    pack = [gbu] + [v.reshape(shards, -1) for v in (vec_two[2], vec_one[0], vec_one[1], vec_two[0], vec_two[1])] + [table_g, jnp.broadcast_to(gate_g, (shards, heads))]
    total = jnp.concatenate(pack, axis=1)
    total = total + send_core(total)
    diagonal = lax.ppermute(total, ("stream", "fsdp"), [(s * shards + i, (1 - s) * shards + (i ^ 2)) for s in range(2) for i in range(shards)])
    total = (total + send_y(total)) + (send_x(total) + diagonal)
    total = (total + send_z(total, 1)) + (send_z(total, 2) + send_z(total, 3))
    total = take(total, lax.axis_index("fsdp"), 0)
    up_all = jnp.stack(both(take(up_sum, c, 2), up_got)).astype(f32)
    up_t = jnp.concatenate([up_all[cc, hf, q_, :, yy * 128 : (yy + 1) * 128] for q_ in range(4) for yy in range(2) for cc in range(2) for hf in range(2)], axis=1)
    down_t = jnp.concatenate([jnp.concatenate([t[q_, 1] for q_ in range(4)], axis=1) for t in (t_f1, t_f2)], axis=0).astype(f32)
    qkv_all = jnp.stack(both(take(qkv_sum, c, 1), qkv_got)).astype(f32)
    qkv_t = jnp.concatenate([qkv_all[cc, h, :, p * dh : (p + 1) * dh] for p in range(3) for cc in range(2) for h in range(4)], axis=1)
    out_t = jnp.concatenate([qkv_all[cc, h, :, 3 * dh :] for cc in range(2) for h in range(4)], axis=1)
    outs, off = [], 0
    for s in sizes + [heads]:
        outs.append(total[off : off + s])
        off += s
    ub, db, ag, ash, fg, fs, pg, gg = outs
    return output[None], token_grad[None], qkv_t, out_t, up_t, ub, down_t, db, ag, ash, fg, fs, pg, gg


def solution(mesh):
    row = P("stream", "fsdp", None)
    return jax.shard_map(
        local_pair if mesh.shape["fsdp"] == 16 else local_wide,
        mesh=mesh,
        in_specs=(
            row, P("stream", "fsdp"), P("stream", "fsdp", None, None), row, row, P("fsdp", None), P("fsdp", None),
            P("fsdp", None), P("fsdp"), P("fsdp", None), P("fsdp"), P("fsdp"), P("fsdp"), P("fsdp"), P("fsdp"),
            P("fsdp"), P(), row,
        ),
        out_specs=(
            row, row, P("fsdp", None), P("fsdp", None), P("fsdp", None), P("fsdp"), P("fsdp", None), P("fsdp"),
            P("fsdp"), P("fsdp"), P("fsdp"), P("fsdp"), P("fsdp"), P(),
        ),
        check_vma=False,
    )
```

```python
import functools
import math
import jax, jax.numpy as jnp
from jax import lax
from jax.experimental import pallas as pl
from jax.experimental.pallas import tpu as pltpu
f32=jnp.float32; bf16=jnp.bfloat16
LOG2E=math.log2(math.e)
NEG=-1e30

def nt(a,b): return lax.dot_general(a,b,(((1,),(1,)),((),())),preferred_element_type=f32)
def nn(a,b): return lax.dot_general(a,b,(((1,),(0,)),((),())),preferred_element_type=f32)
def tn(a,b): return lax.dot_general(a,b,(((0,),(0,)),((),())),preferred_element_type=f32)

from jax.experimental.layout import Layout, with_layout_constraint
from jax.sharding import PartitionSpec as P


def xor_perm(bit, n):
    return [(i, i ^ bit) for i in range(n)]


def places():
    n = lax.axis_size("fsdp")
    i = lax.axis_index("fsdp")
    return n // 4, i // 4, (i // 2) % 2, i % 2, lax.axis_index("stream")


def send_core(v):
    return lax.ppermute(v, "fsdp", xor_perm(1, lax.axis_size("fsdp")))


def send_y(v):
    return lax.ppermute(v, "fsdp", xor_perm(2, lax.axis_size("fsdp")))


def send_z(v, k):
    return lax.ppermute(v, "fsdp", xor_perm(4 * k, lax.axis_size("fsdp")))


def send_x(v):
    return lax.ppermute(v, "stream", [(0, 1), (1, 0)])


def gather_small(memory_keys, memory_values, vectors, heads):
    mem_rows, width = memory_keys.shape[1:]
    keys = memory_keys[0].astype(f32).reshape(mem_rows, heads, width // heads)
    keys = keys * lax.rsqrt(jnp.sum(keys * keys, axis=-1, keepdims=True) + 1e-06)
    small = jnp.concatenate(vectors)
    small = jnp.pad(small[None], ((0, 15), (0, width - small.shape[0])))
    pack = jnp.concatenate([keys.reshape(mem_rows, width).astype(bf16), memory_values[0], small], axis=0)
    pack = lax.all_gather(pack, "fsdp", axis=0)
    return pack[:, 2 * mem_rows], pack[:, :mem_rows].reshape(-1, width), pack[:, mem_rows : 2 * mem_rows].reshape(-1, width)


def scatter_weights(gs):
    whole = [jnp.concatenate([g[q] for q in range(4)], axis=1) for g in gs]
    got = [lax.psum_scatter(g, "fsdp", scatter_dimension=0, tiled=True) for g in whole]
    return [g.astype(f32) for g in lax.psum(got, "stream")]


def summed_everywhere(v):
    bit = 1
    while bit < lax.axis_size("fsdp"):
        v = v + lax.ppermute(v, "fsdp", xor_perm(bit, lax.axis_size("fsdp")))
        bit *= 2
    return v + send_x(v)


def passed_along(block, axis, distance):
    devices = range(lax.axis_size(axis))
    return lax.ppermute(block, axis, [(i - distance, i) for i in devices if i - distance in devices])


def norm_stats(x):
    center = x - jnp.mean(x, axis=-1, keepdims=True)
    spread_sq = jnp.mean(center * center, axis=-1, keepdims=True)
    r = lax.rsqrt(spread_sq + 1e-05)
    return center * r, r


def norm_back(grad, n, r, gain):
    gn = grad * gain
    return r * (gn - jnp.mean(gn, axis=-1, keepdims=True) - n * jnp.mean(gn * n, axis=-1, keepdims=True))


def mask_kernel(p_ref, o_ref, *, rows):
    n, k = p_ref.shape
    mem = o_ref.shape[1]
    for r in range(0, n, rows):
        p = p_ref[r:r+rows, :]
        ids = lax.broadcasted_iota(jnp.int32, (rows, mem), 1)
        hit = p[:, 0:1] == ids
        for t in range(1, k):
            hit = hit | (p[:, t:t+1] == ids)
        o_ref[r:r+rows, :] = jnp.where(hit, 1.0, 0.0).astype(bf16)

def picked_masks(picked, mem, interpret=False):
    h, n, k = picked.shape
    return pl.pallas_call(
        functools.partial(mask_kernel, rows=32),
        grid=(h,),
        in_specs=[pl.BlockSpec((None, n, k), lambda i: (i,0,0))],
        out_specs=pl.BlockSpec((None, n, mem), lambda i: (i,0,0)),
        out_shape=jax.ShapeDtypeStruct((h,n,mem), bf16),
        cost_estimate=pl.CostEstimate(flops=2*h*n*k*mem, bytes_accessed=h*n*(mem*2+512), transcendentals=0),
        interpret=interpret,
    )(picked)

def spread(base, blk):
    w = base.shape[1]
    x = jnp.broadcast_to(base, (8, w))
    r = lax.broadcasted_iota(jnp.int32, (8, w), 0)
    for b in (1, 2, 4):
        x = jnp.where((r & b) != 0, pltpu.roll(x, b, 1), x)
    size = 8
    while size < blk:
        x = jnp.concatenate([x, pltpu.roll(x, size, 1)], axis=0)
        size *= 2
    return x

def gather_diagonals(g):
    size, w = g.shape
    while size > 8:
        half = size // 2
        g = g[:half] + pltpu.roll(g[half:], w - half, 1)
        size = half
    r = lax.broadcasted_iota(jnp.int32, (8, w), 0)
    for b in (4, 2, 1):
        g = jnp.where((r & b) != 0, pltpu.roll(g, w - b, 1), g)
    return jnp.sum(g, axis=0, keepdims=True)

BLK = 128

def unit_back(g, u, r):
    u = u.astype(f32)
    return (r * (g - u * jnp.sum(g * u, axis=1, keepdims=True))).astype(bf16)

edges=[b for b in range(1,16)]+[int(math.ceil(16.0*8.0**((b-16)/16.0))) for b in range(16,32)]
def diagonal_rel(seg):
    wt = 2*seg + seg - BLK + BLK
    k = jnp.arange(wt, dtype=jnp.int32)
    top = 2*seg - BLK
    return jnp.where(k > wt - BLK, top - (k - wt), top - k)

def bucket_hot(seg):
    rel = diagonal_rel(seg)
    counts = jnp.zeros_like(rel)
    for e in edges: counts = counts + (rel >= e).astype(jnp.int32)
    hot = (counts[None,:] == jnp.arange(len(edges)+1)[:,None]) & (rel >= 0)[None,:]
    return hot.astype(f32), rel
def diagonal_bias(table, hot, rel):
    v = jnp.dot(table, hot, precision=lax.Precision.HIGHEST) * LOG2E
    return jnp.where(rel[None,:] >= 0, v, NEG)[:, None, :]


def wide_fwd_kernel(gate_ref, reset_ref, q_ref, kp_ref, kc_ref, vp_ref, vc_ref, base_ref, mk_ref, mv_ref, mask_ref,
                    mix_ref, loc_ref, rem_ref, t_ref):
    seg = q_ref.shape[0]
    h = pl.program_id(0)
    s = gate_ref[h]
    keep = jnp.where(reset_ref[0] == 0, 1.0, 0.0).astype(f32)
    t_ref[...] = spread(base_ref[...], BLK)
    heat = 16.0 * LOG2E
    nb = seg // BLK
    vp = vp_ref[...] * keep.astype(bf16)
    mk = mk_ref[...]; mv = mv_ref[...]
    for i in range(nb):
        rows = slice(i*BLK, (i+1)*BLK)
        q = q_ref[rows, :]
        off = (nb-1-i)*BLK
        cw = (i+1)*BLK
        ep = jnp.exp2(nt(q, kp_ref[...]) * heat + t_ref[:, off:off+seg])
        ec = jnp.exp2(nt(q, kc_ref[:cw, :]) * heat + t_ref[:, off+seg:off+seg+cw])
        il = 1.0 / (keep * jnp.sum(ep, axis=1, keepdims=True) + jnp.sum(ec, axis=1, keepdims=True))
        o = nn((ep * il).astype(bf16), vp) + nn((ec * il).astype(bf16), vc_ref[:cw, :])
        em = jnp.exp2(nt(q, mk) * heat) * mask_ref[rows, :].astype(f32)
        em = em * (1.0 / jnp.sum(em, axis=1, keepdims=True))
        om = nn(em.astype(bf16), mv)
        loc_ref[rows, :] = o.astype(bf16)
        rem_ref[rows, :] = om.astype(bf16)
        mix_ref[rows, :] = (s*om + (1.0-s)*o).astype(bf16)

def attn_fwd(gate, reset, q, kp, kc, vp, vc, base, mk, mv, mask, interpret=False):
    seg, width = q.shape
    heads = base.shape[0]
    dh = width // heads
    mem = mk.shape[0]
    col = lambda n: pl.BlockSpec((n, dh), lambda h, *_: (0, h))
    full = jax.ShapeDtypeStruct((seg, width), bf16)
    wt = base.shape[2]
    return pl.pallas_call(
        wide_fwd_kernel,
        grid_spec=pltpu.PrefetchScalarGridSpec(
            num_scalar_prefetch=2, grid=(heads,),
            in_specs=[col(seg), col(seg), col(seg), col(seg), col(seg),
                      pl.BlockSpec((None,1,wt), lambda h,*_: (h,0,0)), col(mem), col(mem),
                      pl.BlockSpec((None,seg,mem), lambda h,*_: (h,0,0))],
            out_specs=[col(seg), col(seg), col(seg)],
            scratch_shapes=[pltpu.VMEM((BLK, wt), f32)]),
        out_shape=[full, full, full],
        compiler_params=pltpu.CompilerParams(vmem_limit_bytes=48<<20),
        cost_estimate=pl.CostEstimate(flops=heads*seg*(2*seg+mem)*4*dh, bytes_accessed=8*seg*width*2+heads*seg*mem*2, transcendentals=heads*seg*(2*seg+mem)),
        interpret=interpret,
    )(gate, reset, q, kp, kc, vp, vc, base, mk, mv, mask)

def wide_bwd_kernel(gate_ref, reset_ref, q_ref, kp_ref, kc_ref, vp_ref, vc_ref, base_ref, mk_ref, mv_ref, mask_ref,
                    loc_ref, rem_ref, gm_ref, rq_ref, rkp_ref, rkc_ref,
                    dc_ref, dp_ref, diag_ref, dgate_ref, t_ref, g_ref, akp, akc, avp, avc):
    seg = q_ref.shape[0]
    h = pl.program_id(0)
    s = gate_ref[h]
    keep = jnp.where(reset_ref[0] == 0, 1.0, 0.0).astype(f32)
    t_ref[...] = spread(base_ref[...], BLK)
    g_ref[...] = jnp.zeros_like(g_ref)
    heat = 16.0 * LOG2E
    nb = seg // BLK
    mk = mk_ref[...]; mv = mv_ref[...]
    dg = jnp.zeros((BLK, 1), f32)
    for i in range(nb):
        rows = slice(i*BLK, (i+1)*BLK)
        q = q_ref[rows, :]
        gm = gm_ref[rows, :]
        off = (nb-1-i)*BLK
        cw = (i+1)*BLK
        al = jnp.sum(gm * loc_ref[rows, :].astype(f32), axis=1, keepdims=True)
        ar = jnp.sum(gm * rem_ref[rows, :].astype(f32), axis=1, keepdims=True)
        dg = dg + (ar - al)
        gl = ((1.0-s)*gm).astype(bf16)
        gr = (s*gm).astype(bf16)
        ep = jnp.exp2(nt(q, kp_ref[...]) * heat + t_ref[:, off:off+seg])
        ec = jnp.exp2(nt(q, kc_ref[:cw, :]) * heat + t_ref[:, off+seg:off+seg+cw])
        l = keep * jnp.sum(ep, axis=1, keepdims=True) + jnp.sum(ec, axis=1, keepdims=True)
        il = 1.0 / l
        ilp = il * keep
        pp = ep * ilp
        pc = ec * il
        wp = pp * nt(gl, vp_ref[...])
        wc = pc * nt(gl, vc_ref[:cw, :])
        dl = jnp.sum(wp, axis=1, keepdims=True) + jnp.sum(wc, axis=1, keepdims=True)
        dsp = (wp - pp * dl).astype(bf16); dsc = (wc - pc * dl).astype(bf16)
        g_ref[:, off:off+seg] += dsp.astype(f32)
        g_ref[:, off+seg:off+seg+cw] += dsc.astype(f32)
        dq = nn(dsp, kp_ref[...]) + nn(dsc, kc_ref[:cw, :])
        ppb = pp.astype(bf16); pcb = pc.astype(bf16)
        dkp = tn(dsp, q); dvp = tn(ppb, gl)
        dkc = tn(dsc, q); dvc = tn(pcb, gl)
        if i == 0:
            akp[...] = dkp; avp[...] = dvp
            akc[...] = jnp.zeros_like(akc); avc[...] = jnp.zeros_like(avc)
            akc[:cw, :] = dkc; avc[:cw, :] = dvc
        else:
            akp[...] += dkp; avp[...] += dvp
            akc[:cw, :] += dkc; avc[:cw, :] += dvc
        em = jnp.exp2(nt(q, mk) * heat) * mask_ref[rows, :].astype(f32)
        ilm = 1.0 / jnp.sum(em, axis=1, keepdims=True)
        em = em * ilm
        gw = nt(gr, mv)
        dsm = em * (gw - jnp.sum(em * gw, axis=1, keepdims=True))
        dq = dq + nn(dsm.astype(bf16), mk)
        dc_ref[0, rows, :] = unit_back(16.0 * dq, q, rq_ref[rows, :])
    dp_ref[0] = unit_back(16.0 * akp[...], kp_ref[...], rkp_ref[...])
    dc_ref[1] = unit_back(16.0 * akc[...], kc_ref[...], rkc_ref[...])
    dp_ref[1] = avp[...].astype(bf16)
    dc_ref[2] = avc[...].astype(bf16)
    diag_ref[...] = gather_diagonals(g_ref[...])
    dgate_ref[...] = jnp.broadcast_to(jnp.sum(dg) * s * (1.0-s), dgate_ref.shape)

def attn_bwd(gate, reset, q, kp, kc, vp, vc, rq, rkp, rkc, base, mk, mv, mask, loc, rem, gm, interpret=False):
    seg, width = q.shape
    heads = base.shape[0]
    dh = width // heads
    mem = mk.shape[0]
    wt = base.shape[2]
    col = lambda n: pl.BlockSpec((n, dh), lambda h, *_: (0, h))
    row = lambda w: pl.BlockSpec((None,1,w), lambda h,*_: (h,0,0))
    rcol = pl.BlockSpec((None,seg,1), lambda h,*_: (h,0,0))
    fb = jax.ShapeDtypeStruct((seg, width), bf16)
    return pl.pallas_call(
        wide_bwd_kernel,
        grid_spec=pltpu.PrefetchScalarGridSpec(
            num_scalar_prefetch=2, grid=(heads,),
            in_specs=[col(seg)]*5 + [row(wt), col(mem), col(mem),
                      pl.BlockSpec((None,seg,mem), lambda h,*_: (h,0,0)), col(seg), col(seg), col(seg), rcol, rcol, rcol],
            out_specs=[pl.BlockSpec((3,seg,dh), lambda h,*_: (0,0,h)), pl.BlockSpec((2,seg,dh), lambda h,*_: (0,0,h)), row(wt), row(128)],
            scratch_shapes=[pltpu.VMEM((BLK, wt), f32)]*2 + [pltpu.VMEM((seg, dh), f32)]*4),
        out_shape=[jax.ShapeDtypeStruct((3,seg,width),bf16), jax.ShapeDtypeStruct((2,seg,width),bf16), jax.ShapeDtypeStruct((heads,1,wt), f32), jax.ShapeDtypeStruct((heads,1,128), f32)],
        compiler_params=pltpu.CompilerParams(vmem_limit_bytes=48<<20),
        cost_estimate=pl.CostEstimate(flops=heads*seg*(2*seg+mem)*10*dh, bytes_accessed=20*seg*width*2+heads*seg*mem*2, transcendentals=heads*seg*(2*seg+mem)),
        interpret=interpret,
    )(gate, reset, q, kp, kc, vp, vc, base, mk, mv, mask, loc, rem, gm, rq, rkp, rkc)


def wide_qkv_kernel(xp_ref, xc_ref, gain_ref, shift_ref, w_ref, q_ref, kp_ref, kc_ref, vp_ref, vc_ref, rq_ref, rkp_ref, rkc_ref, np_ref, nc_ref, x_ref, *, dh):
    i = pl.program_id(0)
    per = pl.num_programs(0) // 3
    seg = xc_ref.shape[0]

    @pl.when(i == 0)
    def _():
        gain = gain_ref[...].astype(f32)
        shift = shift_ref[...].astype(f32)
        for src, dst, at in ((xp_ref, np_ref, 0), (xc_ref, nc_ref, seg)):
            n, r = norm_stats(src[...].astype(f32))
            low = (n * gain + shift).astype(bf16)
            x_ref[at : at + seg, :] = low
            dst[...] = low

    def unit(y, out_ref, r_ref):
        for k in range(y.shape[1] // dh):
            part = y[:, k * dh : (k + 1) * dh]
            r = lax.rsqrt(jnp.sum(part * part, axis=1, keepdims=True) + 1e-06)
            out_ref[:, k * dh : (k + 1) * dh] = (part * r).astype(bf16)
            r_ref[k] = r

    w = w_ref[...]

    @pl.when(i < per)
    def _():
        unit(nn(x_ref[seg:, :], w), q_ref, rq_ref)

    @pl.when((i >= per) & (i < 2 * per))
    def _():
        unit(nn(x_ref[:seg, :], w), kp_ref, rkp_ref)
        unit(nn(x_ref[seg:, :], w), kc_ref, rkc_ref)

    @pl.when(i >= 2 * per)
    def _():
        vp_ref[...] = nn(x_ref[:seg, :], w).astype(bf16)
        vc_ref[...] = nn(x_ref[seg:, :], w).astype(bf16)


def project_qkv(xp, xc, gain, shift, w, heads):
    seg, width = xc.shape
    dh = width // heads
    two = 2 * dh
    per = width // two
    whole = pl.BlockSpec((seg, width), lambda i: (0, 0))
    vec = pl.BlockSpec((1, width), lambda i: (0, 0))
    at = lambda s: (lambda i: (0, jnp.clip(i - s * per, 0, per - 1)))
    at3 = lambda s: (lambda i: (jnp.clip(i - s * per, 0, per - 1), 0, 0))
    cols = lambda s: pl.BlockSpec((seg, two), at(s))
    rs = lambda s: pl.BlockSpec((2, seg, 1), at3(s))
    low = jax.ShapeDtypeStruct((seg, width), bf16)
    rr = jax.ShapeDtypeStruct((heads, seg, 1), f32)
    return pl.pallas_call(
        functools.partial(wide_qkv_kernel, dh=dh),
        grid=(3 * per,),
        in_specs=[whole, whole, vec, vec, pl.BlockSpec((width, two), lambda i: (0, i))],
        out_specs=[cols(0), cols(1), cols(1), cols(2), cols(2), rs(0), rs(1), rs(1), whole, whole],
        out_shape=[low] * 5 + [rr] * 3 + [low] * 2,
        scratch_shapes=[pltpu.VMEM((2 * seg, width), bf16)],
        compiler_params=pltpu.CompilerParams(vmem_limit_bytes=48 << 20),
        cost_estimate=pl.CostEstimate(flops=2 * seg * width * width * 5, bytes_accessed=3 * width * width * 2 + 9 * seg * width * 2, transcendentals=0),
    )(xp, xc, gain, shift, w)


def middle_kernel(att_ref, tok_ref, cot_ref, wo_ref, up_ref, dn_ref, bu_ref, bd_ref, gain_ref, shift_ref,
                  out_ref, one_ref, gm_ref, gup_ref, gdn_ref, gout_ref, gbu_ref, vec_ref,
                  res_ref, n_ref, low_ref, r_ref, acc_ref, gh_ref):
    j = pl.program_id(0)
    last = pl.num_programs(0) - 1
    width = tok_ref.shape[1]

    @pl.when(j == 0)
    def _():
        res = tok_ref[...].astype(f32) + nn(att_ref[...], wo_ref[...])
        res_ref[...] = res
        n, r = norm_stats(res)
        n_ref[...] = n
        r_ref[...] = r
        low_ref[...] = (n * gain_ref[...].astype(f32) + shift_ref[...].astype(f32)).astype(bf16)

    low = low_ref[...]
    cot = cot_ref[...]
    up = up_ref[...]
    dn = dn_ref[...]
    p = nn(low, up) + bu_ref[...].astype(f32)
    ga = nt(cot, dn)
    k0 = math.sqrt(2.0 / math.pi)
    p2 = p * p
    t = jnp.tanh(p * (k0 + (k0 * 0.044715) * p2))
    half = 0.5 * (1.0 + t)
    act = (p * half).astype(bf16)
    slope = half + 0.5 * p * (1.0 - t * t) * (k0 + (3.0 * k0 * 0.044715) * p2)
    gp = (ga * slope).astype(bf16)
    o = nn(act, dn)
    g = nt(gp, up)
    gup_ref[...] = tn(low, gp).astype(bf16)
    gd = tn(act, cot).astype(bf16)
    cols = width // 4
    for q in range(4):
        gdn_ref[q] = gd[:, q * cols : (q + 1) * cols]
    gbu_ref[...] = jnp.sum(gp.astype(f32), axis=0, keepdims=True)

    @pl.when(j == 0)
    def _():
        acc_ref[...] = o
        gh_ref[...] = g

    @pl.when(j > 0)
    def _():
        acc_ref[...] += o
        gh_ref[...] += g

    @pl.when(j == last)
    def _():
        out_ref[...] = (res_ref[...] + acc_ref[...] + bd_ref[...].astype(f32)).astype(bf16)
        gh = gh_ref[...]
        n = n_ref[...]
        cf = cot.astype(f32)
        vec_ref[0:1, :] = jnp.sum(gh * n, axis=0, keepdims=True)
        vec_ref[1:2, :] = jnp.sum(gh, axis=0, keepdims=True)
        vec_ref[2:3, :] = jnp.sum(cf, axis=0, keepdims=True)
        one = cf + norm_back(gh, n, r_ref[...], gain_ref[...].astype(f32))
        one_ref[...] = one
        ol = one.astype(bf16)
        gm_ref[...] = nt(ol, wo_ref[...])
        go = tn(att_ref[...], ol).astype(bf16)
        for q in range(4):
            gout_ref[q] = go[:, q * cols : (q + 1) * cols]


def middle(att, tok, cot, wo, up, dn, bu, bd, gain, shift):
    seg, width = tok.shape
    ff = up.shape[1]
    blk = 512
    per = ff // 4 // blk
    once = dict(pipeline_mode=pl.Buffered(1))
    whole = pl.BlockSpec((seg, width), lambda j: (0, 0), **once)
    vec = pl.BlockSpec((1, width), lambda j: (0, 0))
    q4 = width // 4
    return pl.pallas_call(
        middle_kernel,
        grid=(ff // blk,),
        in_specs=[whole, whole, whole, pl.BlockSpec((width, width), lambda j: (0, 0), **once),
                  pl.BlockSpec((width, blk), lambda j: (0, j)), pl.BlockSpec((blk, width), lambda j: (j, 0)),
                  pl.BlockSpec((1, blk), lambda j: (0, j)), vec, vec, vec],
        out_specs=[whole, whole, whole,
                   pl.BlockSpec((None, width, blk), lambda j: (j // per, 0, j % per)),
                   pl.BlockSpec((4, blk, q4), lambda j: (0, j, 0)),
                   pl.BlockSpec((4, width, q4), lambda j: (0, 0, 0), **once),
                   pl.BlockSpec((1, blk), lambda j: (0, j)),
                   pl.BlockSpec((8, width), lambda j: (0, 0))],
        out_shape=[jax.ShapeDtypeStruct((seg, width), bf16), jax.ShapeDtypeStruct((seg, width), f32), jax.ShapeDtypeStruct((seg, width), f32),
                   jax.ShapeDtypeStruct((4, width, ff // 4), bf16), jax.ShapeDtypeStruct((4, ff, q4), bf16), jax.ShapeDtypeStruct((4, width, q4), bf16),
                   jax.ShapeDtypeStruct((1, ff), f32), jax.ShapeDtypeStruct((8, width), f32)],
        scratch_shapes=[pltpu.VMEM((seg, width), f32)] * 2 + [pltpu.VMEM((seg, width), bf16), pltpu.VMEM((seg, 1), f32)] + [pltpu.VMEM((seg, width), f32)] * 2,
        compiler_params=pltpu.CompilerParams(vmem_limit_bytes=56 << 20),
        cost_estimate=pl.CostEstimate(flops=2 * seg * width * (6 * ff + 3 * width), bytes_accessed=8 * width * ff + 16 * seg * width, transcendentals=seg * ff),
    )(att, tok, cot, wo, up, dn, bu, bd, gain, shift)


def wide_back_kernel(d_ref, w_ref, o_ref, acc_ref):
    j = pl.program_id(0)
    g = nt(d_ref[...], w_ref[...])

    @pl.when(j == 0)
    def _():
        acc_ref[...] = g

    @pl.when(j > 0)
    def _():
        acc_ref[...] += g

    @pl.when(j == pl.num_programs(0) - 1)
    def _():
        o_ref[...] = acc_ref[...].astype(bf16)


def wide_before_grad(d_prev, w):
    _, seg, width = d_prev.shape
    blk = 512
    per = width // blk
    return pl.pallas_call(
        wide_back_kernel,
        grid=(2 * per,),
        in_specs=[pl.BlockSpec((None, seg, blk), lambda j: (j // per, 0, j % per)), pl.BlockSpec((width, blk), lambda j: (0, per + j))],
        out_specs=pl.BlockSpec((seg, width), lambda j: (0, 0)),
        out_shape=jax.ShapeDtypeStruct((seg, width), bf16),
        scratch_shapes=[pltpu.VMEM((seg, width), f32)],
        compiler_params=pltpu.CompilerParams(vmem_limit_bytes=32 << 20),
        cost_estimate=pl.CostEstimate(flops=4 * seg * width * width, bytes_accessed=4 * width * width, transcendentals=0),
    )(d_prev, w)


def tail_kernel(dc_ref, dp_ref, nc_ref, np_ref, w_ref, g_ref, h_ref):
    j = pl.program_id(0)
    per = pl.num_programs(0) // 3
    dc = dc_ref[...]
    h = nt(dc, w_ref[...])

    @pl.when(j == 0)
    def _():
        h_ref[...] = h

    @pl.when(j > 0)
    def _():
        h_ref[...] += h

    @pl.when(j < per)
    def _():
        g_ref[...] = tn(nc_ref[...], dc).astype(bf16)

    @pl.when(j >= per)
    def _():
        g_ref[...] = (tn(nc_ref[...], dc) + tn(np_ref[...], dp_ref[...])).astype(bf16)


def qkv_back(d_cur, d_prev, n_cur, n_prev, w):
    _, seg, width = d_cur.shape
    blk = 256
    per = width // blk
    quarter = 3 * width // 4
    pq = quarter // blk
    whole = pl.BlockSpec((seg, width), lambda j: (0, 0))
    return pl.pallas_call(
        tail_kernel,
        grid=(3 * per,),
        in_specs=[pl.BlockSpec((None, seg, blk), lambda j: (j // per, 0, j % per)),
                  pl.BlockSpec((None, seg, blk), lambda j: (jnp.maximum(j // per - 1, 0), 0, jnp.where(j < per, 0, j % per))),
                  whole, whole, pl.BlockSpec((width, blk), lambda j: (0, j))],
        out_specs=[pl.BlockSpec((None, width, blk), lambda j: (j // pq, 0, j % pq)), whole],
        out_shape=[jax.ShapeDtypeStruct((4, width, quarter), bf16), jax.ShapeDtypeStruct((seg, width), f32)],
        compiler_params=pltpu.CompilerParams(vmem_limit_bytes=40 << 20),
        cost_estimate=pl.CostEstimate(flops=2 * seg * width * width * 8, bytes_accessed=12 * width * width + 16 * seg * width, transcendentals=0),
    )(d_cur, d_prev, n_cur, n_prev, w)


def last_kernel(h_ref, back_ref, tok_ref, one_ref, gain_ref, out_ref, vec_ref):
    h = h_ref[...] + back_ref[...].astype(f32)
    n, r = norm_stats(tok_ref[...].astype(f32))
    vec_ref[0:1, :] = jnp.sum(h * n, axis=0, keepdims=True)
    vec_ref[1:2, :] = jnp.sum(h, axis=0, keepdims=True)
    out_ref[...] = one_ref[...] + norm_back(h, n, r, gain_ref[...].astype(f32))


def finish(h, back, tok, one, gain):
    seg, width = tok.shape
    return pl.pallas_call(
        last_kernel,
        out_shape=[jax.ShapeDtypeStruct((seg, width), f32), jax.ShapeDtypeStruct((8, width), f32)],
        compiler_params=pltpu.CompilerParams(vmem_limit_bytes=40 << 20),
        cost_estimate=pl.CostEstimate(flops=20 * seg * width, bytes_accessed=16 * seg * width, transcendentals=0),
    )(h, back, tok, one, gain)


def local_wide(
    tokens, resets, retrieved, memory_keys, memory_values, qkv_weight, out_weight, up_weight, up_bias,
    down_weight, down_bias, attn_gain, attn_shift, ffn_gain, ffn_shift, position_bias, memory_gate, cotangent,
):
    heads = memory_gate.shape[0]
    seg, width = tokens.shape[1:]
    dh = width // heads
    mem_rows = memory_keys.shape[1]
    shards = lax.axis_size("fsdp")
    mem = mem_rows * shards
    part = width // shards
    bias_part = up_bias.shape[0]
    pos_part = position_bias.shape[0]
    small, mk, mv = gather_small(memory_keys, memory_values, [up_bias, down_bias, attn_gain, attn_shift, ffn_gain, ffn_shift, position_bias], heads)
    b_up = small[:, :bias_part].reshape(-1)
    vecs = [small[:, bias_part + k * part : bias_part + (k + 1) * part].reshape(1, -1) for k in range(5)]
    b_down, gain_one, shift_one, gain_two, shift_two = vecs
    table = small[:, bias_part + 5 * part : bias_part + 5 * part + pos_part].reshape(heads, -1).astype(f32)
    w_qkv, w_out, w_up, w_down = [lax.all_gather(w, "fsdp", axis=0, tiled=True) for w in (qkv_weight, out_weight, up_weight, down_weight)]
    before = passed_along(tokens[0], "fsdp", 1)
    mask = picked_masks(retrieved[0].transpose(1, 0, 2), mem)
    hot, rel = bucket_hot(seg)
    base = diagonal_bias(table, hot, rel)
    gate = jax.nn.sigmoid(memory_gate.astype(f32))
    reset = resets[0]
    q, kp, kc, vp, vc, rq, rkp, rkc, n_prev, n_cur = project_qkv(before, tokens[0], gain_one, shift_one, w_qkv, heads)
    attn_in, loc, rem = attn_fwd(gate, reset, q, kp, kc, vp, vc, base, mk, mv, mask)
    output, grad_one, gm, up_g, down_g, out_g, up_bias_g, vec_two = middle(
        attn_in, tokens[0], cotangent[0], w_out, w_up, w_down, b_up.reshape(1, -1), b_down, gain_two, shift_two)
    up_t, down_t, out_t = scatter_weights((up_g, down_g, out_g))
    d_cur, d_prev, diag, dgate = attn_bwd(gate, reset, q, kp, kc, vp, vc, rq, rkp, rkc, base, mk, mv, mask, loc, rem, gm)
    gate_g = dgate[:, 0, 0]
    table_g = jnp.dot(diag[:, 0], hot.T, precision=lax.Precision.HIGHEST)
    back = passed_along(wide_before_grad(d_prev, w_qkv), "fsdp", -1)
    qkv_g, grad_h1 = qkv_back(d_cur, d_prev, n_cur, n_prev, w_qkv)
    (qkv_t,) = scatter_weights((qkv_g,))
    token_grad, vec_one = finish(grad_h1, back, tokens[0], grad_one, gain_one)
    gain_two_g, shift_two_g, down_bias_g = vec_two[0], vec_two[1], vec_two[2]
    gain_one_g, shift_one_g = vec_one[0], vec_one[1]
    small_g = jnp.concatenate(
        [up_bias_g.reshape(shards, -1)]
        + [v.reshape(shards, -1) for v in (down_bias_g, gain_one_g, shift_one_g, gain_two_g, shift_two_g, table_g)]
        + [jnp.broadcast_to(gate_g[None], (shards, heads))],
        axis=1,
    )
    small_g = summed_everywhere(small_g)
    small_g = lax.dynamic_index_in_dim(small_g, lax.axis_index("fsdp"), 0, keepdims=False)
    cuts = [bias_part] + [part] * 5 + [pos_part, heads]
    at = 0
    outs = []
    for c in cuts:
        outs.append(small_g[at : at + c])
        at += c
    ub, db, g1, s1, g2, s2, pg, gg = outs
    return output[None], token_grad[None], qkv_t, out_t, up_t, ub, down_t, db, g1, s1, g2, s2, pg, gg


def take(v, i, axis):
    return lax.dynamic_index_in_dim(v, i, axis, keepdims=False)


def fence(*trees):
    return lax.optimization_barrier(trees)


def major_first(v):
    return with_layout_constraint(v, Layout(tuple(range(v.ndim))))


def add_low(u, v):
    return (u.astype(f32) + v.astype(f32)).astype(bf16)


def hits_kernel(at_ref, p_ref, o_ref):
    slots, n = p_ref.shape
    mem = o_ref.shape[0]
    lane = 128
    ids = lax.broadcasted_iota(jnp.int32, (mem, lane), 0)
    rows = mem // 8
    chip = (((ids // rows) & 3) ^ at_ref[0]) * 2 + ((ids // (4 * rows)) ^ at_ref[1])
    ids = chip * rows + ids % rows
    for t in range(n // lane):
        cols = slice(t * lane, (t + 1) * lane)
        acc = jnp.zeros((mem, lane), f32)
        for s in range(slots):
            acc = jnp.where(ids == p_ref[s : s + 1, cols], 1.0, acc)
        o_ref[:, cols] = acc.astype(bf16)


def hit_masks(at, picked, mem):
    h, slots, n = picked.shape
    return pl.pallas_call(
        hits_kernel,
        grid_spec=pltpu.PrefetchScalarGridSpec(
            num_scalar_prefetch=1, grid=(h,),
            in_specs=[pl.BlockSpec((None, slots, n), lambda i, at: (i, 0, 0))],
            out_specs=pl.BlockSpec((None, mem, n), lambda i, at: (i, 0, 0))),
        out_shape=jax.ShapeDtypeStruct((h, mem, n), bf16),
        cost_estimate=pl.CostEstimate(flops=2 * h * n * slots * mem, bytes_accessed=h * n * mem * 2, transcendentals=0),
    )(at, picked)


def prep_kernel(at_ref, reset_ref, wq_ref, up_ref, dn_ref, wo_ref, mk_ref, mv_ref, *refs):
    vectors, (qo_ref, qs_ref, ro_ref, rs_ref, d1_ref) = refs[:-5], refs[-5:]
    r = wq_ref.shape[0]
    m = mk_ref.shape[0]
    c, x = at_ref[2], at_ref[3]
    width = wq_ref.shape[1] // 3
    lane = 128
    at = lambda col: pl.ds(pl.multiple_of(col, lane), lane)
    lanes = lambda k: slice(k * lane, (k + 1) * lane)
    for qd, rd, cc in ((qo_ref, ro_ref, c), (qs_ref, rs_ref, 1 - c)):
        for ab in range(2):
            for part in range(3):
                qd[ab * r : (ab + 1) * r, lanes(part)] = wq_ref[:, at(part * width + (4 * cc + 2 * x + ab) * lane)]
            for half in range(2):
                for yy in range(2):
                    col = ((2 * (2 * x + ab) + yy) * 2 + cc) * 2 * lane + half * lane
                    row = (half * 2 + ab) * r
                    rd[row : row + r, lanes(yy)] = up_ref[:, at(col)]
            rd[4 * r : 5 * r, lanes(ab)] = wo_ref[:, at((4 * cc + 2 * x + ab) * lane)]
        for kv, src in enumerate((mk_ref, mv_ref)):
            for h in range(4):
                row = 5 * r + (kv * 2 + h // 2) * m
                rd[row : row + m, lanes(h % 2)] = src[:, at((4 * cc + h) * lane)]
        qd[2 * r :, :] = jnp.zeros((8, 3 * lane), bf16)
        for k, v in enumerate(vectors):
            qd[2 * r + k : 2 * r + k + 1, : v.shape[1]] = v[...]
        qd[2 * r + 7 : 2 * r + 8, :lane] = jnp.broadcast_to(reset_ref[0, 0].astype(f32), (1, lane)).astype(bf16)
    for ab in range(2):
        for half in range(2):
            for yy in range(2):
                d1_ref[half, ab, :, lanes(yy)] = dn_ref[half * lane : (half + 1) * lane, at((2 * x + ab) * 2 * lane + yy * lane)]


def prepare(at, resets, wq, up, dn, wo, mk, mv, vectors):
    r, m = wq.shape[0], mk.shape[0]
    s = lambda *d: jax.ShapeDtypeStruct(d, bf16)
    return pl.pallas_call(
        prep_kernel,
        in_specs=[pl.BlockSpec(memory_space=pltpu.SMEM)] * 2 + [pl.BlockSpec(memory_space=pltpu.VMEM)] * (6 + len(vectors)),
        out_shape=[s(2 * r + 8, 384), s(2 * r + 8, 384), s(5 * r + 4 * m, 256), s(5 * r + 4 * m, 256), s(2, 2, 128, 256)],
    )(at, resets, wq, up, dn, wo, mk, mv, *[v.reshape(1, -1) for v in vectors])


def pack_kernel(at_ref, own_ref, got_ref, d_ref, f1_ref, f2_ref, *, m):
    c = at_ref[2]
    lane = 128

    def fill(r0, r1):
        for ab in range(2):
            a = 448 * ab
            f1_ref[a : a + 64, :] = r0[64 * ab : 64 * ab + 64, :]
            f1_ref[a + 64 : a + 128, :] = r1[64 * ab : 64 * ab + 64, :]
            f1_ref[a + 128 : a + 256, :] = d_ref[0, ab]
            f1_ref[a + 256 : a + 320, :lane] = r0[256:320, lane * ab : lane * ab + lane]
            f1_ref[a + 256 : a + 320, lane:] = r1[256:320, lane * ab : lane * ab + lane]
            b = 256 * ab
            f2_ref[b : b + 64, :] = r0[128 + 64 * ab : 192 + 64 * ab, :]
            f2_ref[b + 64 : b + 128, :] = r1[128 + 64 * ab : 192 + 64 * ab, :]
            f2_ref[b + 128 : b + 256, :] = d_ref[1, ab]
        for k in range(4):
            at = 320 + 2 * k * m
            f1_ref[at : at + m, :] = r0[320 + k * m : 320 + (k + 1) * m, :]
            f1_ref[at + m : at + 2 * m, :] = r1[320 + k * m : 320 + (k + 1) * m, :]

    @pl.when(c == 0)
    def _():
        fill(own_ref, got_ref)

    @pl.when(c == 1)
    def _():
        fill(got_ref, own_ref)


def pack_ffn(at, own, got, d, m):
    s = lambda *e: jax.ShapeDtypeStruct(e, bf16)
    return pl.pallas_call(
        functools.partial(pack_kernel, m=m),
        in_specs=[pl.BlockSpec(memory_space=pltpu.SMEM)] + [pl.BlockSpec(memory_space=pltpu.VMEM)] * 3,
        out_shape=[s(768, 256), s(512, 256)],
    )(at, own, got, d)


def piece_places(at_ref):
    z, y, x = at_ref[0], at_ref[1], at_ref[3]
    for kind in range(4):
        for i in range(2):
            for k in range(4):
                yy = (y ^ i) if kind < 2 else (y if kind == 2 else 1 - y)
                xx = (x if kind == 0 else 1 - x) if kind < 2 else (x ^ i)
                yield kind * 2 + i, k, (z ^ k) * 2 + yy, 2 * xx + kind // 2


def qkv_kernel(at_ref, tp_ref, own_ref, oth_ref, gain_ref, shift_ref, p0, p1, p2, p3, p4, p5, p6, p7,
               q_ref, k_ref, v_ref, rq_ref, rk_ref, xn_hbm, w_hbm, x_ref, w_ref, sem, osem):
    i = pl.program_id(0)
    seg = tp_ref.shape[0]
    dh = 128
    half = w_ref.shape[1] // 3
    outs = [pltpu.make_async_copy(x_ref, xn_hbm, osem.at[0]), pltpu.make_async_copy(w_ref, w_hbm, osem.at[1])]

    @pl.when(i == 0)
    def _():
        copies = []
        pieces = (p0, p1, p2, p3, p4, p5, p6, p7)
        for kind, slot, chip, quarter in piece_places(at_ref):
            for part in range(3):
                dst = w_ref.at[pl.ds(pl.multiple_of(chip * 128, 128), 128), pl.ds(pl.multiple_of(part * half + quarter * dh, dh), dh)]
                copies.append(pltpu.make_async_copy(pieces[kind].at[slot, pl.ds(0, 128), pl.ds(part * dh, dh)], dst, sem))
        for copy in copies:
            copy.start()
        gain = gain_ref[...].astype(f32)
        shift = shift_ref[...].astype(f32)
        for s, src in enumerate((tp_ref, own_ref, oth_ref)):
            first = 0 if s == 0 else seg * (1 + at_ref[2]) if s == 1 else seg * (2 - at_ref[2])
            for r0 in range(0, seg, 128):
                n, r = norm_stats(src[r0 : r0 + 128, :].astype(f32))
                x_ref[pl.ds(pl.multiple_of(first + r0, 128), 128), :] = (n * gain + shift).astype(bf16)
        for copy in copies:
            copy.wait()
        for copy in outs:
            copy.start()

    def unit(y, out_ref, r_ref):
        for k in range(2):
            part = y[:, k * dh : (k + 1) * dh]
            r = lax.rsqrt(jnp.sum(part * part, axis=1, keepdims=True) + 1e-06)
            out_ref[:, k * dh : (k + 1) * dh] = (part * r).astype(bf16)
            r_ref[k] = r

    w = w_ref[:, pl.ds(pl.multiple_of(i * 256, 256), 256)]

    @pl.when(i < 2)
    def _():
        unit(nn(x_ref[seg:, :], w), q_ref, rq_ref)

    @pl.when((i >= 2) & (i < 4))
    def _():
        unit(nn(x_ref[...], w), k_ref, rk_ref)

    @pl.when(i >= 4)
    def _():
        v_ref[...] = nn(x_ref[...], w).astype(bf16)

    @pl.when(i == 5)
    def _():
        for copy in outs:
            copy.wait()


def project_pair(at, tp, own, oth, gain, shift, pieces):
    seg, width = tp.shape
    half = width // 2
    once = dict(pipeline_mode=pl.Buffered(1))
    whole = pl.BlockSpec((seg, width), lambda i, *_: (0, 0), **once)
    vec = pl.BlockSpec((1, width), lambda i, *_: (0, 0))
    hbm = pl.BlockSpec(memory_space=pltpu.HBM)
    col = lambda n, s: pl.BlockSpec((n * seg, 256), lambda i, *_: (0, jnp.clip(i - s, 0, 1)))
    rs = lambda n, s: pl.BlockSpec((2, n * seg, 1), lambda i, *_: (jnp.clip(i - s, 0, 1), 0, 0))
    sd = jax.ShapeDtypeStruct
    return pl.pallas_call(
        qkv_kernel,
        grid_spec=pltpu.PrefetchScalarGridSpec(
            num_scalar_prefetch=1, grid=(6,),
            in_specs=[whole, whole, whole, vec, vec] + [hbm] * 8,
            out_specs=[col(2, 0), col(3, 2), col(3, 4), rs(2, 0), rs(3, 2), hbm, hbm],
            scratch_shapes=[pltpu.VMEM((3 * seg, width), bf16), pltpu.VMEM((width, 3 * half), bf16), pltpu.SemaphoreType.DMA, pltpu.SemaphoreType.DMA((2,))]),
        out_shape=[sd((2 * seg, half), bf16), sd((3 * seg, half), bf16), sd((3 * seg, half), bf16), sd((4, 2 * seg, 1), f32), sd((4, 3 * seg, 1), f32),
                   sd((3 * seg, width), bf16), sd((width, 3 * half), bf16)],
        compiler_params=pltpu.CompilerParams(vmem_limit_bytes=48 << 20),
        cost_estimate=pl.CostEstimate(flops=2 * seg * width * half * 8, bytes_accessed=20 << 20, transcendentals=0),
    )(at, tp, own, oth, gain, shift, *pieces)


def attn_fwd_kernel(gate_ref, reset_ref, at_ref, q_ref, k_ref, v_ref, base_ref, mk0_ref, mk1_ref, mv0_ref, mv1_ref, mask0_ref, mask1_ref, mix_ref, loc_ref, rem_ref, t_ref):
    seg = q_ref.shape[0] // 2
    s = gate_ref[pl.program_id(0)]
    t_ref[...] = spread(base_ref[...], BLK)
    heat = 16.0 * LOG2E
    nb = seg // BLK
    mk = jnp.concatenate([mk0_ref[...].reshape(-1, 128), mk1_ref[...].reshape(-1, 128)]).astype(f32)
    mk = (mk * lax.rsqrt(jnp.sum(mk * mk, axis=1, keepdims=True) + 1e-06)).astype(bf16)
    mv = jnp.concatenate([mv0_ref[...].reshape(-1, 128), mv1_ref[...].reshape(-1, 128)])
    for u in range(2):
        keep = jnp.where(reset_ref[u] == 0, 1.0, 0.0).astype(f32)
        kp = k_ref[u * seg : (u + 1) * seg, :]
        vp = v_ref[u * seg : (u + 1) * seg, :] * keep.astype(bf16)
        for i in range(nb):
            rows = slice(u * seg + i * BLK, u * seg + (i + 1) * BLK)
            q = q_ref[rows, :]
            off = (nb - 1 - i) * BLK
            cw = (i + 1) * BLK
            kc = k_ref[(u + 1) * seg : (u + 1) * seg + cw, :]
            vc = v_ref[(u + 1) * seg : (u + 1) * seg + cw, :]
            ep = jnp.exp2(nt(q, kp) * heat + t_ref[:, off : off + seg])
            ec = jnp.exp2(nt(q, kc) * heat + t_ref[:, off + seg : off + seg + cw])
            il = 1.0 / (keep * jnp.sum(ep, axis=1, keepdims=True) + jnp.sum(ec, axis=1, keepdims=True))
            o = nn((ep * il).astype(bf16), vp) + nn((ec * il).astype(bf16), vc)
            em = jnp.exp2(nt(mk, q) * heat) * (mask0_ref, mask1_ref)[u][:, i * BLK : (i + 1) * BLK].astype(f32)
            em = em * (1.0 / jnp.sum(em, axis=0, keepdims=True))
            om = tn(em.astype(bf16), mv)
            loc_ref[rows, :] = o.astype(bf16)
            rem_ref[rows, :] = om.astype(bf16)
            mix_ref[rows, :] = (s * om + (1.0 - s) * o).astype(bf16)


def head_specs(seg, mem, wt, head=lambda h: h):
    dh = 128
    col = lambda n: pl.BlockSpec((n, dh), lambda h, *_: (0, head(h)))
    own = lambda k: pl.BlockSpec((4, mem // 8, dh), lambda h, *_: (0, 10 + 2 * k + head(h) // 2, head(h) % 2))
    return [col(2 * seg), col(3 * seg), col(3 * seg), pl.BlockSpec((None, 1, wt), lambda h, *_: (head(h), 0, 0)), own(0), own(0), own(1), own(1)] + [pl.BlockSpec((None, mem, seg), lambda h, *_: (head(h), 0, 0))] * 2


def attend(gate, reset, at, q, k, v, base, pack, masks):
    seg = q.shape[0] // 2
    mem, wt = masks[0].shape[1], base.shape[2]
    col = pl.BlockSpec((2 * seg, 128), lambda h, *_: (0, h))
    full = jax.ShapeDtypeStruct(q.shape, bf16)
    return pl.pallas_call(
        attn_fwd_kernel,
        grid_spec=pltpu.PrefetchScalarGridSpec(
            num_scalar_prefetch=3, grid=(4,), in_specs=head_specs(seg, mem, wt), out_specs=[col] * 3, scratch_shapes=[pltpu.VMEM((BLK, wt), f32)]),
        out_shape=[full] * 3,
        compiler_params=pltpu.CompilerParams(vmem_limit_bytes=48 << 20),
        cost_estimate=pl.CostEstimate(flops=8 * seg * (2 * seg + mem) * 4 * 128, bytes_accessed=20 << 20, transcendentals=8 * seg * (2 * seg + mem)),
    )(gate, reset, at, q, k, v, base, *pack, *pack, *masks)


def attn_bwd_kernel(gate_ref, reset_ref, at_ref, q_ref, k_ref, v_ref, base_ref, mk0_ref, mk1_ref, mv0_ref, mv1_ref, mask0_ref, mask1_ref, loc_ref, rem_ref, ol_ref, ox_ref, wo_ref, rq_ref, rk_ref,
                    dq_ref, dk_ref, dv_ref, diag_ref, dgate_ref, t_ref, g_ref, ak, av, gm_ref, *, part):
    seg = q_ref.shape[0] // 2
    s = gate_ref[2 * pl.program_id(0) + part]
    t_ref[...] = spread(base_ref[...], BLK)
    g_ref[...] = jnp.zeros_like(g_ref)
    ak[...] = jnp.zeros_like(ak)
    av[...] = jnp.zeros_like(av)
    wo = wo_ref[...]
    gm_ref[pl.ds(pl.multiple_of(at_ref[2] * seg, seg), seg), :] = nt(ol_ref[...], wo)
    gm_ref[pl.ds(pl.multiple_of((1 - at_ref[2]) * seg, seg), seg), :] = nt(ox_ref[...], wo)
    heat = 16.0 * LOG2E
    nb = seg // BLK
    mk = jnp.concatenate([mk0_ref[...].reshape(-1, 128), mk1_ref[...].reshape(-1, 128)]).astype(f32)
    mk = (mk * lax.rsqrt(jnp.sum(mk * mk, axis=1, keepdims=True) + 1e-06)).astype(bf16)
    mv = jnp.concatenate([mv0_ref[...].reshape(-1, 128), mv1_ref[...].reshape(-1, 128)])
    dg = jnp.zeros((BLK, 1), f32)
    for u in range(2):
        keep = jnp.where(reset_ref[u] == 0, 1.0, 0.0).astype(f32)
        old = slice(u * seg, (u + 1) * seg)
        kp = k_ref[old, :]
        vp = v_ref[old, :]
        for i in range(nb):
            rows = slice(u * seg + i * BLK, u * seg + (i + 1) * BLK)
            q = q_ref[rows, :]
            gm = gm_ref[rows, :]
            off = (nb - 1 - i) * BLK
            cw = (i + 1) * BLK
            cur = slice((u + 1) * seg, (u + 1) * seg + cw)
            kc = k_ref[cur, :]
            vc = v_ref[cur, :]
            al = jnp.sum(gm * loc_ref[rows, :].astype(f32), axis=1, keepdims=True)
            ar = jnp.sum(gm * rem_ref[rows, :].astype(f32), axis=1, keepdims=True)
            dg = dg + (ar - al)
            gl = ((1.0 - s) * gm).astype(bf16)
            gr = (s * gm).astype(bf16)
            ep = jnp.exp2(nt(q, kp) * heat + t_ref[:, off : off + seg])
            ec = jnp.exp2(nt(q, kc) * heat + t_ref[:, off + seg : off + seg + cw])
            l = keep * jnp.sum(ep, axis=1, keepdims=True) + jnp.sum(ec, axis=1, keepdims=True)
            il = 1.0 / l
            pp = ep * (il * keep)
            pc = ec * il
            wp = pp * nt(gl, vp)
            wc = pc * nt(gl, vc)
            dl = jnp.sum(wp, axis=1, keepdims=True) + jnp.sum(wc, axis=1, keepdims=True)
            dsp = (wp - pp * dl).astype(bf16)
            dsc = (wc - pc * dl).astype(bf16)
            g_ref[:, off : off + seg] += dsp.astype(f32)
            g_ref[:, off + seg : off + seg + cw] += dsc.astype(f32)
            dq = nn(dsp, kp) + nn(dsc, kc)
            ak[old, :] += tn(dsp, q)
            ak[cur, :] += tn(dsc, q)
            av[old, :] += tn(pp.astype(bf16), gl)
            av[cur, :] += tn(pc.astype(bf16), gl)
            em = jnp.exp2(nt(mk, q) * heat) * (mask0_ref, mask1_ref)[u][:, i * BLK : (i + 1) * BLK].astype(f32)
            em = em * (1.0 / jnp.sum(em, axis=0, keepdims=True))
            gw = nt(mv, gr)
            dsm = em * (gw - jnp.sum(em * gw, axis=0, keepdims=True))
            dq = dq + tn(dsm.astype(bf16), mk)
            dq_ref[rows, :] = unit_back(16.0 * dq, q, rq_ref[rows, :])
    dk_ref[...] = unit_back(16.0 * ak[...], k_ref[...], rk_ref[...])
    dv_ref[...] = av[...].astype(bf16)
    diag_ref[...] = gather_diagonals(g_ref[...])
    dgate_ref[...] = jnp.broadcast_to(jnp.sum(dg) * s * (1.0 - s), dgate_ref.shape)


def attend_back(part, gate, reset, at, q, k, v, base, pack, masks, loc, rem, ol, ox, wo, rq, rk):
    seg, half = q.shape[0] // 2, q.shape[1]
    mem, wt = masks[0].shape[1], base.shape[2]
    width = ol.shape[1]
    col = lambda n: pl.BlockSpec((n * seg, 128), lambda h, *_: (0, h))
    head = lambda h: 2 * h + part
    col_in = lambda n: pl.BlockSpec((n * seg, 128), lambda h, *_: (0, head(h)))
    row = lambda w: pl.BlockSpec((None, 1, w), lambda h, *_: (h, 0, 0))
    rcol = lambda n: pl.BlockSpec((None, n * seg, 1), lambda h, *_: (head(h), 0, 0))
    sd = jax.ShapeDtypeStruct
    return pl.pallas_call(
        functools.partial(attn_bwd_kernel, part=part),
        grid_spec=pltpu.PrefetchScalarGridSpec(
            num_scalar_prefetch=3, grid=(2,),
            in_specs=head_specs(seg, mem, wt, head) + [col_in(2), col_in(2), pl.BlockSpec((seg, width), lambda h, *_: (0, 0), pipeline_mode=pl.Buffered(1)), pl.BlockSpec((seg, width), lambda h, *_: (0, 0), pipeline_mode=pl.Buffered(1)),
                      pl.BlockSpec((128, width), lambda h, g, r, at: (4 * at[2] + head(h), 0)), rcol(2), rcol(3)],
            out_specs=[col(2), col(3), col(3), row(wt), row(128)],
            scratch_shapes=[pltpu.VMEM((BLK, wt), f32)] * 2 + [pltpu.VMEM((3 * seg, 128), f32)] * 2 + [pltpu.VMEM((2 * seg, 128), f32)]),
        out_shape=[sd((2 * seg, half // 2), bf16), sd((3 * seg, half // 2), bf16), sd((3 * seg, half // 2), bf16), sd((2, 1, wt), f32), sd((2, 1, 128), f32)],
        compiler_params=pltpu.CompilerParams(vmem_limit_bytes=48 << 20),
        cost_estimate=pl.CostEstimate(flops=8 * seg * (2 * seg + mem) * 10 * 128, bytes_accessed=30 << 20, transcendentals=8 * seg * (2 * seg + mem)),
    )(gate, reset, at, q, k, v, base, *pack, *pack, *masks, loc, rem, ol, ox, wo, rq, rk)


def ffn_kernel(at_ref, *refs, first):
    refs = list(refs)
    if first:
        ao_ref, ax_ref, tok_ref, tokx_ref, gain_ref, shift_ref, other_ref = refs[:7]
        refs = refs[7:]
    else:
        lo_ref, oi_ref, gi_ref = refs[:3]
        refs = refs[3:]
    cot_ref, cotx_ref, bu_ref = refs[:3]
    pieces = refs[3:11]
    refs = refs[11:]
    if first:
        lowo_ref, res_ref, o_ref, g_ref, wout_ref = refs[:5]
        refs = refs[5:]
    else:
        oo_ref, ox_ref, go_ref, gx_ref = refs[:4]
        refs = refs[4:]
    oa_ref, xa_ref, ob_ref, yb_ref, gbu_ref, up_s, dn_s, low_s, cot_s, act_s, gp_s, sem, osem, tmp = refs[:14]
    i = pl.program_id(0)
    rb, width = cot_ref.shape
    rows = pl.ds(pl.multiple_of(i * rb, rb), rb)
    q4 = 256
    copies = []
    for kind, slot, chip, quarter in piece_places(at_ref):
        where = (pl.ds(pl.multiple_of(chip * 128, 128), 128), pl.ds(pl.multiple_of(quarter * q4, q4), q4))
        for w, dst in enumerate((up_s, dn_s)):
            copies.append(pltpu.make_async_copy(pieces[kind].at[slot, pl.ds(w * 128, 128)], dst.at[where], sem))
    outs = []
    if first:
        wout_s = refs[14]
        c = at_ref[2]
        for whose, cc in ((0, c), (1, 1 - c)):
            for kind, slot, chip, quarter in piece_places(at_ref):
                for core in range(2):
                    src = pieces[kind].at[slot, pl.ds(256, 64), pl.ds(core * 128, 128)] if whose == 0 else other_ref.at[kind * 4 + slot, :, pl.ds(core * 128, 128)]
                    dst = wout_s.at[pl.ds(pl.multiple_of(chip * 128 + core * 64, 64), 64), pl.ds(pl.multiple_of((4 * cc + quarter) * 128, 128), 128)]
                    outs.append(pltpu.make_async_copy(src, dst, osem.at[0]))
        keep = pltpu.make_async_copy(wout_s, wout_ref, osem.at[1])

    @pl.when(i == 0)
    def _():
        for copy in outs + copies:
            copy.start()
        for copy in outs:
            copy.wait()
        if first:
            keep.start()

    if first:
        half_w = ao_ref.shape[1]
        wrow = lambda cc: wout_s[pl.ds(pl.multiple_of(cc * half_w, half_w), half_w), :]
        res = jnp.where(i < 2, tok_ref[...].astype(f32), tokx_ref[...].astype(f32)) + nn(ao_ref[...], wrow(c)) + nn(ax_ref[...], wrow(1 - c))
        n, r = norm_stats(res)
        low = (n * gain_ref[...].astype(f32) + shift_ref[...].astype(f32)).astype(bf16)
        lowo_ref[...] = low

        @pl.when(i < 2)
        def _():
            res_ref[...] = res
    else:
        low = lo_ref[...]
    low_s[rows, :] = low
    cot = jnp.where(i < 2, cot_ref[...].astype(f32), cotx_ref[...].astype(f32)).astype(bf16)
    cot_s[rows, :] = cot

    @pl.when(i == 0)
    def _():
        for copy in copies:
            copy.wait()

    p = nn(low, up_s[...]) + bu_ref[...].astype(f32)
    ga = nt(cot, dn_s[...])
    k0 = math.sqrt(2.0 / math.pi)
    p2_ = p * p
    t = jnp.tanh(p * (k0 + (k0 * 0.044715) * p2_))
    half = 0.5 * (1.0 + t)
    act = (p * half).astype(bf16)
    slope = half + 0.5 * p * (1.0 - t * t) * (k0 + (3.0 * k0 * 0.044715) * p2_)
    gp = (ga * slope).astype(bf16)
    act_s[rows, :] = act
    gp_s[rows, :] = gp
    o = nn(act, dn_s[...])
    g = nt(gp, up_s[...])
    if first:
        o_ref[...] = o
        g_ref[...] = g
    else:
        o = o + oi_ref[...]
        g = g + gi_ref[...]

        @pl.when(i < 2)
        def _():
            oo_ref[...] = o
            go_ref[...] = g

        @pl.when(i >= 2)
        def _():
            ox_ref[...] = o.astype(bf16)
            gx_ref[...] = g.astype(bf16)

    @pl.when(i == pl.num_programs(0) - 1)
    def _():
        z, y, x = at_ref[0], at_ref[1], at_ref[3]
        for part in range(2):
            for xr in range(2):
                cols = pl.ds(pl.multiple_of((2 * (x ^ xr) + part) * q4, q4), q4)
                for w, (left, right) in enumerate(((low_s, gp_s), (act_s, cot_s))):
                    tmp[w] = tn(left[...], right[:, cols]).astype(bf16)
                    for yr in range(2):
                        dst = ((oa_ref, xa_ref)[xr], yr) if part == 0 else ((ob_ref, yb_ref)[yr], xr)
                        for k in range(4):
                            chip = (z ^ k) * 2 + (y ^ yr)
                            dst[0][dst[1], w, k] = tmp[w, pl.ds(pl.multiple_of(chip * 128, 128), 128), :]
        if first:
            keep.wait()
        gbu_ref[...] = jnp.broadcast_to(jnp.sum(gp_s[...].astype(f32), axis=0, keepdims=True), gbu_ref.shape)


def ffn_half(at, first, ins, cot, cotx, bu, pieces):
    seg, width = cot.shape
    pair = 2 * seg
    rb = 256
    once = dict(pipeline_mode=pl.Buffered(1))
    there = lambda w: pl.BlockSpec((rb, w), lambda i, at: ((i + 2 * at[2]) % 4, 0))
    here = lambda w: pl.BlockSpec((rb, w), lambda i, at: (i, 0))
    own = pl.BlockSpec((rb, width), lambda i, at: (jnp.minimum(i, 1), 0))
    other = pl.BlockSpec((rb, width), lambda i, at: (jnp.maximum(i - 2, 0), 0))
    vec = pl.BlockSpec((1, width), lambda i, at: (0, 0))
    hbm = pl.BlockSpec(memory_space=pltpu.HBM)
    sd = jax.ShapeDtypeStruct
    half = width // 2
    if first:
        in_specs = [there(half), there(half), own, other, vec, vec, hbm]
        out_specs = [here(width), own, here(width), here(width), hbm]
        out_shape = [sd((pair, width), bf16), sd((seg, width), f32), sd((pair, width), f32), sd((pair, width), f32), sd((width, width), bf16)]
    else:
        in_specs = [here(width)] * 3
        out_specs = [own, other, own, other]
        out_shape = [sd((seg, width), f32), sd((seg, width), bf16), sd((seg, width), f32), sd((seg, width), bf16)]
    ff = bu.shape[1]
    grads = pl.BlockSpec((2, 2, 4, 128, 256), lambda i, at: (0, 0, 0, 0, 0), **once)
    return pl.pallas_call(
        functools.partial(ffn_kernel, first=first),
        grid_spec=pltpu.PrefetchScalarGridSpec(
            num_scalar_prefetch=1, grid=(4,),
            in_specs=in_specs + [own, other, vec] + [hbm] * 8,
            out_specs=out_specs + [grads] * 4 + [pl.BlockSpec((8, ff), lambda i, at: (0, 0))],
            scratch_shapes=[pltpu.VMEM((width, ff), bf16)] * 2 + [pltpu.VMEM((pair, width), bf16)] * 2 + [pltpu.VMEM((pair, ff), bf16)] * 2 + [pltpu.SemaphoreType.DMA, pltpu.SemaphoreType.DMA((2,)), pltpu.VMEM((2, width, 256), bf16)]
            + ([pltpu.VMEM((width, width), bf16)] if first else [])),
        out_shape=out_shape + [sd((2, 2, 4, 128, 256), bf16)] * 4 + [sd((8, ff), f32)],
        compiler_params=pltpu.CompilerParams(vmem_limit_bytes=56 << 20),
        cost_estimate=pl.CostEstimate(flops=2 * pair * width * ff * 6, bytes_accessed=30 << 20, transcendentals=pair * ff),
    )(at, *ins, cot, cotx, bu, *pieces)


def rows_kernel(*refs):
    pieces, out, buf, sem, osem = refs[:8], refs[8], refs[9], refs[10], refs[11]
    n = out.shape[1]
    copies = [pltpu.make_async_copy(v.at[:, pl.ds(256, n)], buf.at[pl.ds(4 * k, 4)], sem) for k, v in enumerate(pieces)]
    for copy in copies:
        copy.start()
    for copy in copies:
        copy.wait()
    done = pltpu.make_async_copy(buf, out, osem)
    done.start()
    done.wait()


def out_rows_of(pieces):
    n, cols = min(v.shape[1] for v in pieces) - 256, pieces[0].shape[2]
    hbm = pl.BlockSpec(memory_space=pltpu.HBM)
    return pl.pallas_call(
        rows_kernel,
        in_specs=[hbm] * 8,
        out_specs=hbm,
        out_shape=jax.ShapeDtypeStruct((32, n, cols), bf16),
        scratch_shapes=[pltpu.VMEM((32, n, cols), bf16), pltpu.SemaphoreType.DMA, pltpu.SemaphoreType.DMA],
        cost_estimate=pl.CostEstimate(flops=0, bytes_accessed=2 << 20, transcendentals=0),
    )(*pieces)


def join_kernel(res_ref, oo_ref, ox_ref, go_ref, gx_ref, cot_ref, gain_ref, bd_ref, out_ref, one_ref, ol_ref, vec_ref):
    res = res_ref[...]
    out_ref[...] = (res + oo_ref[...] + ox_ref[...].astype(f32) + bd_ref[...].astype(f32)).astype(bf16)
    gh = go_ref[...] + gx_ref[...].astype(f32)
    n, r = norm_stats(res)
    cf = cot_ref[...].astype(f32)
    one = cf + norm_back(gh, n, r, gain_ref[...].astype(f32))
    one_ref[...] = one
    ol_ref[...] = one.astype(bf16)

    @pl.when(pl.program_id(0) == 0)
    def _():
        vec_ref[...] = jnp.zeros_like(vec_ref)

    vec_ref[0:1, :] += jnp.sum(gh * n, axis=0, keepdims=True)
    vec_ref[1:2, :] += jnp.sum(gh, axis=0, keepdims=True)
    vec_ref[2:3, :] += jnp.sum(cf, axis=0, keepdims=True)


def join(res, oo, ox, go, gx, cot, gain, bd):
    seg, width = res.shape
    blk = pl.BlockSpec((128, width), lambda i: (i, 0))
    vec = pl.BlockSpec((1, width), lambda i: (0, 0))
    sd = jax.ShapeDtypeStruct
    return pl.pallas_call(
        join_kernel,
        grid=(seg // 128,),
        in_specs=[blk] * 6 + [vec, vec],
        out_specs=[blk, blk, blk, pl.BlockSpec((8, width), lambda i: (0, 0))],
        out_shape=[sd((seg, width), bf16), sd((seg, width), f32), sd((seg, width), bf16), sd((8, width), f32)],
        cost_estimate=pl.CostEstimate(flops=40 * seg * width, bytes_accessed=24 * seg * width, transcendentals=0),
    )(res, oo, ox, go, gx, cot, gain, bd)


def rows_by_head(refs):
    a, b = refs[0][...], refs[1][...]
    return jnp.concatenate([a[:, :128], b[:, :128], a[:, 128:], b[:, 128:]], axis=1)


def before_kernel(ka_ref, kb_ref, va_ref, vb_ref, wk_ref, wv_ref, o_ref):
    o_ref[...] = (nt(rows_by_head((ka_ref, kb_ref)), wk_ref[...]) + nt(rows_by_head((va_ref, vb_ref)), wv_ref[...])).astype(bf16)


def before_grad(dk, dv, w):
    seg, half = dk[0].shape[0] // 3, dk[0].shape[1] * 2
    width = w.shape[0]
    rb = 256
    d = pl.BlockSpec((rb, half // 2), lambda i: (i, 0))
    wb = lambda k: pl.BlockSpec((width, half), lambda i: (0, k))
    return pl.pallas_call(
        before_kernel,
        grid=(seg // rb,),
        in_specs=[d] * 4 + [wb(1), wb(2)],
        out_specs=pl.BlockSpec((rb, width), lambda i: (i, 0)),
        out_shape=jax.ShapeDtypeStruct((seg, width), bf16),
        cost_estimate=pl.CostEstimate(flops=4 * seg * half * width, bytes_accessed=4 << 20, transcendentals=0),
        compiler_params=pltpu.CompilerParams(vmem_limit_bytes=32 << 20),
    )(*dk, *dv, w, w)


def wgrad_kernel(at_ref, x_ref, dq_ref, dk_ref, dv_ref, att_ref, attx_ref, ol_ref, olx_ref, oa_ref, xa_ref, ob_ref, yb_ref, tmp, ol_s, *, pair):
    seg = dk_ref.shape[0] // 3
    z, y, c, x = at_ref[0], at_ref[1], at_ref[2], at_ref[3]
    for xr in range(2):
        cols = pl.ds(pl.multiple_of((x ^ xr) * 128, 128), 128)
        tmp[:, :128] = tn(x_ref[seg:, :], dq_ref[:, cols]).astype(bf16)
        tmp[:, 128:384] = tn(x_ref[...], jnp.concatenate([dk_ref[:, cols], dv_ref[:, cols]], axis=1)).astype(bf16)
        ocols = pl.ds(pl.multiple_of((4 * c + 2 * (x ^ xr) + pair) * 128, 128), 128)
        ol_s[pl.ds(pl.multiple_of(c * seg, seg), seg), :] = ol_ref[:, ocols]
        ol_s[pl.ds(pl.multiple_of((1 - c) * seg, seg), seg), :] = olx_ref[:, ocols]
        half = att_ref.shape[1]
        tmp[pl.ds(pl.multiple_of(c * half, half), half), 384:] = tn(att_ref[...], ol_s[...]).astype(bf16)
        tmp[pl.ds(pl.multiple_of((1 - c) * half, half), half), 384:] = tn(attx_ref[...], ol_s[...]).astype(bf16)
        for part in range(2):
            for yr in range(2):
                dst = ((oa_ref, xa_ref)[xr], yr) if part == 0 else ((ob_ref, yb_ref)[yr], xr)
                for k in range(4):
                    row = ((z ^ k) * 2 + (y ^ yr)) * 128 + part * 64
                    dst[0][dst[1], 0, k] = tmp[pl.ds(pl.multiple_of(row, 64), 64), :]


def qkv_wgrad(pair, at, x, dq, dk, dv, att, attx, ol, olx):
    n, width = x.shape
    vm = pl.BlockSpec(memory_space=pltpu.VMEM)
    return pl.pallas_call(
        functools.partial(wgrad_kernel, pair=pair),
        in_specs=[pl.BlockSpec(memory_space=pltpu.SMEM)] + [vm] * 8,
        out_specs=[vm] * 4,
        out_shape=[jax.ShapeDtypeStruct((2, 1, 4, 64, 512), bf16)] * 4,
        scratch_shapes=[pltpu.VMEM((width, 512), bf16), pltpu.VMEM((att.shape[0], 128), bf16)],
        compiler_params=pltpu.CompilerParams(vmem_limit_bytes=32 << 20),
        cost_estimate=pl.CostEstimate(flops=2 * n * width * 768, bytes_accessed=12 << 20, transcendentals=0),
    )(at, x, dq, dk, dv, att, attx, ol, olx)


def hgrad_kernel(at_ref, qa_ref, qb_ref, ka_ref, kb_ref, va_ref, vb_ref, wq_ref, wk_ref, wv_ref, back_ref, ho_ref, hx_ref):
    i = pl.program_id(0)
    c = at_ref[2]
    g = nt(rows_by_head((qa_ref, qb_ref)), wq_ref[...]) + nt(rows_by_head((ka_ref, kb_ref)), wk_ref[...]) + nt(rows_by_head((va_ref, vb_ref)), wv_ref[...])
    mine = jnp.where((i + 2 * c) % 4 == 2 + c, 1.0, 0.0).astype(f32)
    g = g + mine * back_ref[...].astype(f32)

    @pl.when(i < 2)
    def _():
        ho_ref[...] = g

    @pl.when(i >= 2)
    def _():
        hx_ref[...] = g.astype(bf16)


def hgrad(at, dq, dk, dv, w, back):
    pair, half = dq[0].shape[0], dq[0].shape[1] * 2
    seg, width = pair // 2, w.shape[0]
    rb = 256
    once = dict(pipeline_mode=pl.Buffered(1))
    wb = lambda k: pl.BlockSpec((width, half), lambda i, at: (0, k), **once)
    sd = jax.ShapeDtypeStruct
    return pl.pallas_call(
        hgrad_kernel,
        grid_spec=pltpu.PrefetchScalarGridSpec(
            num_scalar_prefetch=1, grid=(4,),
            in_specs=[pl.BlockSpec((rb, half // 2), lambda i, at: ((i + 2 * at[2]) % 4, 0))] * 2 + [pl.BlockSpec((rb, half // 2), lambda i, at: (2 + (i + 2 * at[2]) % 4, 0))] * 4
            + [wb(0), wb(1), wb(2), pl.BlockSpec((rb, width), lambda i, at: (0, 0))],
            out_specs=[pl.BlockSpec((rb, width), lambda i, at: (jnp.minimum(i, 1), 0)), pl.BlockSpec((rb, width), lambda i, at: (jnp.maximum(i - 2, 0), 0))]),
        out_shape=[sd((seg, width), f32), sd((seg, width), bf16)],
        compiler_params=pltpu.CompilerParams(vmem_limit_bytes=32 << 20),
        cost_estimate=pl.CostEstimate(flops=6 * pair * half * width, bytes_accessed=12 << 20, transcendentals=0),
    )(at, *dq, *dk, *dv, w, w, w, back)


def gather_z(own, steps):
    return [send_z(own, k) for k in steps]


def columns(got, cuts):
    return [jnp.stack([g[lo:hi] for g in got]) for lo, hi in cuts]


def scatter_one(g):
    return send_x(g[1]), send_y(g[3])


def two_blocks(g, one):
    return add_low(g[0][1], one[0][1]), add_low(g[2][1], one[1][1])


def scatter_two(blocks):
    return send_y(blocks[0]), send_x(blocks[1])


def scatter_total(g, one, two):
    total = lambda u, v, w: (u.astype(f32) + v.astype(f32) + w.astype(f32)).astype(bf16)
    a, b = total(g[0][0], one[0][0], two[0]), total(g[2][0], one[1][0], two[1])
    return [jnp.stack([a[:, k], b[:, k]]) for k in range(4)]


def scatter_z(v):
    return [send_z(v[k], k) for k in range(1, 4)]


def z_sum(v, got):
    total = v[0].astype(f32)
    for g in got:
        total = total + g.astype(f32)
    return total.astype(bf16)


def scatter_x(total, other):
    x = lax.axis_index("stream")
    return jnp.concatenate([jnp.where(x == 0, total, other), jnp.where(x == 0, other, total)])


def local_pair(
    tokens, resets, retrieved, memory_keys, memory_values, qkv_weight, out_weight, up_weight, up_bias,
    down_weight, down_bias, attn_gain, attn_shift, ffn_gain, ffn_shift, position_bias, memory_gate, cotangent,
):
    heads = memory_gate.shape[0]
    seg, width = tokens.shape[1:]
    dh = width // heads
    shards = lax.axis_size("fsdp")
    chips = shards // 2
    mem_rows = memory_keys.shape[1]
    mem = mem_rows * shards
    nz, z, y, c, x = places()
    at = jnp.stack([z, y, c, x]).astype(jnp.int32)
    low_core = c == 0
    both = lambda own, other: (jnp.where(low_core, own, other), jnp.where(low_core, other, own))
    tok, cot = tokens[0], cotangent[0]
    part = width // shards
    vectors = [up_bias, down_bias, attn_gain, attn_shift, ffn_gain, ffn_shift, position_bias]
    sizes = [v.shape[0] for v in vectors]
    tok_other, cot_other = send_core(tok), send_core(cot)
    ret = jnp.transpose(retrieved[0], (1, 2, 0)).reshape(2, 4, retrieved.shape[3], seg)
    p0, p1 = both(take(ret, c, 0), send_core(take(ret, 1 - c, 0)))
    q_own, q_swap, r_own, r_swap, d_own = prepare(
        at, resets, qkv_weight, up_weight, down_weight, out_weight, memory_keys[0], memory_values[0], vectors)
    q_got, r_got = send_core(q_swap), send_core(r_swap)
    hot, rel = bucket_hot(seg)
    gate = lax.dynamic_slice_in_dim(jax.nn.sigmoid(memory_gate.astype(f32)), 4 * c, 4, 0)
    q0, q1 = both(q_own, q_got)
    own_qkv = jnp.concatenate([q0[:64], q1[:64], q0[128:], q1[128:], q0[64:128], q1[64:128]])
    reset = jnp.stack([q0[135, 0], q1[135, 0]]).astype(jnp.int32)
    second = jnp.where(low_core, tok_other, tok)
    own_qkv, r_got, tok, tok_other, cot_other, p0, p1 = fence(own_qkv, r_got, tok, tok_other, cot_other, p0, p1)
    g0 = [own_qkv] + gather_z(own_qkv, (1, 2, 3))
    ty = lax.ppermute(tok, "fsdp", [(i, i ^ 2) for i in range(1, shards, 2)])
    masks = (hit_masks(at, p0, mem), hit_masks(at, p1, mem))
    own_f1, own_f2 = pack_ffn(at, r_own, r_got, d_own, mem_rows)
    g0, masks, own_f1, own_f2, ty = fence(g0, masks, own_f1, own_f2, ty)
    a, b = columns(g0, ((0, 144), (144, 272)))
    a, b, own_f1 = fence(a, b, own_f1)
    ya, xb, xa, yb = send_y(a), send_x(b), send_x(a), send_y(b)
    z2 = send_z(own_f1, 2)
    a, ya, xb, b, xa, yb, z2, own_f1, ty = fence(a, ya, xb, b, xa, yb, z2, own_f1, ty)
    g0 = [a, ya, xa, send_x(ya), b, xb, yb, send_y(xb)]
    f1 = [own_f1, send_z(own_f1, 1), z2, send_z(own_f1, 3)]
    tz = lax.ppermute(ty, "fsdp", [(i, i + 4) for i in range(1, shards - 4, 4)])
    small = jnp.stack([a[:, 128:, :256], ya[:, 128:, :256]]).reshape(2, 2, 2, 16, 256)
    for axis, bit in enumerate((y, z // 2, z % 2)):
        small = jnp.where(bit == 1, jnp.flip(small, axis), small)
    small = jnp.transpose(small.reshape(2, 4, 16, 256), (1, 0, 2, 3)).reshape(shards, 8, 256)
    cols = [small[:, k, :s] for k, s in enumerate(sizes)]
    b_down, gain_one, shift_one, gain_two, shift_two = [v.reshape(1, -1) for v in cols[1:6]]
    b_up = take(cols[0].reshape(chips, 2, 2, 128), c, 1)
    b_up = [b_up[:, k].reshape(1, -1) for k in range(2)]
    table = lax.dynamic_slice_in_dim(cols[6].reshape(heads, -1).astype(f32), 4 * c, 4, 0)
    base = diagonal_bias(table, hot, rel)
    g0, ty, tz, f1, own_f2, base, b_up, gain_one, shift_one, b_down, gain_two, shift_two = fence(
        g0, ty, tz, f1, own_f2, base, b_up, gain_one, shift_one, b_down, gain_two, shift_two)
    tp = jnp.where(y == 0, tz, ty)
    tp = jnp.where(low_core, lax.ppermute(tp, "fsdp", [(i, i - 1) for i in range(1, shards, 2)]), tp)
    a, b = columns(f1, ((0, 448), (448, 768)))
    a, b, tp = fence(a, b, tp)
    ya, xb = send_y(a), send_x(b)
    f2 = [own_f2] + gather_z(own_f2, (1, 2))
    q, k, v, rq, rk, xn, w_qkv = project_pair(at, tp, tok, tok_other, gain_one, shift_one, g0)
    q, k, v, a, b, ya, xb, f2 = fence(q, k, v, a, b, ya, xb, f2)
    pack = (a, ya)
    xa, xra, q = fence(a[:, :320], ya[:, :320], q)
    f1 = [a, ya, send_x(xa), send_x(xra), b, xb, send_y(b), send_y(xb)]
    f2 = f2 + gather_z(f2[0], (3,))
    att, loc, rem = attend(gate, reset, at, q, k, v, base, pack, masks)
    att, f1, f2 = fence(att, f1, f2)
    att_other = send_core(att)
    out_other = out_rows_of(f1)
    a, b = columns(f2, ((0, 256), (256, 512)))
    att_other, out_other, a, b = fence(att_other, out_other, a, b)
    out_other = send_core(out_other)
    ya, xb = send_y(a), send_x(b)
    att_other, out_other, f1, a, b, ya, xb = fence(att_other, out_other, f1, a, b, ya, xb)
    f2 = [a, ya, send_x(a), send_x(ya), b, xb, send_y(b), send_y(xb)]
    low, res, o1, h1, w_out, *n1, gbu1 = ffn_half(at, True, (att, att_other, tok, tok_other, gain_two, shift_two, out_other), cot, cot_other, b_up[0], f1)
    low, o1, h1, n1, f2 = fence(low, o1, h1, n1, f2)
    s1 = scatter_one(n1)
    oo, ox, go, gx, *n2, gbu2 = ffn_half(at, False, (low, o1, h1), cot, cot_other, b_up[1], f2)
    gx, ox, s1, n2, oo, go = fence(gx, ox, s1, n2, oo, go)
    gx, ox, w1 = send_core(gx), send_core(ox), two_blocks(n1, s1)
    gx, ox, w1 = fence(gx, ox, w1)
    u1 = scatter_two(w1)
    output, one, ol, vec_two = join(res, oo, ox, go, gx, cot, gain_two, b_down)
    ol, u1 = fence(ol, u1)
    ol_other = send_core(ol)
    v1 = scatter_total(n1, s1, u1)
    ol_other, ol, v1, n2 = fence(ol_other, ol, v1, n2)
    s2 = scatter_one(n2)
    z1 = scatter_z(v1)
    dqa, dka, dva, diag_a, dgate_a = attend_back(0, gate, reset, at, q, k, v, base, pack, masks, loc, rem, ol, ol_other, w_out, rq, rk)
    dqa, dka, dva, s2, z1, ol, diag_a, dgate_a = fence(dqa, dka, dva, s2, z1, ol, diag_a, dgate_a)
    w2, dqa, ol = fence(two_blocks(n2, s2), dqa, ol)
    u2 = scatter_two(w2)
    na = qkv_wgrad(0, at, xn, dqa, dka, dva, att, att_other, ol, ol_other)
    na, u2, ol = fence(na, u2, ol)
    v2, t1, ol = fence(scatter_total(n2, s2, u2), z_sum(v1, z1), ol)
    sa = scatter_one(na)
    z2 = scatter_z(v2)
    dqb, dkb, dvb, diag_b, dgate_b = attend_back(1, gate, reset, at, q, k, v, base, pack, masks, loc, rem, ol, ol_other, w_out, rq, rk)
    dqb, dkb, dvb, sa, z2, diag_b, dgate_b = fence(dqb, dkb, dvb, sa, z2, diag_b, dgate_b)
    wa, dkb, t1 = fence(two_blocks(na, sa), dkb, t1)
    ua = scatter_two(wa)
    x1 = send_x(t1)
    back = before_grad((dka, dkb), (dva, dvb), w_qkv).reshape(2, seg // 2, width)
    back_out, dqb = fence(take(back, 1 - c, 0), dqb)
    back_got = send_core(back_out)
    nb = qkv_wgrad(1, at, xn, dqb, dkb, dvb, att, att_other, ol, ol_other)
    nb, back, back_got, ua, x1, z2 = fence(nb, back, back_got, ua, x1, z2)
    va, back, nb = fence(scatter_total(na, sa, ua), add_low(take(back, c, 0), back_got), nb)
    sb = scatter_one(nb)
    back = lax.ppermute(back, "fsdp", [(i, i - 2) for i in range(2, shards)])
    t2 = z_sum(v2, z2)
    sb, t2, va, back = fence(sb, t2, va, back)
    wb, va, t2, back = fence(two_blocks(nb, sb), va, t2, back)
    ub = scatter_two(wb)
    za = scatter_z(va)
    ho, hx = hgrad(at, (dqa, dqb), (dka, dkb), (dva, dvb), w_qkv, back)
    ub, za, hx, ho, t2 = fence(ub, za, hx, ho, t2)
    vb, hx, t2 = fence(scatter_total(nb, sb, ub), hx, t2)
    hx = send_core(hx)
    zb = scatter_z(vb)
    x2 = send_x(t2)
    token_grad, vec_one = finish(ho, hx, tok, one, gain_one)
    zb, x2, vec_one, diag_a, diag_b, dgate_a, dgate_b, gbu1, gbu2, vec_two = fence(zb, x2, vec_one, diag_a, diag_b, dgate_a, dgate_b, gbu1, gbu2, vec_two)
    t_ab = jnp.concatenate([z_sum(va, za), z_sum(vb, zb)], axis=1)
    x_ab = send_x(t_ab)
    t_f1, t_f2 = scatter_x(t1, x1), scatter_x(t2, x2)
    by_head = lambda a, b: jnp.stack([a, b], axis=1).reshape((4,) + a.shape[1:])
    diag, dgate = by_head(diag_a, diag_b), by_head(dgate_a, dgate_b)
    mine_core = jnp.arange(2) == c
    gbu = jnp.stack([gbu1[0].reshape(chips, 128), gbu2[0].reshape(chips, 128)], axis=1)
    gbu = jnp.where(mine_core[None, :, None, None], gbu[:, None], 0.0).reshape(shards, -1)
    table_g = jnp.dot(diag[:, 0], hot.T, precision=lax.Precision.HIGHEST)
    table_g = jnp.where(mine_core[:, None, None], table_g[None], 0.0).reshape(shards, -1)
    gate_g = jnp.where(mine_core[:, None], dgate[:, 0, 0][None], 0.0).reshape(1, heads)
    up_sum = jnp.stack([t_f1[:, 0], t_f2[:, 0]]).reshape(2, 4, 2, 64, 256)
    up_got = send_core(take(up_sum, 1 - c, 2))
    x_ab, up_got = fence(x_ab, up_got)
    t_qkv = jnp.transpose(scatter_x(t_ab, x_ab).reshape(2, 2, 2, 64, 512), (0, 2, 1, 3, 4))
    qkv_sum = t_qkv.reshape(4, 2, 64, 512)
    qkv_got = send_core(take(qkv_sum, 1 - c, 1))
    pack = [gbu] + [v.reshape(shards, -1) for v in (vec_two[2], vec_one[0], vec_one[1], vec_two[0], vec_two[1])] + [table_g, jnp.broadcast_to(gate_g, (shards, heads))]
    total = jnp.concatenate(pack, axis=1)
    total = total + send_core(total)
    diagonal = lax.ppermute(total, ("stream", "fsdp"), [(s * shards + i, (1 - s) * shards + (i ^ 2)) for s in range(2) for i in range(shards)])
    total = (total + send_y(total)) + (send_x(total) + diagonal)
    total = (total + send_z(total, 1)) + (send_z(total, 2) + send_z(total, 3))
    total = take(total, lax.axis_index("fsdp"), 0)
    up_all = jnp.stack(both(take(up_sum, c, 2), up_got)).astype(f32)
    up_t = jnp.concatenate([up_all[cc, hf, q_, :, yy * 128 : (yy + 1) * 128] for q_ in range(4) for yy in range(2) for cc in range(2) for hf in range(2)], axis=1)
    down_t = jnp.concatenate([jnp.concatenate([t[q_, 1] for q_ in range(4)], axis=1) for t in (t_f1, t_f2)], axis=0).astype(f32)
    qkv_all = jnp.stack(both(take(qkv_sum, c, 1), qkv_got)).astype(f32)
    qkv_t = jnp.concatenate([qkv_all[cc, h, :, p * dh : (p + 1) * dh] for p in range(3) for cc in range(2) for h in range(4)], axis=1)
    out_t = jnp.concatenate([qkv_all[cc, h, :, 3 * dh :] for cc in range(2) for h in range(4)], axis=1)
    outs, off = [], 0
    for s in sizes + [heads]:
        outs.append(total[off : off + s])
        off += s
    ub, db, ag, ash, fg, fs, pg, gg = outs
    return output[None], token_grad[None], qkv_t, out_t, up_t, ub, down_t, db, ag, ash, fg, fs, pg, gg


def solution(mesh):
    row = P("stream", "fsdp", None)
    return jax.shard_map(
        local_pair if mesh.shape["fsdp"] == 16 else local_wide,
        mesh=mesh,
        in_specs=(
            row, P("stream", "fsdp"), P("stream", "fsdp", None, None), row, row, P("fsdp", None), P("fsdp", None),
            P("fsdp", None), P("fsdp"), P("fsdp", None), P("fsdp"), P("fsdp"), P("fsdp"), P("fsdp"), P("fsdp"),
            P("fsdp"), P(), row,
        ),
        out_specs=(
            row, row, P("fsdp", None), P("fsdp", None), P("fsdp", None), P("fsdp"), P("fsdp", None), P("fsdp"),
            P("fsdp"), P("fsdp"), P("fsdp"), P("fsdp"), P("fsdp"), P(),
        ),
        check_vma=False,
    )
```
